256 devices in a mesh: px: 32 (over z, y), py: 8 (over x, core).
Axes of the slice: x: 4, y: 4, z: 8, core: 2. Of those that a mesh axis runs over, the one named last changes fastest.
Arguments:
- source: float32 [17, 512, 1024], P(None, 'px', 'py'), may hold values from -8 to 8
- water_depth: float32 [512, 1024], P('px', 'py'), may hold values from 0.5 to 2
- potential_start: float32 [17, 512, 1024], P(None, 'px', 'py'), may hold values from -6 to 6
- velocity: float32 [3, 32, 8, 4096], P(None, 'px', 'py'), may hold values from -6 to 6
- fraction: float32 [32, 8, 4096], P('px', 'py'), may hold values from 0 to 1
- pressure: float32 [32, 8, 4096], P('px', 'py'), may hold values from -24 to 24
- neighbour: int32 [6, 32, 8, 4096], P(None, 'px', 'py'), may hold values from 0 to 4864, as said below
- send_slot: int32 [4, 32, 8, 192], P(None, 'px', 'py'), may hold values from 0 to 4095
- face_normal: float32 [3, 6, 32, 8, 4096], P(None, None, 'px', 'py'), may hold values from -3 to 3
- face_weight: float32 [6, 32, 8, 4096], P(None, 'px', 'py'), may hold values from 0.5 to 2
- step_scale: float32 [32, 8, 4096], P('px', 'py'), may hold values from 0.02 to 0.08
- height: float32 [32, 8, 4096], P('px', 'py'), may hold values from -1 to 1
- blend_weight: float32 [32, 8, 4096], P('px', 'py'), may hold values from 0.2 to 0.9
- corner: int32 [32, 8, 4096], P('px', 'py'), may hold values from 0 to 32638, as said below
- stencil_weight: float32 [4, 8, 32, 8, 4096], P(None, None, 'px', 'py'), may hold values from -2 to 2
- receive_cell: int32 [32, 8, 4096], P('px', 'py'), may hold values from 0 to 4096, as said below
Outputs:
- potential: float32 [17, 512, 1024], P(None, 'px', 'py')
- velocity_out: float32 [3, 32, 8, 4096], P(None, 'px', 'py')
- fraction_out: float32 [32, 8, 4096], P('px', 'py')
- pressure_out: float32 [32, 8, 4096], P('px', 'py')
The draws below stay inside these ranges and needn't reach their ends.
Inputs may be any that keep to these rules, and one draw needn't show every extreme that they name: Each value is a cell of the device (below 4096), a slot of the four received blocks of 192 values in the order lower px, upper px, lower py, upper py neighbour, or 4864, a slot that holds zero. `send_slot`: block 0 goes to the lower px neighbour, 1 to the upper px, 2 to the lower py, 3 to the upper py. corner = layer * 16 * 128 + row * 128 + column with layer < 16, row < 15, column < 127, so all eight stencil points lie in the owner's tile. `receive_cell`: block o of 128 slots holds what potential device (o, same py index) sends; each slot names the cell it relaxes or 4096 if it carries nothing; the live slots of a block come first, no cell is named twice on a device, and in every draw some blocks are full.
All inputs are finite; a program needn't handle non-finite values.
Results may differ from the reference program's by a relative error of at most 0.0001.
Values sent between devices are 32-bit elements; how exact they have to be, the bound alone decides.
A program may use at most 128 MiB of HBM per device.

```python
import math
import jax
import jax.numpy as jnp
from jax import lax

NZ = 17
CX = 16
CY = 128
LEVELS = 5
SMOOTH = 2
COARSE_SWEEPS = 4
CYCLES = 2
CAP = 4096
FACES = 6
JACOBI = 3
SLOTS = 128
GHOST = 192
NX = 512
NY = 1024
SUBX = 32
SUBY = 8
PAIRS = 4096


def draw_source(key, part):
    rough = jax.random.normal(key, (NZ, NX, NY), jnp.float32)
    return jnp.clip(rough, -6.0, 6.0)


def draw_neighbour(key, part):
    extent = (FACES, SUBX, SUBY, CAP)
    kind_key, local_key, ghost_key = jax.random.split(key, 3)
    kinds = jax.random.randint(kind_key, extent, 0, 16)
    local_index = jax.random.randint(local_key, extent, 0, CAP)
    ghost_index = jax.random.randint(ghost_key, extent, CAP, CAP + 4 * GHOST)
    return jnp.where(kinds < 12, local_index, jnp.where(kinds < 15, ghost_index, CAP + 4 * GHOST)).astype(jnp.int32)


def draw_corner(key, part):
    extent = (SUBX, SUBY, PAIRS)
    layer_key, row_key, column_key = jax.random.split(key, 3)
    layer_index = jax.random.randint(layer_key, extent, 0, NZ - 1)
    row_index = jax.random.randint(row_key, extent, 0, CX - 1)
    column_index = jax.random.randint(column_key, extent, 0, CY - 1)
    return (layer_index * (CX * CY) + row_index * CY + column_index).astype(jnp.int32)


def draw_receive_cell(key, part):
    order_key, hot_key, count_key = jax.random.split(key, 3)
    device_keys = jax.random.split(order_key, SUBX * SUBY)
    orders = jax.vmap(lambda one_key: jax.random.permutation(one_key, CAP)[:PAIRS])(device_keys)
    orders = orders.reshape(SUBX, SUBY, SUBX, SLOTS)
    hot_start = jax.random.randint(hot_key, (), 0, SUBX)
    owner_index = jnp.arange(SUBX)
    hot_owner = (owner_index - hot_start) % SUBX < max(1, SUBX // 8)
    quiet_counts = jax.random.randint(count_key, (SUBX, SUBY, SUBX), 0, SLOTS // 2 + 1)
    counts = jnp.where(hot_owner[None, None, :], SLOTS, quiet_counts)
    slot_index = jnp.arange(SLOTS)
    live_slot = slot_index[None, None, None, :] < counts[..., None]
    return jnp.where(live_slot, orders, CAP).reshape(SUBX, SUBY, PAIRS).astype(jnp.int32)


def place_ends(values, rng, low, top_value):
    longest = values.shape.index(max(values.shape))
    spots = []
    for shift in (0, 1):
        where = [jax.random.randint(jax.random.fold_in(rng, axis), (), 0, length) for axis, length in enumerate(values.shape)]
        where[longest] = (where[longest] + shift) % values.shape[longest]
        spots.append(tuple(where))
    return values.at[spots[0]].set(low).at[spots[1]].set(top_value)


def block_scale(rng, shape, cuts, low, largest):
    factor_of = 1.0
    for position, blocks in cuts:
        draws = jax.random.uniform(jax.random.fold_in(jax.random.fold_in(rng, 6), position), (blocks,), jnp.float32, low / len(cuts), largest / len(cuts))
        factor_of = factor_of * jnp.repeat(jnp.exp(draws), shape[position] // blocks).reshape((-1,) + (1,) * (len(shape) - 1 - position))
    return factor_of


def bell_draw(rng, shape, width, reach, shards=(), kind=jnp.bfloat16):
    values = jax.random.normal(rng, shape, jnp.float32) * width
    if len(shards) > 0:
        values = block_scale(rng, shape, shards, -0.22, 0.18) * values
    return jnp.clip(values, min=-reach, max=reach).astype(kind)


def setup_inputs(seed: int = 0) -> dict:
    key_of = jax.random.split(jax.random.key(seed), 17)
    source = draw_source(jax.random.fold_in(key_of[16], 71), 0)
    water_depth = jnp.clip(jnp.exp(math.log(2.0) - 1.3862944 * jax.random.uniform(key_of[1], (NX, NY), jnp.float32) ** block_scale(key_of[1], (NX, NY), ((0, 32), (1, 8)), -0.2, 0.2)), 0.5, 2.0)
    potential_start = bell_draw(key_of[2], (NZ, NX, NY), 1.0, 6.0, ((1, 32), (2, 8)), jnp.float32)
    velocity = bell_draw(key_of[3], (3, SUBX, SUBY, CAP), 1.0, 6.0, ((1, 32), (2, 8)), jnp.float32)
    fraction = jnp.clip(1.0 * jax.random.uniform(key_of[4], (SUBX, SUBY, CAP), jnp.float32) ** block_scale(key_of[4], (SUBX, SUBY, CAP), ((0, 32), (1, 8)), -0.2, 0.2), 0.0, 1.0)
    pressure = bell_draw(key_of[5], (SUBX, SUBY, CAP), 4.0, 24.0, ((0, 32), (1, 8)), jnp.float32)
    neighbour = draw_neighbour(jax.random.fold_in(key_of[16], 71), 0)
    send_slot = place_ends(jax.random.randint(key_of[7], (4, SUBX, SUBY, GHOST), 0, CAP), jax.random.fold_in(key_of[7], 1), 0, CAP - 1).astype(jnp.int32)
    face_normal = bell_draw(key_of[8], (3, FACES, SUBX, SUBY, CAP), 0.5, 3.0, ((2, 32), (3, 8)), jnp.float32)
    face_weight = jnp.clip(jnp.exp(math.log(2.0) - 1.3862944 * jax.random.uniform(key_of[9], (FACES, SUBX, SUBY, CAP), jnp.float32) ** block_scale(key_of[9], (FACES, SUBX, SUBY, CAP), ((1, 32), (2, 8)), -0.2, 0.2)), 0.5, 2.0)
    step_scale = jnp.clip(jnp.exp(math.log(0.08) - 1.3862944 * jax.random.uniform(key_of[10], (SUBX, SUBY, CAP), jnp.float32) ** block_scale(key_of[10], (SUBX, SUBY, CAP), ((0, 32), (1, 8)), -0.2, 0.2)), 0.02, 0.08)
    height = jnp.clip(jax.random.uniform(key_of[11], (SUBX, SUBY, CAP), jnp.float32, -1.0, 1.0) * block_scale(key_of[11], (SUBX, SUBY, CAP), ((0, 32), (1, 8)), -0.4, 0.0), -1.0, 1.0)
    blend_weight = jnp.clip(0.2 + 0.7 * jax.random.uniform(key_of[12], (SUBX, SUBY, CAP), jnp.float32) ** block_scale(key_of[12], (SUBX, SUBY, CAP), ((0, 32), (1, 8)), -0.2, 0.2), 0.2, 0.9)
    corner = draw_corner(jax.random.fold_in(key_of[16], 71), 0)
    stencil_weight = bell_draw(key_of[14], (4, 8, SUBX, SUBY, PAIRS), 8 ** -0.5, 2.0, ((2, 32), (3, 8)), jnp.float32)
    receive_cell = draw_receive_cell(jax.random.fold_in(key_of[16], 71), 0)
    return dict(source=source, water_depth=water_depth, potential_start=potential_start, velocity=velocity, fraction=fraction, pressure=pressure, neighbour=neighbour, send_slot=send_slot, face_normal=face_normal, face_weight=face_weight, step_scale=step_scale, height=height, blend_weight=blend_weight, corner=corner, stencil_weight=stencil_weight, receive_cell=receive_cell)


VERTICAL = 0.01
RELAX = 0.8
SHARPNESS = 4.0


def face_couplings(depth_pad):
    centre = depth_pad[1:-1, 1:-1]
    east_face = 0.5 * (centre + depth_pad[2:, 1:-1])
    west_face = 0.5 * (centre + depth_pad[:-2, 1:-1])
    north_face = 0.5 * (centre + depth_pad[1:-1, 2:])
    south_face = 0.5 * (centre + depth_pad[1:-1, :-2])
    return east_face, west_face, north_face, south_face


def diagonal_of(couplings, level_scale, layers):
    east_face, west_face, north_face, south_face = couplings
    bottom = (lax.broadcasted_iota(jnp.int32, (layers, 1, 1), 0) == 0).astype(east_face.dtype)
    return level_scale * (east_face + west_face + north_face + south_face)[None] + VERTICAL * (2.0 - bottom)


def apply_operator(grid_values, padded, couplings, level_scale):
    east_face, west_face, north_face, south_face = couplings
    horizontal = east_face * (grid_values - padded[:, 2:, 1:-1]) + west_face * (grid_values - padded[:, :-2, 1:-1])
    horizontal = horizontal + north_face * (grid_values - padded[:, 1:-1, 2:]) + south_face * (grid_values - padded[:, 1:-1, :-2])
    above_values = jnp.concatenate([grid_values[1:], jnp.zeros_like(grid_values[:1])], axis=0)
    below_values = jnp.concatenate([grid_values[:1], grid_values[:-1]], axis=0)
    return level_scale * horizontal + VERTICAL * (2.0 * grid_values - above_values - below_values)


def sweep_with(grid_values, padded, right_side, level_setup, level_scale):
    couplings, diagonal = level_setup
    return grid_values + RELAX * (right_side - apply_operator(grid_values, padded, couplings, level_scale)) / diagonal


def pad_zero(grid_values):
    return jnp.pad(grid_values, ((0, 0), (1, 1), (1, 1)))


def coarsen(grid_values):
    extent = grid_values.shape
    return grid_values.reshape(extent[:-2] + (extent[-2] // 2, 2, extent[-1] // 2, 2)).mean(axis=(-3, -1))


def refine(grid_values):
    return jnp.repeat(jnp.repeat(grid_values, 2, axis=-2), 2, axis=-1)


def vcycle(level_index, right_side, grid_values, setups):
    level_setup = setups[level_index]
    level_scale = 0.25 ** level_index
    if level_index == LEVELS - 1:
        grid_values = RELAX * right_side / level_setup[1]
        for sweep_index in range(COARSE_SWEEPS - 1):
            grid_values = sweep_with(grid_values, pad_zero(grid_values), right_side, level_setup, level_scale)
        return grid_values
    if grid_values is None:
        grid_values = RELAX * right_side / level_setup[1]
        first_sweep = 1
    else:
        first_sweep = 0
    for sweep_index in range(first_sweep, SMOOTH):
        grid_values = sweep_with(grid_values, pad_zero(grid_values), right_side, level_setup, level_scale)
    residual = right_side - apply_operator(grid_values, pad_zero(grid_values), level_setup[0], level_scale)
    correction = vcycle(level_index + 1, coarsen(residual), None, setups)
    grid_values = grid_values + refine(correction)
    for sweep_index in range(SMOOTH):
        grid_values = sweep_with(grid_values, pad_zero(grid_values), right_side, level_setup, level_scale)
    return grid_values


def stencil_offsets(tile_along, tile_across):
    plane_cells = tile_along * tile_across
    return jnp.array([0, 1, tile_across, tile_across + 1, plane_cells, plane_cells + 1,
                      plane_cells + tile_across, plane_cells + tile_across + 1], jnp.int32)


def advect(extended, neighbour_rows, normals, step_rows):
    cells_here = step_rows.shape[-1]
    own_values = extended[:, :cells_here]
    beside = extended[:, neighbour_rows]
    face_flux = 0.5 * jnp.sum(normals * (own_values[:3, None, :] + beside[:3]), axis=0)
    upwind = jnp.maximum(face_flux, 0.0)[None] * own_values[:, None, :] + jnp.minimum(face_flux, 0.0)[None] * beside
    return own_values - step_rows[None] * jnp.sum(upwind, axis=1)


def divergence(extended, neighbour_rows, normals):
    cells_here = neighbour_rows.shape[-1]
    velocity_part = extended[:3]
    beside = velocity_part[:, neighbour_rows]
    return 0.5 * jnp.sum(normals * (velocity_part[:, None, :cells_here] + beside), axis=(0, 1))


def jacobi(pressure_ext, neighbour_rows, weights, divergence_rows):
    beside = pressure_ext[neighbour_rows]
    return (jnp.sum(weights * beside, axis=0) - divergence_rows) / jnp.sum(weights, axis=0)


def correct(velocity_star, pressure_ext, neighbour_rows, normals, step_rows):
    cells_here = velocity_star.shape[-1]
    difference = pressure_ext[neighbour_rows] - pressure_ext[None, :cells_here]
    return velocity_star - step_rows[None] * 0.5 * jnp.sum(normals * difference[None], axis=1)


def relax_cells(state_rows, potential_rows, received, blend_rows, height_rows):
    target = jnp.concatenate([potential_rows[..., :3, :],
                              jax.nn.sigmoid(SHARPNESS * (potential_rows[..., 3:, :] - height_rows))], axis=-2)
    return state_rows - (blend_rows * received) * (state_rows - target)


def place_rows(arrived_rows, cells):
    potential_rows = jnp.zeros((4, CAP + 1), arrived_rows.dtype).at[:, cells].add(arrived_rows)
    received = jnp.zeros((CAP + 1,), arrived_rows.dtype).at[cells].add(1.0)
    return potential_rows[:, :CAP], received[:CAP]


def pick_rows(device_values, device_rows):
    return device_values[:, device_rows]


def exchange_ghosts(values, send_rows):
    buffers = jax.vmap(jax.vmap(pick_rows))(values, send_rows)
    from_lower_x = jnp.pad(buffers[:-1, :, :, 1], ((1, 0), (0, 0), (0, 0), (0, 0)))
    from_upper_x = jnp.pad(buffers[1:, :, :, 0], ((0, 1), (0, 0), (0, 0), (0, 0)))
    from_lower_y = jnp.pad(buffers[:, :-1, :, 3], ((0, 0), (1, 0), (0, 0), (0, 0)))
    from_upper_y = jnp.pad(buffers[:, 1:, :, 2], ((0, 0), (0, 1), (0, 0), (0, 0)))
    zero_slot = jnp.zeros(values.shape[:3] + (1,), values.dtype)
    return jnp.concatenate([values, from_lower_x, from_upper_x, from_lower_y, from_upper_y, zero_slot], axis=3)


def over_devices(function, *arrays):
    per_row = jax.vmap(function)
    return lax.map(lambda row_arrays: per_row(*row_arrays), arrays)


def reference(source, water_depth, potential_start, velocity, fraction, pressure, neighbour, send_slot,
              face_normal, face_weight, step_scale, height, blend_weight, corner, stencil_weight, receive_cell):
    layers = source.shape[0]
    depths = [water_depth]
    for level_index in range(1, LEVELS):
        depths.append(coarsen(depths[-1]))
    setups = []
    for level_index in range(LEVELS):
        couplings = face_couplings(jnp.pad(depths[level_index], 1))
        setups.append((couplings, diagonal_of(couplings, 0.25 ** level_index, layers)))
    potential = potential_start
    for cycle_index in range(CYCLES):
        potential = vcycle(0, source, potential, setups)

    owner_tiles = potential.reshape(layers, SUBX, CX, SUBY, CY).transpose(1, 3, 0, 2, 4).reshape(SUBX, SUBY, layers * CX * CY)
    points = corner[:, :, None, :] + stencil_offsets(CX, CY)[None, None, :, None]
    picked = jnp.take_along_axis(owner_tiles, points.reshape(SUBX, SUBY, 8 * PAIRS), axis=2).reshape(SUBX, SUBY, 8, PAIRS)
    weights = jnp.moveaxis(stencil_weight, (0, 1), (2, 3))
    sent_values = jnp.sum(weights * picked[:, :, None], axis=3)
    arrived = sent_values.reshape(SUBX, SUBY, 4, SUBX, SLOTS).transpose(3, 1, 2, 0, 4).reshape(SUBX, SUBY, 4, PAIRS)
    potential_rows, received = over_devices(place_rows, arrived, receive_cell)

    velocity_rows = jnp.moveaxis(velocity, 0, 2)
    neighbour_rows = jnp.moveaxis(neighbour, 0, 2)
    normals = jnp.moveaxis(face_normal, (0, 1), (2, 3))
    weights_face = jnp.moveaxis(face_weight, 0, 2)
    send_rows = jnp.moveaxis(send_slot, 0, 2)
    first_ext = exchange_ghosts(jnp.concatenate([velocity_rows, fraction[:, :, None]], axis=2), send_rows)
    state_rows = over_devices(advect, first_ext, neighbour_rows, normals, step_scale)
    second_ext = exchange_ghosts(jnp.concatenate([state_rows[:, :, :3], pressure[:, :, None]], axis=2), send_rows)
    divergence_rows = over_devices(divergence, second_ext, neighbour_rows, normals)
    pressure_now = over_devices(jacobi, second_ext[:, :, 3], neighbour_rows, weights_face, divergence_rows)
    for sweep_index in range(JACOBI - 1):
        pressure_ext = exchange_ghosts(pressure_now[:, :, None], send_rows)[:, :, 0]
        pressure_now = over_devices(jacobi, pressure_ext, neighbour_rows, weights_face, divergence_rows)
    pressure_ext = exchange_ghosts(pressure_now[:, :, None], send_rows)[:, :, 0]
    corrected = over_devices(correct, state_rows[:, :, :3], pressure_ext, neighbour_rows, normals, step_scale)
    relaxed = relax_cells(jnp.concatenate([corrected, state_rows[:, :, 3:]], axis=2), potential_rows,
                          received[:, :, None, :], blend_weight[:, :, None, :], height[:, :, None, :])
    return potential, jnp.moveaxis(relaxed[:, :, :3], 2, 0), relaxed[:, :, 3], pressure_now
```

```python
import jax
import jax.numpy as jnp
from jax import lax
from jax.experimental import pallas as pl
from jax.experimental.pallas import tpu as pltpu
from jax.sharding import PartitionSpec as P

F32 = jnp.float32
I32 = jnp.int32
MESH = pl.DeviceIdType.MESH
NPX, NPY = 32, 8
NZ = 17
FACES = 6
ROWS = 32
EXT = 40
VERT = 0.01
RELAX = 0.8
REACH = 7

GATHER_DIMS = lax.GatherDimensionNumbers(
    offset_dims=(),
    collapsed_slice_dims=(1,),
    start_index_map=(1,),
    operand_batching_dims=(0,),
    start_indices_batching_dims=(0,),
)


def lane_gather(values, lanes):
    return lax.gather(
        values,
        lanes[..., None],
        GATHER_DIMS,
        slice_sizes=(1, 1),
        mode=lax.GatherScatterMode.PROMISE_IN_BOUNDS,
    )


def lane_iota(rows):
    return lax.broadcasted_iota(I32, (rows, 128), 1)


def row_iota(rows):
    return lax.broadcasted_iota(I32, (rows, 128), 0)


def roll(values, shift, axis):
    shift = shift % values.shape[axis]
    return values if shift == 0 else pltpu.roll(values, shift, axis)


def over_layers(body, chunk=4):
    whole = NZ // chunk

    @pl.loop(0, whole)
    def _(step):
        for j in range(chunk):
            body(step * chunk + j)

    for k in range(whole * chunk, NZ):
        body(k)


def kind(k):
    return min(k, 1) if isinstance(k, int) else jnp.minimum(k, 1)


def inside_of(x, y, rows, row_first, lane_split, width, height, depth):
    row = row_iota(rows) + row_first
    lane = lane_iota(rows)
    column = jnp.where(lane < lane_split, lane, lane - 128) + y * width
    return (row >= 0) & (row < height) & (column >= 0) & (column < depth)


def set_coefficients(level, depth, inside, scale):
    rows = depth.shape[0]
    half = 0.5 * scale
    faces = (
        half * (depth + roll(depth, rows - 1, 0)),
        half * (depth + roll(depth, 1, 0)),
        half * (depth + roll(depth, 127, 1)),
        half * (depth + roll(depth, 1, 1)),
    )
    total = faces[0] + faces[1] + faces[2] + faces[3]
    for i, face in enumerate(faces):
        level["C"][i] = face
    for i, extra in enumerate((VERT, 2 * VERT)):
        diagonal = total + extra
        level["D"][i] = diagonal
        level["W"][i] = jnp.where(inside, RELAX / diagonal, 0.0)


def neighbour_sum(level, source, k):
    values = source[k + 1]
    rows = values.shape[0]
    total = level["C"][0] * roll(values, rows - 1, 0) + level["C"][1] * roll(values, 1, 0)
    total = total + level["C"][2] * roll(values, 127, 1) + level["C"][3] * roll(values, 1, 1)
    return values, total + VERT * (source[k] + source[k + 2])


def point_step(level):
    def body(k):
        level["V"][k + 1] = level["W"][kind(k)] * level["B"][k]

    over_layers(body)


def sweep_step(level, source, target):
    def body(k):
        values, total = neighbour_sum(level, source, k)
        target[k + 1] = (1.0 - RELAX) * values + level["W"][kind(k)] * (level["B"][k] + total)

    over_layers(body)


def residual_step(level, source):
    def body(k):
        values, total = neighbour_sum(level, source, k)
        level["T"][k] = level["B"][k] + total - level["D"][kind(k)] * values

    over_layers(body)


def pair_mean_rows(even, odd):
    total = even + odd
    return 0.25 * (total + roll(total, 127, 1))


def coarsen_step(fine, coarse):
    half = coarse["R"]
    lanes = (2 * lane_iota(half)) & 127

    def body(k):
        total = pair_mean_rows(
            fine["T"][k, pl.ds(0, half, stride=2), :], fine["T"][k, pl.ds(1, half, stride=2), :]
        )
        coarse["B"][k] = lane_gather(total, lanes)

    over_layers(body)


def refine_add(correction, first, fine, target, lane_split):
    rows = fine["R"]
    half = rows // 2
    lane = lane_iota(half)
    lanes = jnp.where(lane < lane_split, lane >> 1, (lane >> 1) + 64)

    def body(k):
        spread = lane_gather(correction[k + 1, first : first + half, :], lanes)
        fine["T"][k, pl.ds(0, half, stride=2), :] = spread
        fine["T"][k, pl.ds(1, half, stride=2), :] = spread
        target[k + 1] = target[k + 1] + fine["T"][k]

    over_layers(body)


def fine_neighbours(top, source_a, source_b, k, lo, hi):
    rows = hi - lo
    lane = lane_iota(rows)
    first, last = lane == 0, lane == 127
    a, b = source_a[k + 1, lo:hi, :], source_b[k + 1, lo:hi, :]
    right_a, right_b = roll(a, 127, 1), roll(b, 127, 1)
    left_a, left_b = roll(a, 1, 1), roll(b, 1, 1)
    results = []
    for side, values, right, left in (
        ("a", a, jnp.where(last, right_b, right_a), jnp.where(first, left_b, left_a)),
        ("b", b, jnp.where(last, right_a, right_b), jnp.where(first, left_a, left_b)),
    ):
        faces = top["C" + side]
        source = source_a if side == "a" else source_b
        total = faces[0, lo:hi, :] * roll(values, rows - 1, 0) + faces[1, lo:hi, :] * roll(values, 1, 0)
        total = total + faces[2, lo:hi, :] * right + faces[3, lo:hi, :] * left
        total = total + VERT * (source[k, lo:hi, :] + source[k + 2, lo:hi, :])
        results.append((values, total))
    return results


def fine_sweep(top, source, target, lo=0, hi=48):
    def body(k):
        pairs = fine_neighbours(top, source[0], source[1], k, lo, hi)
        for side, (values, total), into in zip("ab", pairs, target):
            relax = top["W" + side][kind(k), lo:hi, :]
            into[k + 1, lo:hi, :] = (1.0 - RELAX) * values + relax * (top["B" + side][k, lo:hi, :] + total)

    over_layers(body, 2)


def fine_residual(top, source, target, lo=0, hi=48):
    def body(k):
        pairs = fine_neighbours(top, source[0], source[1], k, lo, hi)
        for side, (values, total), into in zip("ab", pairs, target):
            into[k + 1, lo:hi, :] = (
                top["B" + side][k, lo:hi, :] + total - top["D" + side][kind(k), lo:hi, :] * values
            )

    over_layers(body, 2)


def table_gather(read_row, count, components, hi, lo):
    rows = hi.shape[0]
    picked = [jnp.zeros((rows, 128), F32) for _ in range(components)]
    for j in range(count):
        mask = hi == j
        for c in range(components):
            row = jnp.broadcast_to(read_row(c, j), (rows, 128))
            picked[c] = jnp.where(mask, lane_gather(row, lo), picked[c])
    return picked


def scratch_plan():
    plan = {}

    def vmem(name, *shape, dtype=F32):
        plan[name] = pltpu.VMEM(shape, dtype)

    for name in ("VA", "VB", "UA", "UB"):
        vmem(name, NZ + 2, 48, 128)
    for name in ("BA", "BB"):
        vmem(name, NZ, 48, 128)
    for side in "AB":
        vmem("C0" + side, 4, 48, 128)
        vmem("W0" + side, 2, 48, 128)
        vmem("D0" + side, 2, 48, 128)
        vmem("DEP" + side, 48, 128)
    for level, rows in ((1, 24), (2, 64), (3, 32), (4, 16)):
        vmem(f"V{level}", NZ + 2, rows, 128)
        vmem(f"U{level}", NZ + 2, rows, 128)
        vmem(f"B{level}", NZ, rows, 128)
        vmem(f"T{level}", NZ, rows, 128)
        vmem(f"C{level}", 4, rows, 128)
        vmem(f"W{level}", 2, rows, 128)
        vmem(f"D{level}", 2, rows, 128)
        vmem(f"DEP{level}", rows, 128)
    vmem("M1", 24, 128)
    vmem("SF", 5, 16, 128)
    vmem("SL", 5, 16, 128)
    vmem("RS", 6, 5, 16, 128)
    vmem("Q", NZ + 1, 8, 128)
    for cycle in range(2):
        vmem(f"P{cycle}", 3, 8, 128)
        vmem(f"G{cycle}", 16, 3, 3, 8, 128)
        vmem(f"E{cycle}", 9, 9, 8, 128)
        vmem(f"EP{cycle}", 9, 8, 128)
    vmem("HI", FACES * ROWS, 128, dtype=I32)
    vmem("LO", FACES * ROWS, 128, dtype=I32)
    vmem("SI", 8, 128, dtype=I32)
    vmem("TQ", 4 * EXT, 128)
    vmem("TS", 4 * EXT, 128)
    for i in range(3):
        vmem(f"TP{i}", EXT, 128)
    for i, components in enumerate((4, 4, 1, 1, 1)):
        vmem(f"CS{i}", components, 8, 128)
        vmem(f"CR{i}", 4, components, 8, 128)
    vmem("FRAC", ROWS, 128)
    vmem("DIV", ROWS, 128)
    vmem("IWS", ROWS, 128)
    vmem("COR", 3 * ROWS, 128)
    vmem("INV", 2 * ROWS, 128, dtype=I32)
    vmem("PK", 8 * ROWS, 128)
    vmem("S", 256, 128)
    vmem("RB", 256, 128)
    dma = pltpu.SemaphoreType.DMA
    for name, count in (("tile", 6), ("strip", 6), ("deep0", 48), ("deep1", 48), ("near0", 9), ("near1", 9), ("all", 32)):
        plan[name + "_s"] = dma((count,))
        plan[name + "_r"] = dma((count,))
    for i in range(5):
        plan[f"cfd{i}_s"] = dma((4,))
        plan[f"cfd{i}_r"] = dma((4,))
    return plan


INPUTS = (
    "source", "depth", "start", "velocity", "fraction", "pressure", "neighbour", "slot",
    "normal", "weight", "step", "height", "blend", "corner", "stencil", "receive",
)
OUTPUTS = ("potential", "velocity_out", "fraction_out", "pressure_out")


def kernel(*refs):
    names = list(INPUTS) + list(OUTPUTS) + list(scratch_plan())
    r = dict(zip(names, refs))
    x, y = lax.axis_index("px"), lax.axis_index("py")

    def at(dx, dy):
        return (lax.rem(x + dx + NPX, NPX), lax.rem(y + dy + NPY, NPY))

    def send(source, target, name, slot, where):
        copy = pltpu.make_async_remote_copy(
            src_ref=source,
            dst_ref=target,
            send_sem=r[name + "_s"].at[slot],
            recv_sem=r[name + "_r"].at[slot],
            device_id=where,
            device_id_type=MESH,
        )
        copy.start()
        return copy

    sent = []

    barrier = pltpu.get_barrier_semaphore()
    partners = [(dx, 0) for dx in range(1, NPX)]
    partners += [(dx, dy) for dx in range(-REACH, REACH + 1) for dy in (-1, 1)]
    for dx, dy in partners:
        pl.semaphore_signal(barrier, inc=1, device_id=at(dx, dy), device_id_type=MESH)

    for c in range(3):
        r["TQ"][c * EXT : c * EXT + ROWS, :] = r["velocity"][c * ROWS : (c + 1) * ROWS, :]
    r["TQ"][3 * EXT : 3 * EXT + ROWS, :] = r["fraction"][...]
    r["SI"][...] = jnp.zeros((8, 128), I32)
    r["SI"][0:4, :] = r["slot"][:, 0:128]
    r["SI"][4:8, 0:64] = r["slot"][:, 128:192]
    send_hi, send_lo = r["SI"][...] >> 7, r["SI"][...] & 127

    def cfd_send(i, table, components):
        values = table_gather(
            lambda c, j: r[table][c * EXT + j : c * EXT + j + 1, :], ROWS, components, send_hi, send_lo
        )
        for c in range(components):
            r[f"CS{i}"][c] = values[c]

    def cfd_start(i):
        copies = []
        for slot, (dx, dy) in enumerate(((1, 0), (-1, 0), (0, 1), (0, -1))):
            copies.append(send(r[f"CS{i}"], r[f"CR{i}"].at[slot], f"cfd{i}", slot, at(dx, dy)))
        return copies

    there = (x > 0, x < NPX - 1, y > 0, y < NPY - 1)
    block = (1, 0, 3, 2)

    def cfd_wait(i, table, components, copies):
        for copy in copies:
            copy.wait_recv()
        sent.extend(copies)
        for c in range(components):
            for b in range(4):
                for h in range(2):
                    row = r[f"CR{i}"][b, c, block[b] + 4 * h : block[b] + 4 * h + 1, :]
                    place = c * EXT + ROWS + 2 * b + h
                    r[table][place : place + 1, :] = jnp.where(there[b], row, 0.0)

    cfd_send(0, "TQ", 4)

    lane16 = lane_iota(16)
    groups_f = [jnp.zeros((16, 128), F32) for _ in range(5)]
    groups_l = [jnp.zeros((16, 128), F32) for _ in range(5)]
    for t in range(2 * NZ + 1):
        if t < NZ:
            tile = r["start"][t]
        elif t < 2 * NZ:
            tile = r["source"][t - NZ]
        else:
            tile = r["depth"][...]
        g, q = t // 8, t % 8
        mine = (lane16 >= 16 * q) & (lane16 < 16 * q + 16)
        groups_f[g] = jnp.where(mine, roll(tile, 16 * q, 1), groups_f[g])
        groups_l[g] = jnp.where(mine, roll(tile, 16 * q + 16, 1), groups_l[g])
    for g in range(5):
        r["SF"][g] = groups_f[g]
        r["SL"][g] = groups_l[g]

    pl.semaphore_wait(barrier, len(partners))

    copies0 = cfd_start(0)
    strips = []
    for dx in (-1, 0, 1):
        strips.append(send(r["SL"], r["RS"].at[2 * (1 - dx)], "strip", 2 * (1 - dx), at(dx, 1)))
        strips.append(send(r["SF"], r["RS"].at[2 * (1 - dx) + 1], "strip", 2 * (1 - dx) + 1, at(dx, -1)))
    tiles = []
    for s, (dx, first) in enumerate(((1, 0), (-1, 32))):
        rows = pl.ds(first, 16)
        tiles.append(send(r["start"], r["VA"].at[pl.ds(1, NZ), rows, :], "tile", 3 * s, at(dx, 0)))
        tiles.append(send(r["source"], r["BA"].at[:, rows, :], "tile", 3 * s + 1, at(dx, 0)))
        tiles.append(send(r["depth"], r["DEPA"].at[rows, :], "tile", 3 * s + 2, at(dx, 0)))

    cells = r["receive"][...]
    hi_of, lo_of = cells >> 7, cells & 127
    inverse = jnp.zeros((2 * ROWS, 128), F32)
    for chunk in range(4):
        lefts, rights = [], []
        for o in range(8 * chunk, 8 * chunk + 8):
            match = row_iota(ROWS) == jnp.broadcast_to(hi_of[o : o + 1, :], (ROWS, 128))
            lanes = lane_iota(ROWS).astype(F32)
            lefts.append(
                jnp.concatenate([jnp.where(match, F32(o + 1), 0.0), jnp.where(match, lanes, 0.0)], axis=0)
            )
            low = row_iota(128) == jnp.broadcast_to(lo_of[o : o + 1, :], (128, 128))
            rights.append(jnp.where(low, F32(1.0), 0.0))
        left = jnp.concatenate(lefts, axis=1).astype(jnp.bfloat16)
        right = jnp.concatenate(rights, axis=1).astype(jnp.bfloat16)
        inverse = inverse + lax.dot_general(
            left, right, (((1,), (1,)), ((), ())), preferred_element_type=F32
        )
    r["INV"][...] = inverse.astype(I32)

    index = r["neighbour"][...]
    for edge in (4288, 4480, 4672, 4864):
        index = index + jnp.where(r["neighbour"][...] >= edge, 64, 0)
    r["HI"][...] = index >> 7
    r["LO"][...] = index & 127

    for name, rows in (("VA", 48), ("VB", 48), ("UA", 48), ("UB", 48)) + tuple(
        (f"{v}{level}", rows) for level, rows in ((1, 24), (2, 64), (3, 32), (4, 16)) for v in "VU"
    ):
        r[name][0] = jnp.zeros((rows, 128), F32)
        r[name][NZ + 1] = jnp.zeros((rows, 128), F32)
    r["VA"][1 : NZ + 1, 16:32, :] = r["start"][...]
    r["BA"][:, 16:32, :] = r["source"][...]
    r["DEPA"][16:32, :] = r["depth"][...]
    for cycle in range(2):
        r[f"G{cycle}"][0] = jnp.zeros((3, 3, 8, 128), F32)

    cfd_wait(0, "TQ", 4, copies0)

    def face_rows(f):
        base = pl.multiple_of(f * ROWS, ROWS)
        return r["HI"][pl.ds(base, ROWS), :], r["LO"][pl.ds(base, ROWS), :]

    def normal_of(c, f):
        return r["normal"][pl.ds(pl.multiple_of(c * FACES * ROWS + f * ROWS, ROWS), ROWS), :]

    def weight_of(f):
        return r["weight"][pl.ds(pl.multiple_of(f * ROWS, ROWS), ROWS), :]

    def reader(table):
        return lambda c, j: r[table][c * EXT + j : c * EXT + j + 1, :]

    def own(table, c):
        return r[table][c * EXT : c * EXT + ROWS, :]

    def advect_face(f, totals):
        hi, lo = face_rows(f)
        beside = table_gather(reader("TQ"), EXT, 4, hi, lo)
        flux = normal_of(0, f) * (own("TQ", 0) + beside[0])
        for c in (1, 2):
            flux = flux + normal_of(c, f) * (own("TQ", c) + beside[c])
        flux = 0.5 * flux
        out, into = jnp.maximum(flux, 0.0), jnp.minimum(flux, 0.0)
        return tuple(totals[c] + out * own("TQ", c) + into * beside[c] for c in range(4))

    zero = jnp.zeros((ROWS, 128), F32)
    totals = lax.fori_loop(0, FACES, advect_face, (zero,) * 4)
    scale = r["step"][...]
    for c in range(3):
        r["TS"][c * EXT : c * EXT + ROWS, :] = own("TQ", c) - scale * totals[c]
    r["FRAC"][...] = own("TQ", 3) - scale * totals[3]
    r["TS"][3 * EXT : 3 * EXT + ROWS, :] = r["pressure"][...]
    cfd_send(1, "TS", 4)
    copies1 = cfd_start(1)

    for copy in tiles + strips:
        copy.wait_recv()
    sent.extend(tiles + strips)
    for block_row in range(3):
        rows = slice(16 * block_row, 16 * block_row + 16)
        for t in range(2 * NZ + 1):
            g, q = t // 8, t % 8
            lower = r["RS"][2 * block_row, g]
            upper = r["RS"][2 * block_row + 1, g]
            value = jnp.where(
                lane16 < 16,
                roll(upper, -16 * q, 1),
                jnp.where(lane16 >= 112, roll(lower, 112 - 16 * q, 1), 0.0),
            )
            if t < NZ:
                r["VB"][t + 1, rows, :] = value
            elif t < 2 * NZ:
                r["BB"][t - NZ, rows, :] = value
            else:
                r["DEPB"][rows, :] = value

    fine_rows = row_iota(48) + 16 * (x - 1)
    inside_a = (fine_rows >= 0) & (fine_rows < 16 * NPX)
    side_ok = jnp.where(lane_iota(48) < 64, jnp.where(y < NPY - 1, 1, 0), jnp.where(y > 0, 1, 0)) > 0
    inside_b = inside_a & side_ok

    def mask_start(k):
        r["VA"][k + 1] = jnp.where(inside_a, r["VA"][k + 1], 0.0)
        r["VB"][k + 1] = jnp.where(inside_b, r["VB"][k + 1], 0.0)

    over_layers(mask_start)

    depth_a = jnp.where(inside_a, r["DEPA"][...], 0.0)
    depth_b = jnp.where(inside_b, r["DEPB"][...], 0.0)
    r["DEPA"][...] = depth_a
    r["DEPB"][...] = depth_b
    lane48 = lane_iota(48)
    for side, depth, other, inside in (("A", depth_a, depth_b, inside_a), ("B", depth_b, depth_a, inside_b)):
        right = jnp.where(lane48 == 127, roll(other, 127, 1), roll(depth, 127, 1))
        left = jnp.where(lane48 == 0, roll(other, 1, 1), roll(depth, 1, 1))
        faces = (
            0.5 * (depth + roll(depth, 47, 0)),
            0.5 * (depth + roll(depth, 1, 0)),
            0.5 * (depth + right),
            0.5 * (depth + left),
        )
        total = faces[0] + faces[1] + faces[2] + faces[3]
        for i, face in enumerate(faces):
            r["C0" + side][i] = face
        for i, extra in enumerate((VERT, 2 * VERT)):
            r["D0" + side][i] = total + extra
            r["W0" + side][i] = jnp.where(inside, RELAX / (total + extra), 0.0)

    top = {"Ca": r["C0A"], "Cb": r["C0B"], "Wa": r["W0A"], "Wb": r["W0B"], "Da": r["D0A"], "Db": r["D0B"],
           "Ba": r["BA"], "Bb": r["BB"]}
    fine_v, fine_u = (r["VA"], r["VB"]), (r["UA"], r["UB"])
    levels = {
        level: {**{key: r[f"{key}{level}"] for key in ("V", "U", "B", "T", "C", "W", "D")}, "R": rows}
        for level, rows in ((1, 24), (2, 64), (3, 32), (4, 16))
    }
    lane24 = lane_iota(24)
    down24 = (2 * lane24) & 127

    def fine_pair(a_even, a_odd, b_even, b_odd):
        mean_a = lane_gather(pair_mean_rows(a_even, a_odd), down24)
        mean_b = lane_gather(pair_mean_rows(b_even, b_odd), down24)
        return jnp.where(lane24 < 64, mean_a, mean_b)

    even24, odd24 = pl.ds(0, 24, stride=2), pl.ds(1, 24, stride=2)
    inside_1 = inside_of(x, y, 24, 8 * (x - 1), 96, 64, 8 * NPX, 64 * NPY)
    r["M1"][...] = jnp.where(inside_1, F32(1.0), 0.0)
    depth_1 = fine_pair(r["DEPA"][even24, :], r["DEPA"][odd24, :], r["DEPB"][even24, :], r["DEPB"][odd24, :])
    depth_1 = jnp.where(inside_1, depth_1, 0.0)
    r["DEP1"][...] = depth_1
    set_coefficients(levels[1], depth_1, inside_1, 0.25)

    def fine_coarsen(k):
        levels[1]["B"][k] = fine_pair(
            r["UA"][k + 1, even24, :], r["UA"][k + 1, odd24, :], r["UB"][k + 1, even24, :], r["UB"][k + 1, odd24, :]
        )

    lane8 = lane_iota(8)
    row8 = row_iota(8)

    def pack_deep(cycle):
        count = NZ + 1 if cycle == 0 else NZ
        for k in range(count):
            if k < NZ:
                even, odd = r["T1"][k, pl.ds(8, 4, stride=2), :], r["T1"][k, pl.ds(9, 4, stride=2), :]
            else:
                even, odd = r["DEP1"][pl.ds(8, 4, stride=2), :], r["DEP1"][pl.ds(9, 4, stride=2), :]
            mean = pair_mean_rows(even, odd)
            r["Q"][k, 0:4, :] = mean
            r["Q"][k, 4:8, :] = mean
        for v in range(3):
            packed = jnp.zeros((8, 128), F32)
            for within in range(8):
                k = 8 * v + within
                if k >= count:
                    continue
                h, q = within // 4, within % 4
                lanes = (2 * lane8 + (64 if q % 2 else 0)) & 127
                mine = (lane8 >= 32 * q) & (lane8 < 32 * q + 32) & ((row8 >= 4) if h else (row8 < 4))
                packed = jnp.where(mine, lane_gather(r["Q"][k], lanes), packed)
            r[f"P{cycle}"][v] = packed
            r[f"G{cycle}"][8, 1, v] = packed

    def start_deep(cycle):
        copies = []
        for dx in range(-REACH, REACH + 1):
            for dy in (-1, 0, 1):
                if dx == 0 and dy == 0:
                    continue
                d, j = 8 - dx, 1 - dy
                copies.append(send(r[f"P{cycle}"], r[f"G{cycle}"].at[d, j], f"deep{cycle}", 3 * d + j, at(dx, dy)))
        return copies

    def unpack_deep(cycle):
        grid_of = r[f"G{cycle}"]

        @pl.loop(0, 8)
        def _(m):
            rows = pl.ds(pl.multiple_of(8 * m, 8), 8)
            for v in range(3):
                halves = []
                for j in range(3):
                    first, second = grid_of[2 * m, j, v], grid_of[2 * m + 1, j, v]
                    halves.append(
                        (
                            jnp.where(row8 < 4, first, roll(second, 4, 0)),
                            jnp.where(row8 < 4, roll(first, 4, 0), second),
                        )
                    )
                for within in range(8):
                    k = 8 * v + within
                    if k > NZ or (k == NZ and cycle > 0):
                        continue
                    h, q = within // 4, within % 4
                    value = jnp.where(
                        lane8 < 32,
                        roll(halves[1][h], -32 * q, 1),
                        jnp.where(
                            lane8 < 64,
                            roll(halves[2][h], 32 - 32 * q, 1),
                            roll(halves[0][h], 96 - 32 * q, 1),
                        ),
                    )
                    if k < NZ:
                        r["B2"][k, rows, :] = value
                    else:
                        r["DEP2"][rows, :] = value

    def deep_coefficients():
        for level, rows, tile, width in ((2, 64, 4, 32), (3, 32, 2, 16), (4, 16, 1, 8)):
            inside = inside_of(x, y, rows, tile * (x - 8), 64, width, tile * NPX, width * NPY)
            if level > 2:
                above = r[f"DEP{level - 1}"]
                mean = pair_mean_rows(above[pl.ds(0, rows, stride=2), :], above[pl.ds(1, rows, stride=2), :])
                depth = lane_gather(mean, (2 * lane_iota(rows)) & 127)
            else:
                depth = r["DEP2"][...]
            depth = jnp.where(inside, depth, 0.0)
            r[f"DEP{level}"][...] = depth
            set_coefficients(levels[level], depth, inside, 0.25**level)

    def solve_deep():
        for level in (2, 3):
            point_step(levels[level])
            sweep_step(levels[level], levels[level]["V"], levels[level]["U"])
            residual_step(levels[level], levels[level]["U"])
            coarsen_step(levels[level], levels[level + 1])
        last = levels[4]
        point_step(last)
        sweep_step(last, last["V"], last["U"])
        sweep_step(last, last["U"], last["V"])
        sweep_step(last, last["V"], last["U"])
        for level in (3, 2):
            here = levels[level]
            refine_add(levels[level + 1]["U"], 0, here, here["U"], 64)
            sweep_step(here, here["U"], here["V"])
            sweep_step(here, here["V"], here["U"])
        here = levels[1]
        refine_add(levels[2]["U"], 28, here, here["U"], 96)
        sweep_step(here, here["U"], here["V"])
        sweep_step(here, here["V"], here["U"])

    def down(lo, hi):
        fine_residual(top, fine_v, fine_u, lo, hi)
        over_layers(fine_coarsen)
        point_step(levels[1])
        sweep_step(levels[1], levels[1]["V"], levels[1]["U"])
        residual_step(levels[1], levels[1]["U"])

    def start_near(cycle):
        for pair in range(9):
            value = r["U1"][2 * pair + 1, 8:16, :]
            if 2 * pair + 1 < NZ:
                value = jnp.where(lane8 < 64, value, roll(r["U1"][2 * pair + 2, 8:16, :], 64, 1))
            r[f"EP{cycle}"][pair] = value
            r[f"E{cycle}"][4, pair] = value
        copies = []
        for dx in (-1, 0, 1):
            for dy in (-1, 0, 1):
                if dx or dy:
                    slot = 3 * (1 - dx) + 1 - dy
                    copies.append(send(r[f"EP{cycle}"], r[f"E{cycle}"].at[slot], f"near{cycle}", slot, at(dx, dy)))
        return copies

    def add_near(cycle):
        got = r[f"E{cycle}"]
        half_lane = lane24 >> 1
        for k in range(NZ):
            pair, odd = k // 2, k % 2
            parts = []
            for block_row in range(3):
                lower, middle, upper = (got[3 * block_row + j, pair] for j in range(3))
                middle = roll(middle, 64 * odd, 1)
                aside = jnp.where(lane8 < 96, upper, lower)
                parts.append(jnp.where(lane8 < 64, middle, roll(aside, 0 if odd else 64, 1) if odd else
                                       jnp.where(lane8 < 96, roll(upper, 64, 1), roll(lower, 64, 1))))
            for block_row in range(3):
                r["T1"][k, 8 * block_row : 8 * block_row + 8, :] = parts[block_row]

        def body(k):
            value = r["T1"][k] * r["M1"][...]
            for name, into, lanes in (("UA", "VA", half_lane), ("UB", "VB", half_lane + 64)):
                spread = lane_gather(value, lanes)
                r[name][k + 1, even24, :] = spread
                r[name][k + 1, odd24, :] = spread
                r[into][k + 1] = r[into][k + 1] + r[name][k + 1]

        over_layers(body)

    fine_sweep(top, fine_v, fine_u)
    fine_sweep(top, fine_u, fine_v)
    down(0, 48)
    pack_deep(0)
    deep0 = start_deep(0)

    cfd_wait(1, "TS", 4, copies1)

    def first_face(f, carry):
        flow, pull, weights = carry
        hi, lo = face_rows(f)
        beside = table_gather(reader("TS"), EXT, 4, hi, lo)
        for c in range(3):
            flow = flow + normal_of(c, f) * (own("TS", c) + beside[c])
        weight = weight_of(f)
        return flow, pull + weight * beside[3], weights + weight

    flow, pull, weights = lax.fori_loop(0, FACES, first_face, (zero,) * 3)
    r["DIV"][...] = 0.5 * flow
    r["IWS"][...] = 1.0 / weights
    r["TP0"][0:ROWS, :] = (pull - r["DIV"][...]) * r["IWS"][...]
    cfd_send(2, "TP0", 1)
    copies2 = cfd_start(2)

    for copy in deep0:
        copy.wait_recv()
    sent.extend(deep0)
    unpack_deep(0)
    deep_coefficients()
    solve_deep()
    near0 = start_near(0)

    def pressure_sweep(i, before, after):
        def face(f, pull):
            hi, lo = face_rows(f)
            return pull + weight_of(f) * table_gather(reader(before), EXT, 1, hi, lo)[0]

        pull = lax.fori_loop(0, FACES, face, zero)
        r[after][0:ROWS, :] = (pull - r["DIV"][...]) * r["IWS"][...]

    cfd_wait(2, "TP0", 1, copies2)
    pressure_sweep(2, "TP0", "TP1")
    cfd_send(3, "TP1", 1)
    copies3 = cfd_start(3)

    for copy in near0:
        copy.wait_recv()
    sent.extend(near0)
    add_near(0)
    fine_sweep(top, fine_v, fine_u)
    fine_sweep(top, fine_u, fine_v)
    fine_sweep(top, fine_v, fine_u)
    fine_sweep(top, fine_u, fine_v)
    down(8, 40)
    pack_deep(1)
    deep1 = start_deep(1)

    cfd_wait(3, "TP1", 1, copies3)
    pressure_sweep(3, "TP1", "TP2")
    r["pressure_out"][...] = r["TP2"][0:ROWS, :]
    cfd_send(4, "TP2", 1)
    copies4 = cfd_start(4)

    for copy in deep1:
        copy.wait_recv()
    sent.extend(deep1)
    unpack_deep(1)
    solve_deep()
    near1 = start_near(1)

    cfd_wait(4, "TP2", 1, copies4)

    def correct_face(f, totals):
        hi, lo = face_rows(f)
        difference = table_gather(reader("TP2"), EXT, 1, hi, lo)[0] - r["TP2"][0:ROWS, :]
        return tuple(totals[c] + normal_of(c, f) * difference for c in range(3))

    totals = lax.fori_loop(0, FACES, correct_face, (zero,) * 3)
    for c in range(3):
        r["COR"][c * ROWS : (c + 1) * ROWS, :] = own("TS", c) - r["step"][...] * (0.5 * totals[c])

    for copy in near1:
        copy.wait_recv()
    sent.extend(near1)
    add_near(1)
    fine_sweep(top, fine_v, fine_u, 8, 40)
    fine_sweep(top, fine_u, fine_v, 8, 40)

    for half in range(2):
        rows = slice(16 * half, 16 * half + 16)
        corner = r["corner"][rows, :]
        column = corner & 127
        beyond = column + 1
        point_row = (corner >> 7) & 15
        point_layer = corner >> 11

        def layer(k, picks):
            found = [jnp.zeros((16, 128), F32) for _ in range(4)]
            before = None
            for i in range(16):
                row = jnp.broadcast_to(r["VA"][k + 1, 16 + i : 17 + i, :], (16, 128))
                here = point_row == i
                left, right = lane_gather(row, column), lane_gather(row, beyond)
                if i < 15:
                    found[0] = jnp.where(here, left, found[0])
                    found[1] = jnp.where(here, right, found[1])
                if before is not None:
                    found[2] = jnp.where(before, left, found[2])
                    found[3] = jnp.where(before, right, found[3])
                before = here
            low, high = point_layer == k, point_layer == k - 1
            return tuple(jnp.where(low, found[i], picks[i]) for i in range(4)) + tuple(
                jnp.where(high, found[i], picks[4 + i]) for i in range(4)
            )

        picks = lax.fori_loop(0, NZ, layer, (jnp.zeros((16, 128), F32),) * 8)
        for quantity in range(4):
            total = jnp.zeros((16, 128), F32)
            for p in range(8):
                base = (quantity * 8 + p) * ROWS + 16 * half
                total = total + r["stencil"][base : base + 16, :] * picks[p]
            r["S"][pl.ds(128 * half + quantity, 16, stride=8), :] = total

    own_rows = pl.ds(pl.multiple_of(x * 8, 8), 8)
    everyone = []
    for o in range(1, NPX):
        there_x = lax.rem(x + o, NPX)
        rows = pl.ds(pl.multiple_of(there_x * 8, 8), 8)
        everyone.append(send(r["S"].at[rows, :], r["RB"].at[own_rows, :], "all", o, (there_x, y)))
    r["RB"][own_rows, :] = r["S"][own_rows, :]
    r["potential"][...] = r["VA"][1 : NZ + 1, 16:32, :]
    for copy in everyone:
        copy.wait_recv()
    sent.extend(everyone)

    slot_hi, slot_lo = r["INV"][0:ROWS, :] - 1, r["INV"][ROWS : 2 * ROWS, :]
    targets = table_gather(lambda c, j: r["RB"][8 * j + c : 8 * j + c + 1, :], NPX, 4, slot_hi, slot_lo)
    strength = jnp.where(slot_hi >= 0, r["blend"][...], 0.0)
    for c in range(3):
        velocity = r["COR"][c * ROWS : (c + 1) * ROWS, :]
        r["velocity_out"][c * ROWS : (c + 1) * ROWS, :] = velocity - strength * (velocity - targets[c])
    level_target = jax.nn.sigmoid(4.0 * (targets[3] - r["height"][...]))
    fraction = r["FRAC"][...]
    r["fraction_out"][...] = fraction - strength * (fraction - level_target)

    for copy in sent:
        copy.wait_send()


def on_device(
    source, water_depth, potential_start, velocity, fraction, pressure, neighbour, send_slot,
    face_normal, face_weight, step_scale, height, blend_weight, corner, stencil_weight, receive_cell,
):
    def lanes(array):
        return array.reshape(-1, 128)

    args = (
        source, water_depth, potential_start, lanes(velocity), lanes(fraction), lanes(pressure), lanes(neighbour),
        send_slot[:, 0, 0], lanes(face_normal), lanes(face_weight), lanes(step_scale), lanes(height),
        lanes(blend_weight), lanes(corner), lanes(stencil_weight), lanes(receive_cell),
    )
    shapes = ((NZ, 16, 128), (3 * ROWS, 128), (ROWS, 128), (ROWS, 128))
    results = pl.pallas_call(
        kernel,
        name="step",
        out_shape=[jax.ShapeDtypeStruct(shape, F32) for shape in shapes],
        in_specs=[pl.BlockSpec(memory_space=pltpu.VMEM)] * len(args),
        out_specs=[pl.BlockSpec(memory_space=pltpu.VMEM)] * len(shapes),
        scratch_shapes=list(scratch_plan().values()),
        compiler_params=pltpu.CompilerParams(
            collective_id=0, has_side_effects=True, vmem_limit_bytes=48 * 1024 * 1024
        ),
    )(*args)
    potential, velocity_out, fraction_out, pressure_out = results
    return (
        potential,
        velocity_out.reshape(3, 1, 1, -1),
        fraction_out.reshape(1, 1, -1),
        pressure_out.reshape(1, 1, -1),
    )


def solution(mesh):
    in_specs = (
        P(None, "px", "py"),
        P("px", "py"),
        P(None, "px", "py"),
        P(None, "px", "py", None),
        P("px", "py", None),
        P("px", "py", None),
        P(None, "px", "py", None),
        P(None, "px", "py", None),
        P(None, None, "px", "py", None),
        P(None, "px", "py", None),
        P("px", "py", None),
        P("px", "py", None),
        P("px", "py", None),
        P("px", "py", None),
        P(None, None, "px", "py", None),
        P("px", "py", None),
    )
    out_specs = (
        P(None, "px", "py"),
        P(None, "px", "py", None),
        P("px", "py", None),
        P("px", "py", None),
    )
    return jax.shard_map(on_device, mesh=mesh, in_specs=in_specs, out_specs=out_specs, check_vma=False)
```

```python
from types import SimpleNamespace

import jax
import jax.numpy as jnp
from jax import lax
from jax.experimental import pallas as pl
from jax.experimental.pallas import tpu as pltpu
from jax.sharding import PartitionSpec as P

F32 = jnp.float32
I32 = jnp.int32
MESH = pl.DeviceIdType.MESH
NPX, NPY = 32, 8
NZ = 17
FACES = 6
ROWS = 32
EXT = 40
PAD = 8
VERT = 0.01
RELAX = 0.8
REACH = 7

GATHER_DIMS = lax.GatherDimensionNumbers(
    offset_dims=(),
    collapsed_slice_dims=(1,),
    start_index_map=(1,),
    operand_batching_dims=(0,),
    start_indices_batching_dims=(0,),
)


def lane_gather(values, lanes):
    return lax.gather(
        values,
        lanes[..., None],
        GATHER_DIMS,
        slice_sizes=(1, 1),
        mode=lax.GatherScatterMode.PROMISE_IN_BOUNDS,
    )


def lane_iota(rows):
    return lax.broadcasted_iota(I32, (rows, 128), 1)


def row_iota(rows):
    return lax.broadcasted_iota(I32, (rows, 128), 0)


def roll(values, shift, axis):
    shift = shift % values.shape[axis]
    return values if shift == 0 else pltpu.roll(values, shift, axis)


def over_layers(body, chunk=4):
    whole = NZ // chunk
    if whole > 1:

        @pl.loop(0, whole)
        def _(step):
            body([step * chunk + j for j in range(chunk)])

    rest = list(range(whole * chunk if whole > 1 else 0, NZ))
    if rest:
        body(rest)


def each_layer(body, chunk=4):
    def bodies(layers):
        for k in layers:
            body(k)

    over_layers(bodies, chunk)


def kind(k):
    return min(k, 1) if isinstance(k, int) else jnp.minimum(k, 1)


def inside_of(x, y, rows, row_first, lane_split, width, height, depth):
    row = row_iota(rows) + row_first
    lane = lane_iota(rows)
    column = jnp.where(lane < lane_split, lane, lane - 128) + y * width
    return (row >= 0) & (row < height) & (column >= 0) & (column < depth)


def set_coefficients(level, depth, inside, scale):
    rows = depth.shape[0]
    half = 0.5 * scale
    faces = (
        half * (depth + roll(depth, rows - 1, 0)),
        half * (depth + roll(depth, 1, 0)),
        half * (depth + roll(depth, 127, 1)),
        half * (depth + roll(depth, 1, 1)),
    )
    total = faces[0] + faces[1] + faces[2] + faces[3]
    for i, face in enumerate(faces):
        level.C[i] = face
    for i, extra in enumerate((VERT, 2 * VERT)):
        diagonal = total + extra
        level.D[i] = diagonal
        level.W[i] = jnp.where(inside, RELAX / diagonal, 0.0)


def point_step(level):
    def body(k):
        level.V[k + 1, PAD : PAD + level.R, :] = level.W[kind(k)] * level.B[k]

    each_layer(body)


CHUNK = {24: NZ, 64: 8, 32: NZ, 16: NZ}


def operate(level, source, target, residual):
    def body(layers):
        for lo in range(0, level.R, 8):
            rows, mid = slice(lo, lo + 8), slice(PAD + lo, PAD + lo + 8)
            up, down = slice(PAD + lo + 1, PAD + lo + 9), slice(PAD + lo - 1, PAD + lo + 7)
            faces = [level.C[i, rows, :] for i in range(4)]
            below, values = source[layers[0], mid, :], source[layers[0] + 1, mid, :]
            for k in layers:
                above = source[k + 2, mid, :]
                total = faces[0] * source[k + 1, up, :] + faces[1] * source[k + 1, down, :]
                total = total + (faces[2] * roll(values, 127, 1) + faces[3] * roll(values, 1, 1))
                total = (total + VERT * (below + above)) + level.B[k, rows, :]
                if residual:
                    target[k, rows, :] = total - level.D[kind(k), rows, :] * values
                else:
                    target[k + 1, mid, :] = (1.0 - RELAX) * values + level.W[kind(k), rows, :] * total
                below, values = values, above

    over_layers(body, CHUNK[level.R])


def sweep_step(level, source, target):
    operate(level, source, target, False)


def pair_mean_rows(even, odd):
    total = even + odd
    return 0.25 * (total + roll(total, 127, 1))


def coarsen_step(fine, coarse):
    half = coarse.R
    lanes = (2 * lane_iota(half)) & 127

    def body(k):
        total = pair_mean_rows(fine.T[k, pl.ds(0, half, stride=2), :], fine.T[k, pl.ds(1, half, stride=2), :])
        coarse.B[k] = lane_gather(total, lanes)

    each_layer(body)


def refine_add(correction, first, fine, target, lane_split):
    rows = fine.R
    half = rows // 2
    lane = lane_iota(half)
    lanes = jnp.where(lane < lane_split, lane >> 1, (lane >> 1) + 64)

    def body(k):
        spread = lane_gather(correction[k + 1, PAD + first : PAD + first + half, :], lanes)
        fine.T[k, pl.ds(0, half, stride=2), :] = spread
        fine.T[k, pl.ds(1, half, stride=2), :] = spread
        target[k + 1, PAD : PAD + rows, :] = target[k + 1, PAD : PAD + rows, :] + fine.T[k]

    each_layer(body)


def fine_operate(top, source, target, residual, lo, hi):
    lane = lane_iota(8)
    first, last = lane == 0, lane == 127

    def body(layers):
        for start in range(lo, hi, 8):
            rows, mid = slice(start, start + 8), slice(PAD + start, PAD + start + 8)
            up, down = slice(PAD + start + 1, PAD + start + 9), slice(PAD + start - 1, PAD + start + 7)
            faces = [[top.C[s][i, rows, :] for i in range(4)] for s in range(2)]
            below = [source[s][layers[0], mid, :] for s in range(2)]
            values = [source[s][layers[0] + 1, mid, :] for s in range(2)]
            for k in layers:
                above = [source[s][k + 2, mid, :] for s in range(2)]
                rights = [roll(values[s], 127, 1) for s in range(2)]
                lefts = [roll(values[s], 1, 1) for s in range(2)]
                for s in range(2):
                    right = jnp.where(last, rights[1 - s], rights[s])
                    left = jnp.where(first, lefts[1 - s], lefts[s])
                    total = faces[s][0] * source[s][k + 1, up, :] + faces[s][1] * source[s][k + 1, down, :]
                    total = total + (faces[s][2] * right + faces[s][3] * left)
                    total = (total + VERT * (below[s] + above[s])) + top.B[s][k, rows, :]
                    if residual:
                        value = total - top.D[s][kind(k), rows, :] * values[s]
                    else:
                        value = (1.0 - RELAX) * values[s] + top.W[s][kind(k), rows, :] * total
                    target[s][k + 1, mid, :] = value
                below, values = values, above

    over_layers(body, 4)


def table_gather(read_row, count, components, hi, lo):
    picked = [jnp.zeros((8, 128), F32) for _ in range(components)]
    for j in range(count):
        mask = hi == j
        for c in range(components):
            row = jnp.broadcast_to(read_row(c, j), (8, 128))
            picked[c] = jnp.where(mask, lane_gather(row, lo), picked[c])
    return picked


CHANNELS = (4, 4, 1, 1, 1)


def scratch_plan():
    def vmem(*shape, dtype=F32):
        return pltpu.VMEM(shape, dtype)

    def pair(*shape):
        return [vmem(*shape), vmem(*shape)]

    def sems(count):
        return [pltpu.SemaphoreType.DMA((count,)), pltpu.SemaphoreType.DMA((count,))]

    def level(rows):
        return dict(
            V=vmem(NZ + 2, rows + 2 * PAD, 128),
            U=vmem(NZ + 2, rows + 2 * PAD, 128),
            B=vmem(NZ, rows, 128),
            T=vmem(NZ, rows, 128),
            C=vmem(4, rows, 128),
            W=vmem(2, rows, 128),
            D=vmem(2, rows, 128),
            E=vmem(rows, 128),
        )

    return dict(
        V=pair(NZ + 2, 48 + 2 * PAD, 128),
        U=pair(NZ + 2, 48 + 2 * PAD, 128),
        B=pair(NZ, 48, 128),
        C=pair(4, 48, 128),
        W=pair(2, 48, 128),
        D=pair(2, 48, 128),
        E=pair(48, 128),
        levels=[level(24), level(64), level(32), level(16)],
        M1=vmem(24, 128),
        first=vmem(5, 16, 128),
        final=vmem(5, 16, 128),
        strips=vmem(6, 5, 16, 128),
        P=pair(5, 4, 128),
        G=pair(16, 3, 5, 4, 128),
        near=pair(9, 9, 8, 128),
        mine=pair(9, 8, 128),
        HI=vmem(FACES * ROWS, 128, dtype=I32),
        LO=vmem(FACES * ROWS, 128, dtype=I32),
        SI=vmem(8, 128, dtype=I32),
        TQ=vmem(4 * EXT, 128),
        TS=vmem(4 * EXT, 128),
        TP=[vmem(EXT, 128) for _ in range(3)],
        CS=[vmem(n, 8, 128) for n in CHANNELS],
        CR=[vmem(4, n, 8, 128) for n in CHANNELS],
        FRAC=vmem(ROWS, 128),
        DIV=vmem(ROWS, 128),
        IWS=vmem(ROWS, 128),
        COR=vmem(3 * ROWS, 128),
        INV=vmem(2 * ROWS, 128, dtype=I32),
        S=vmem(256, 128),
        RB=vmem(256, 128),
        neighbour=vmem(FACES * ROWS, 128, dtype=I32),
        slot=vmem(4, 1, 1, 192, dtype=I32),
        normal=vmem(3 * FACES * ROWS, 128),
        weight=vmem(FACES * ROWS, 128),
        step=vmem(ROWS, 128),
        height=vmem(ROWS, 128),
        blend=vmem(ROWS, 128),
        corner=vmem(ROWS, 128, dtype=I32),
        stencil=vmem(32 * ROWS, 128),
        receive=vmem(ROWS, 128, dtype=I32),
        load=pltpu.SemaphoreType.DMA((20,)),
        s_tile=sems(6),
        s_strip=sems(6),
        s_deep=[sems(48), sems(48)],
        s_near=[sems(9), sems(9)],
        s_all=sems(32),
        s_cfd=[sems(4) for _ in range(5)],
    )


def kernel(*refs):
    (source_in, depth_in, start_in, velocity_in, fraction_in, pressure_in, neighbour_in, slot_in, normal_in,
     weight_in, step_in, height_in, blend_in, corner_in, stencil_in, receive_in,
     potential_out, velocity_out, fraction_out, pressure_out) = refs[:20]
    plan = scratch_plan()
    r = SimpleNamespace(**jax.tree_util.tree_unflatten(jax.tree_util.tree_structure(plan), refs[20:]))
    levels = [None] + [
        SimpleNamespace(R=rows, **fields) for rows, fields in zip((24, 64, 32, 16), r.levels)
    ]
    x, y = lax.axis_index("px"), lax.axis_index("py")

    def at(dx, dy):
        return (lax.rem(x + dx + NPX, NPX), lax.rem(y + dy + NPY, NPY))

    def send(source, target, semaphores, slot, where):
        copy = pltpu.make_async_remote_copy(
            src_ref=source,
            dst_ref=target,
            send_sem=semaphores[0].at[slot],
            recv_sem=semaphores[1].at[slot],
            device_id=where,
            device_id_type=MESH,
        )
        copy.start()
        return copy

    sent = []

    barrier = pltpu.get_barrier_semaphore()
    partners = [(dx, 0) for dx in range(1, NPX)]
    partners += [(dx, dy) for dx in range(-REACH, REACH + 1) for dy in (-1, 1)]
    for dx, dy in partners:
        pl.semaphore_signal(barrier, inc=1, device_id=at(dx, dy), device_id_type=MESH)

    middle = pl.ds(PAD + 16, 16)
    moves = [(velocity_in.at[pl.ds(c * ROWS, ROWS), :], r.TQ.at[pl.ds(c * EXT, ROWS), :]) for c in range(3)]
    moves += [
        (fraction_in, r.TQ.at[pl.ds(3 * EXT, ROWS), :]),
        (slot_in, r.slot),
        (start_in, r.V[0].at[pl.ds(1, NZ), middle, :]),
        (source_in, r.B[0].at[:, pl.ds(16, 16), :]),
        (depth_in, r.E[0].at[pl.ds(16, 16), :]),
        (receive_in, r.receive),
        (neighbour_in, r.neighbour),
        (normal_in, r.normal),
        (step_in, r.step),
        (pressure_in, r.TS.at[pl.ds(3 * EXT, ROWS), :]),
        (weight_in, r.weight),
        (corner_in, r.corner),
        (stencil_in, r.stencil),
        (height_in, r.height),
        (blend_in, r.blend),
    ]
    loads = [pltpu.make_async_copy(a, b, r.load.at[i]) for i, (a, b) in enumerate(moves)]
    for load in loads:
        load.start()

    def loaded(first, last):
        for load in loads[first:last]:
            load.wait()

    for rows, refs_of in [(48, r.V + r.U)] + [(level.R, [level.V, level.U]) for level in levels[1:]]:
        for ref in refs_of:
            ref[0] = jnp.zeros((rows + 2 * PAD, 128), F32)
            ref[NZ + 1] = jnp.zeros((rows + 2 * PAD, 128), F32)
            ref[1 : NZ + 1, 0:PAD, :] = jnp.zeros((NZ, PAD, 128), F32)
            ref[1 : NZ + 1, PAD + rows : 2 * PAD + rows, :] = jnp.zeros((NZ, PAD, 128), F32)
    for cycle in range(2):
        r.G[cycle][0] = jnp.zeros((3, 5, 4, 128), F32)

    loaded(0, 5)
    r.SI[...] = jnp.zeros((8, 128), I32)
    for b in range(4):
        r.SI[b : b + 1, :] = r.slot[b, 0, :, 0:128]
        r.SI[4 + b : 5 + b, 0:64] = r.slot[b, 0, :, 128:192]
    send_hi, send_lo = r.SI[...] >> 7, r.SI[...] & 127

    def reader(table):
        return lambda c, j: table[c * EXT + j : c * EXT + j + 1, :]

    def cfd_send(i, table):
        values = table_gather(reader(table), ROWS, CHANNELS[i], send_hi, send_lo)
        for c in range(CHANNELS[i]):
            r.CS[i][c] = values[c]

    def cfd_start(i):
        copies = []
        for slot, (dx, dy) in enumerate(((1, 0), (-1, 0), (0, 1), (0, -1))):
            copies.append(send(r.CS[i], r.CR[i].at[slot], r.s_cfd[i], slot, at(dx, dy)))
        return copies

    there = (x > 0, x < NPX - 1, y > 0, y < NPY - 1)
    block = (1, 0, 3, 2)

    def cfd_wait(i, table, copies):
        for copy in copies:
            copy.wait_recv()
        sent.extend(copies)
        for c in range(CHANNELS[i]):
            for b in range(4):
                for h in range(2):
                    row = r.CR[i][b, c, block[b] + 4 * h : block[b] + 4 * h + 1, :]
                    place = c * EXT + ROWS + 2 * b + h
                    table[place : place + 1, :] = jnp.where(there[b], row, 0.0)

    cfd_send(0, r.TQ)

    loaded(5, 8)
    lane16 = lane_iota(16)
    groups_f = [jnp.zeros((16, 128), F32) for _ in range(5)]
    groups_l = [jnp.zeros((16, 128), F32) for _ in range(5)]
    for t in range(2 * NZ + 1):
        if t < NZ:
            tile = r.V[0][t + 1, PAD + 16 : PAD + 32, :]
        elif t < 2 * NZ:
            tile = r.B[0][t - NZ, 16:32, :]
        else:
            tile = r.E[0][16:32, :]
        g, q = t // 8, t % 8
        own = (lane16 >= 16 * q) & (lane16 < 16 * q + 16)
        groups_f[g] = jnp.where(own, roll(tile, 16 * q, 1), groups_f[g])
        groups_l[g] = jnp.where(own, roll(tile, 16 * q + 16, 1), groups_l[g])
    for g in range(5):
        r.first[g] = groups_f[g]
        r.final[g] = groups_l[g]

    pl.semaphore_wait(barrier, len(partners))

    copies0 = cfd_start(0)
    strips = []
    for dx in (-1, 0, 1):
        slot = 2 * (1 - dx)
        strips.append(send(r.final, r.strips.at[slot], r.s_strip, slot, at(dx, 1)))
        strips.append(send(r.first, r.strips.at[slot + 1], r.s_strip, slot + 1, at(dx, -1)))
    tiles = []
    for s, (dx, row) in enumerate(((1, 0), (-1, 32))):
        padded = pl.ds(PAD + row, 16)
        rows = pl.ds(row, 16)
        tiles.append(send(start_in, r.V[0].at[pl.ds(1, NZ), padded, :], r.s_tile, 3 * s, at(dx, 0)))
        tiles.append(send(source_in, r.B[0].at[:, rows, :], r.s_tile, 3 * s + 1, at(dx, 0)))
        tiles.append(send(depth_in, r.E[0].at[rows, :], r.s_tile, 3 * s + 2, at(dx, 0)))

    loaded(8, 10)
    cells = r.receive[...]
    hi_of, lo_of = cells >> 7, cells & 127
    inverse = jnp.zeros((2 * ROWS, 128), F32)
    for chunk in range(4):
        lefts, rights = [], []
        for o in range(8 * chunk, 8 * chunk + 8):
            match = row_iota(ROWS) == jnp.broadcast_to(hi_of[o : o + 1, :], (ROWS, 128))
            lanes = lane_iota(ROWS).astype(F32)
            lefts.append(
                jnp.concatenate([jnp.where(match, F32(o + 1), 0.0), jnp.where(match, lanes, 0.0)], axis=0)
            )
            low = row_iota(128) == jnp.broadcast_to(lo_of[o : o + 1, :], (128, 128))
            rights.append(jnp.where(low, F32(1.0), 0.0))
        left = jnp.concatenate(lefts, axis=1).astype(jnp.bfloat16)
        right = jnp.concatenate(rights, axis=1).astype(jnp.bfloat16)
        inverse = inverse + lax.dot_general(
            left, right, (((1,), (1,)), ((), ())), preferred_element_type=F32
        )
    r.INV[...] = inverse.astype(I32)

    index = r.neighbour[...]
    for edge in (4288, 4480, 4672, 4864):
        index = index + jnp.where(r.neighbour[...] >= edge, 64, 0)
    r.HI[...] = index >> 7
    r.LO[...] = index & 127

    cfd_wait(0, r.TQ, copies0)
    loaded(10, 13)

    def part(f, quarter):
        return pl.ds(pl.multiple_of(f * ROWS + 8 * quarter, 8), 8)

    def cells_of(base, quarter):
        return pl.ds(pl.multiple_of(base + 8 * quarter, 8), 8)

    def beside_of(table, components, f, quarter):
        rows = part(f, quarter)
        return table_gather(reader(table), EXT, components, r.HI[rows, :], r.LO[rows, :])

    def normal_of(c, f, quarter):
        return r.normal[part(c * FACES + f, quarter), :]

    zero = jnp.zeros((8, 128), F32)

    @pl.loop(0, 4)
    def _(quarter):
        mine = [r.TQ[cells_of(c * EXT, quarter), :] for c in range(4)]

        def face(f, totals):
            beside = beside_of(r.TQ, 4, f, quarter)
            flux = normal_of(0, f, quarter) * (mine[0] + beside[0])
            for c in (1, 2):
                flux = flux + normal_of(c, f, quarter) * (mine[c] + beside[c])
            flux = 0.5 * flux
            out, into = jnp.maximum(flux, 0.0), jnp.minimum(flux, 0.0)
            return tuple(totals[c] + (out * mine[c] + into * beside[c]) for c in range(4))

        totals = lax.fori_loop(0, FACES, face, (zero,) * 4)
        scale = r.step[cells_of(0, quarter), :]
        for c in range(3):
            r.TS[cells_of(c * EXT, quarter), :] = mine[c] - scale * totals[c]
        r.FRAC[cells_of(0, quarter), :] = mine[3] - scale * totals[3]

    cfd_send(1, r.TS)
    copies1 = cfd_start(1)

    for copy in tiles + strips:
        copy.wait_recv()
    sent.extend(tiles + strips)
    for block_row in range(3):
        rows = slice(16 * block_row, 16 * block_row + 16)
        padded = slice(PAD + 16 * block_row, PAD + 16 * block_row + 16)
        for t in range(2 * NZ + 1):
            g, q = t // 8, t % 8
            lower = r.strips[2 * block_row, g]
            upper = r.strips[2 * block_row + 1, g]
            value = jnp.where(
                lane16 < 16,
                roll(upper, -16 * q, 1),
                jnp.where(lane16 >= 112, roll(lower, 112 - 16 * q, 1), 0.0),
            )
            if t < NZ:
                r.V[1][t + 1, padded, :] = value
            elif t < 2 * NZ:
                r.B[1][t - NZ, rows, :] = value
            else:
                r.E[1][rows, :] = value

    fine_rows = row_iota(48) + 16 * (x - 1)
    inside_a = (fine_rows >= 0) & (fine_rows < 16 * NPX)
    side_ok = jnp.where(lane_iota(48) < 64, jnp.where(y < NPY - 1, 1, 0), jnp.where(y > 0, 1, 0)) > 0
    insides = [inside_a, inside_a & side_ok]
    data = slice(PAD, PAD + 48)

    def mask_start(k):
        for s in range(2):
            r.V[s][k + 1, data, :] = jnp.where(insides[s], r.V[s][k + 1, data, :], 0.0)

    each_layer(mask_start)

    depths = [jnp.where(insides[s], r.E[s][...], 0.0) for s in range(2)]
    lane48 = lane_iota(48)
    for s in range(2):
        depth, other = depths[s], depths[1 - s]
        r.E[s][...] = depth
        right = jnp.where(lane48 == 127, roll(other, 127, 1), roll(depth, 127, 1))
        left = jnp.where(lane48 == 0, roll(other, 1, 1), roll(depth, 1, 1))
        faces = (
            0.5 * (depth + roll(depth, 47, 0)),
            0.5 * (depth + roll(depth, 1, 0)),
            0.5 * (depth + right),
            0.5 * (depth + left),
        )
        total = faces[0] + faces[1] + faces[2] + faces[3]
        for i, face in enumerate(faces):
            r.C[s][i] = face
        for i, extra in enumerate((VERT, 2 * VERT)):
            r.D[s][i] = total + extra
            r.W[s][i] = jnp.where(insides[s], RELAX / (total + extra), 0.0)

    def fine_sweep(source, target, lo=0, hi=48):
        fine_operate(r, source, target, False, lo, hi)

    lane24 = lane_iota(24)
    down24 = (2 * lane24) & 127

    def fine_pair(a_even, a_odd, b_even, b_odd):
        mean_a = lane_gather(pair_mean_rows(a_even, a_odd), down24)
        mean_b = lane_gather(pair_mean_rows(b_even, b_odd), down24)
        return jnp.where(lane24 < 64, mean_a, mean_b)

    even24, odd24 = pl.ds(0, 24, stride=2), pl.ds(1, 24, stride=2)
    even_pad, odd_pad = pl.ds(PAD, 24, stride=2), pl.ds(PAD + 1, 24, stride=2)
    inside_1 = inside_of(x, y, 24, 8 * (x - 1), 96, 64, 8 * NPX, 64 * NPY)
    r.M1[...] = jnp.where(inside_1, F32(1.0), 0.0)
    depth_1 = fine_pair(r.E[0][even24, :], r.E[0][odd24, :], r.E[1][even24, :], r.E[1][odd24, :])
    depth_1 = jnp.where(inside_1, depth_1, 0.0)
    levels[1].E[...] = depth_1
    set_coefficients(levels[1], depth_1, inside_1, 0.25)

    def fine_coarsen(k):
        levels[1].B[k] = fine_pair(
            r.U[0][k + 1, even_pad, :], r.U[0][k + 1, odd_pad, :],
            r.U[1][k + 1, even_pad, :], r.U[1][k + 1, odd_pad, :],
        )

    lane8 = lane_iota(8)

    lane4 = lane_iota(4)

    def pack_deep(cycle):
        count = NZ + 1 if cycle == 0 else NZ
        even, odd = pl.ds(8, 4, stride=2), pl.ds(9, 4, stride=2)
        for g in range(5):
            packed = jnp.zeros((4, 128), F32)
            for q in range(4):
                k = 4 * g + q
                if k >= count:
                    continue
                if k < NZ:
                    mean = pair_mean_rows(levels[1].T[k, even, :], levels[1].T[k, odd, :])
                else:
                    mean = pair_mean_rows(levels[1].E[even, :], levels[1].E[odd, :])
                own = (lane4 >= 32 * q) & (lane4 < 32 * q + 32)
                packed = jnp.where(own, lane_gather(mean, (2 * lane4 + 64 * (q % 2)) & 127), packed)
            r.P[cycle][g] = packed
            r.G[cycle][8, 1, g] = packed

    def start_deep(cycle):
        copies = []
        for dx in range(-REACH, REACH + 1):
            for dy in (-1, 0, 1):
                if dx == 0 and dy == 0:
                    continue
                d, j = 8 - dx, 1 - dy
                copies.append(send(r.P[cycle], r.G[cycle].at[d, j], r.s_deep[cycle], 3 * d + j, at(dx, dy)))
        return copies

    def unpack_deep(cycle):
        grid_of = r.G[cycle]

        @pl.loop(0, 8)
        def _(m):
            rows = pl.ds(pl.multiple_of(8 * m, 8), 8)
            for g in range(5):
                tiles_of = [
                    jnp.concatenate([grid_of[2 * m, j, g], grid_of[2 * m + 1, j, g]], axis=0) for j in range(3)
                ]
                for q in range(4):
                    k = 4 * g + q
                    if k > NZ or (k == NZ and cycle > 0):
                        continue
                    value = jnp.where(
                        lane8 < 32,
                        roll(tiles_of[1], -32 * q, 1),
                        jnp.where(
                            lane8 < 64,
                            roll(tiles_of[2], 32 - 32 * q, 1),
                            roll(tiles_of[0], 96 - 32 * q, 1),
                        ),
                    )
                    if k < NZ:
                        levels[2].B[k, rows, :] = value
                    else:
                        levels[2].E[rows, :] = value

    def deep_coefficients():
        for level, tile, width in ((2, 4, 32), (3, 2, 16), (4, 1, 8)):
            here = levels[level]
            rows = here.R
            inside = inside_of(x, y, rows, tile * (x - 8), 64, width, tile * NPX, width * NPY)
            if level > 2:
                above = levels[level - 1].E
                mean = pair_mean_rows(above[pl.ds(0, rows, stride=2), :], above[pl.ds(1, rows, stride=2), :])
                depth = lane_gather(mean, (2 * lane_iota(rows)) & 127)
            else:
                depth = here.E[...]
            depth = jnp.where(inside, depth, 0.0)
            here.E[...] = depth
            set_coefficients(here, depth, inside, 0.25**level)

    def solve_deep():
        for level in (2, 3):
            here = levels[level]
            point_step(here)
            sweep_step(here, here.V, here.U)
            operate(here, here.U, here.T, True)
            coarsen_step(here, levels[level + 1])
        last = levels[4]
        point_step(last)
        sweep_step(last, last.V, last.U)
        sweep_step(last, last.U, last.V)
        sweep_step(last, last.V, last.U)
        for level, first, split in ((3, 0, 64), (2, 0, 64), (1, 28, 96)):
            here = levels[level]
            refine_add(levels[level + 1].U, first, here, here.U, split)
            sweep_step(here, here.U, here.V)
            sweep_step(here, here.V, here.U)

    def down(lo, hi):
        fine_operate(r, r.V, r.U, True, lo, hi)
        each_layer(fine_coarsen)
        point_step(levels[1])
        sweep_step(levels[1], levels[1].V, levels[1].U)
        operate(levels[1], levels[1].U, levels[1].T, True)

    def start_near(cycle):
        own = slice(PAD + 8, PAD + 16)
        for pair in range(9):
            value = levels[1].U[2 * pair + 1, own, :]
            if 2 * pair + 1 < NZ:
                value = jnp.where(lane8 < 64, value, roll(levels[1].U[2 * pair + 2, own, :], 64, 1))
            r.mine[cycle][pair] = value
            r.near[cycle][4, pair] = value
        copies = []
        for dx in (-1, 0, 1):
            for dy in (-1, 0, 1):
                if dx or dy:
                    slot = 3 * (1 - dx) + 1 - dy
                    copies.append(send(r.mine[cycle], r.near[cycle].at[slot], r.s_near[cycle], slot, at(dx, dy)))
        return copies

    def add_near(cycle):
        got = r.near[cycle]
        half_lane = lane24 >> 1
        for k in range(NZ):
            pair, odd = k // 2, k % 2
            for block_row in range(3):
                lower, middle, upper = (got[3 * block_row + j, pair] for j in range(3))
                aside = jnp.where(lane8 < 96 if odd else lane8 < 32, upper, lower)
                value = jnp.where(lane8 < 64, roll(middle, 64 * odd, 1), roll(aside, 64 - 64 * odd, 1))
                levels[1].T[k, 8 * block_row : 8 * block_row + 8, :] = value

        def body(k):
            value = levels[1].T[k] * r.M1[...]
            for s, lanes in ((0, half_lane), (1, half_lane + 64)):
                spread = lane_gather(value, lanes)
                r.U[s][k + 1, even_pad, :] = spread
                r.U[s][k + 1, odd_pad, :] = spread
                r.V[s][k + 1, data, :] = r.V[s][k + 1, data, :] + r.U[s][k + 1, data, :]

        each_layer(body)

    fine_sweep(r.V, r.U)
    fine_sweep(r.U, r.V)
    down(0, 48)
    pack_deep(0)
    deep0 = start_deep(0)

    cfd_wait(1, r.TS, copies1)
    loaded(13, 14)

    @pl.loop(0, 4)
    def _(quarter):
        mine = [r.TS[cells_of(c * EXT, quarter), :] for c in range(3)]

        def face(f, carry):
            flow, pull, weights = carry
            beside = beside_of(r.TS, 4, f, quarter)
            for c in range(3):
                flow = flow + normal_of(c, f, quarter) * (mine[c] + beside[c])
            weight = r.weight[part(f, quarter), :]
            return flow, pull + weight * beside[3], weights + weight

        flow, pull, weights = lax.fori_loop(0, FACES, face, (zero,) * 3)
        here = cells_of(0, quarter)
        flow, inverse_sum = 0.5 * flow, 1.0 / weights
        r.DIV[here, :] = flow
        r.IWS[here, :] = inverse_sum
        r.TP[0][here, :] = (pull - flow) * inverse_sum

    cfd_send(2, r.TP[0])
    copies2 = cfd_start(2)

    for copy in deep0:
        copy.wait_recv()
    sent.extend(deep0)
    unpack_deep(0)
    deep_coefficients()
    solve_deep()
    near0 = start_near(0)

    def pressure_sweep(before, after):
        @pl.loop(0, 4)
        def _(quarter):
            pull = zero
            for f in range(FACES):
                pull = pull + r.weight[part(f, quarter), :] * beside_of(before, 1, f, quarter)[0]
            here = cells_of(0, quarter)
            after[here, :] = (pull - r.DIV[here, :]) * r.IWS[here, :]

    cfd_wait(2, r.TP[0], copies2)
    pressure_sweep(r.TP[0], r.TP[1])
    cfd_send(3, r.TP[1])
    copies3 = cfd_start(3)

    for copy in near0:
        copy.wait_recv()
    sent.extend(near0)
    add_near(0)
    fine_sweep(r.V, r.U)
    fine_sweep(r.U, r.V)
    fine_sweep(r.V, r.U)
    fine_sweep(r.U, r.V)
    down(8, 40)
    pack_deep(1)
    deep1 = start_deep(1)

    cfd_wait(3, r.TP[1], copies3)
    pressure_sweep(r.TP[1], r.TP[2])
    pressure_out[...] = r.TP[2][0:ROWS, :]
    cfd_send(4, r.TP[2])
    copies4 = cfd_start(4)

    for copy in deep1:
        copy.wait_recv()
    sent.extend(deep1)
    unpack_deep(1)
    solve_deep()
    near1 = start_near(1)

    cfd_wait(4, r.TP[2], copies4)

    @pl.loop(0, 4)
    def _(quarter):
        here = cells_of(0, quarter)
        pressure = r.TP[2][here, :]
        totals = [zero] * 3
        for f in range(FACES):
            difference = beside_of(r.TP[2], 1, f, quarter)[0] - pressure
            totals = [totals[c] + normal_of(c, f, quarter) * difference for c in range(3)]
        for c in range(3):
            r.COR[cells_of(c * ROWS, quarter), :] = r.TS[cells_of(c * EXT, quarter), :] - r.step[here, :] * (
                0.5 * totals[c]
            )

    for copy in near1:
        copy.wait_recv()
    sent.extend(near1)
    add_near(1)
    fine_sweep(r.V, r.U, 8, 40)
    fine_sweep(r.U, r.V, 8, 40)

    loaded(14, 18)

    own_rows = pl.ds(pl.multiple_of(x * 8, 8), 8)

    def interpolate(quarter):
        corner = r.corner[cells_of(0, quarter), :]
        column = corner & 127
        point_row = (corner >> 7) & 15
        point_layer = corner >> 11

        def layer(k, picks):
            found = []
            for lanes in (column, column + 1):
                low, high = zero, zero
                before = None
                for i in range(16):
                    row = jnp.broadcast_to(r.V[0][k + 1, PAD + 16 + i : PAD + 17 + i, :], (8, 128))
                    value = lane_gather(row, lanes)
                    here = point_row == i
                    if i < 15:
                        low = jnp.where(here, value, low)
                    if before is not None:
                        high = jnp.where(before, value, high)
                    before = here
                found.append((low, high))
            found = (found[0][0], found[1][0], found[0][1], found[1][1])
            lower, upper = point_layer == k, point_layer == k - 1
            return tuple(jnp.where(lower, found[i], picks[i]) for i in range(4)) + tuple(
                jnp.where(upper, found[i], picks[4 + i]) for i in range(4)
            )

        def layers(step, picks):
            return layer(2 * step + 1, layer(2 * step, picks))

        picks = layer(NZ - 1, lax.fori_loop(0, NZ // 2, layers, (zero,) * 8))
        for quantity in range(4):
            total = zero
            for p in range(8):
                total = total + r.stencil[cells_of((quantity * 8 + p) * ROWS, quarter), :] * picks[p]
            for i in range(8):
                r.S[pl.ds(64 * quarter + 8 * i + quantity, 1), :] = total[i : i + 1, :]

    everyone = []
    for away in (2, 1, 3, 0):
        quarter = lax.rem(x // 8 + away, 4)
        interpolate(quarter)
        for i in range(0 if away else 1, 8):
            there_x = quarter * 8 + (i if away else lax.rem(x + i, 8))
            rows = pl.ds(pl.multiple_of(there_x * 8, 8), 8)
            slot = lax.rem(there_x - x + NPX, NPX)
            everyone.append(send(r.S.at[rows, :], r.RB.at[own_rows, :], r.s_all, slot, (there_x, y)))
    r.RB[own_rows, :] = r.S[own_rows, :]
    potential_out[...] = r.V[0][1 : NZ + 1, PAD + 16 : PAD + 32, :]
    for o in range(1, NPX):
        pltpu.make_async_remote_copy(
            src_ref=r.S.at[0:8, :],
            dst_ref=r.RB.at[0:8, :],
            send_sem=r.s_all[0].at[o],
            recv_sem=r.s_all[1].at[o],
            device_id=at(o, 0),
            device_id_type=MESH,
        ).wait_recv()
    sent.extend(everyone)

    @pl.loop(0, 4)
    def _(quarter):
        here = cells_of(0, quarter)
        slot_hi, slot_lo = r.INV[here, :] - 1, r.INV[cells_of(ROWS, quarter), :]
        targets = table_gather(lambda c, j: r.RB[8 * j + c : 8 * j + c + 1, :], NPX, 4, slot_hi, slot_lo)
        strength = jnp.where(slot_hi >= 0, r.blend[here, :], 0.0)
        for c in range(3):
            velocity = r.COR[cells_of(c * ROWS, quarter), :]
            velocity_out[cells_of(c * ROWS, quarter), :] = velocity - strength * (velocity - targets[c])
        level_target = jax.nn.sigmoid(4.0 * (targets[3] - r.height[here, :]))
        fraction = r.FRAC[here, :]
        fraction_out[here, :] = fraction - strength * (fraction - level_target)

    for copy in sent:
        copy.wait_send()


def on_device(
    source, water_depth, potential_start, velocity, fraction, pressure, neighbour, send_slot,
    face_normal, face_weight, step_scale, height, blend_weight, corner, stencil_weight, receive_cell,
):
    def lanes(array):
        return array.reshape(-1, 128)

    args = (
        source, water_depth, potential_start, lanes(velocity), lanes(fraction), lanes(pressure), lanes(neighbour),
        send_slot, lanes(face_normal), lanes(face_weight), lanes(step_scale), lanes(height),
        lanes(blend_weight), lanes(corner), lanes(stencil_weight), lanes(receive_cell),
    )
    shapes = ((NZ, 16, 128), (3 * ROWS, 128), (ROWS, 128), (ROWS, 128))
    results = pl.pallas_call(
        kernel,
        name="step",
        out_shape=[jax.ShapeDtypeStruct(shape, F32) for shape in shapes],
        in_specs=[pl.BlockSpec(memory_space=pltpu.HBM)] * len(args),
        out_specs=[pl.BlockSpec(memory_space=pltpu.VMEM)] * len(shapes),
        scratch_shapes=jax.tree_util.tree_leaves(scratch_plan()),
        compiler_params=pltpu.CompilerParams(
            collective_id=0, has_side_effects=True, vmem_limit_bytes=67043328
        ),
    )(*args)
    potential, velocity_out, fraction_out, pressure_out = results
    return (
        potential,
        velocity_out.reshape(3, 1, 1, -1),
        fraction_out.reshape(1, 1, -1),
        pressure_out.reshape(1, 1, -1),
    )


def solution(mesh):
    in_specs = (
        P(None, "px", "py"),
        P("px", "py"),
        P(None, "px", "py"),
        P(None, "px", "py", None),
        P("px", "py", None),
        P("px", "py", None),
        P(None, "px", "py", None),
        P(None, "px", "py", None),
        P(None, None, "px", "py", None),
        P(None, "px", "py", None),
        P("px", "py", None),
        P("px", "py", None),
        P("px", "py", None),
        P("px", "py", None),
        P(None, None, "px", "py", None),
        P("px", "py", None),
    )
    out_specs = (
        P(None, "px", "py"),
        P(None, "px", "py", None),
        P("px", "py", None),
        P("px", "py", None),
    )
    return jax.shard_map(on_device, mesh=mesh, in_specs=in_specs, out_specs=out_specs, check_vma=False)
```

```python
from types import SimpleNamespace

import jax
import jax.numpy as jnp
from jax import lax
from jax.experimental import pallas as pl
from jax.experimental.pallas import tpu as pltpu
from jax.sharding import PartitionSpec as P

F32 = jnp.float32
I32 = jnp.int32
MESH = pl.DeviceIdType.MESH
NPX, NPY = 32, 8
NZ = 17
FACES = 6
ROWS = 32
EXT = 40
PAD = 8
VERT = 0.01
RELAX = 0.8
REACH = 7

GATHER_DIMS = lax.GatherDimensionNumbers(
    offset_dims=(),
    collapsed_slice_dims=(1,),
    start_index_map=(1,),
    operand_batching_dims=(0,),
    start_indices_batching_dims=(0,),
)


def lane_gather(values, lanes):
    return lax.gather(
        values,
        lanes[..., None],
        GATHER_DIMS,
        slice_sizes=(1, 1),
        mode=lax.GatherScatterMode.PROMISE_IN_BOUNDS,
    )


def lane_iota(rows):
    return lax.broadcasted_iota(I32, (rows, 128), 1)


def row_iota(rows):
    return lax.broadcasted_iota(I32, (rows, 128), 0)


def roll(values, shift, axis):
    shift = shift % values.shape[axis]
    return values if shift == 0 else pltpu.roll(values, shift, axis)


def over_layers(body, chunk=4):
    whole = NZ // chunk
    if whole > 1:

        @pl.loop(0, whole)
        def _(step):
            body([step * chunk + j for j in range(chunk)])

    rest = list(range(whole * chunk if whole > 1 else 0, NZ))
    if rest:
        body(rest)


def each_layer(body, chunk=4):
    def bodies(layers):
        for k in layers:
            body(k)

    over_layers(bodies, chunk)


def kind(k):
    return min(k, 1) if isinstance(k, int) else jnp.minimum(k, 1)


def inside_of(x, y, rows, row_first, lane_split, width, height, depth):
    row = row_iota(rows) + row_first
    lane = lane_iota(rows)
    column = jnp.where(lane < lane_split, lane, lane - 128) + y * width
    return (row >= 0) & (row < height) & (column >= 0) & (column < depth)


def set_coefficients(level, depth, inside, scale):
    rows = depth.shape[0]
    half = 0.5 * scale
    faces = (
        half * (depth + roll(depth, rows - 1, 0)),
        half * (depth + roll(depth, 1, 0)),
        half * (depth + roll(depth, 127, 1)),
        half * (depth + roll(depth, 1, 1)),
    )
    total = faces[0] + faces[1] + faces[2] + faces[3]
    for i, face in enumerate(faces):
        level.C[i] = face
    for i, extra in enumerate((VERT, 2 * VERT)):
        diagonal = total + extra
        level.D[i] = diagonal
        level.W[i] = jnp.where(inside, RELAX / diagonal, 0.0)


def point_step(level):
    def body(k):
        level.V[k + 1, PAD : PAD + level.R, :] = level.W[kind(k)] * level.B[k]

    each_layer(body)


def operate(level, source, target, residual):
    def body(layers):
        for lo in range(0, level.R, 8):
            rows, mid = slice(lo, lo + 8), slice(PAD + lo, PAD + lo + 8)
            up, down = slice(PAD + lo + 1, PAD + lo + 9), slice(PAD + lo - 1, PAD + lo + 7)
            faces = [level.C[i, rows, :] for i in range(4)]
            below, values = source[layers[0], mid, :], source[layers[0] + 1, mid, :]
            for k in layers:
                above = source[k + 2, mid, :]
                total = faces[0] * source[k + 1, up, :] + faces[1] * source[k + 1, down, :]
                total = total + (faces[2] * roll(values, 127, 1) + faces[3] * roll(values, 1, 1))
                total = (total + VERT * (below + above)) + level.B[k, rows, :]
                if residual:
                    target[k, rows, :] = total - level.D[kind(k), rows, :] * values
                else:
                    target[k + 1, mid, :] = (1.0 - RELAX) * values + level.W[kind(k), rows, :] * total
                below, values = values, above

    over_layers(body, NZ)


def sweep_step(level, source, target):
    operate(level, source, target, False)


def pair_mean_rows(even, odd):
    total = even + odd
    return 0.25 * (total + roll(total, 127, 1))


def coarsen_step(fine, coarse):
    half = coarse.R
    lanes = (2 * lane_iota(half)) & 127

    def body(k):
        total = pair_mean_rows(fine.T[k, pl.ds(0, half, stride=2), :], fine.T[k, pl.ds(1, half, stride=2), :])
        coarse.B[k] = lane_gather(total, lanes)

    each_layer(body)


def refine_add(correction, first, fine, target, lane_split):
    rows = fine.R
    half = rows // 2
    lane = lane_iota(half)
    lanes = jnp.where(lane < lane_split, lane >> 1, (lane >> 1) + 64)

    def body(k):
        spread = lane_gather(correction[k + 1, PAD + first : PAD + first + half, :], lanes)
        fine.T[k, pl.ds(0, half, stride=2), :] = spread
        fine.T[k, pl.ds(1, half, stride=2), :] = spread
        target[k + 1, PAD : PAD + rows, :] = target[k + 1, PAD : PAD + rows, :] + fine.T[k]

    each_layer(body)


def fine_operate(top, source, target, residual, lo, hi):
    lane = lane_iota(8)
    first, last = lane == 0, lane == 127

    def body(layers):
        for start in range(lo, hi, 8):
            rows, mid = slice(start, start + 8), slice(PAD + start, PAD + start + 8)
            up, down = slice(PAD + start + 1, PAD + start + 9), slice(PAD + start - 1, PAD + start + 7)
            faces = [[top.C[s][i, rows, :] for i in range(4)] for s in range(2)]
            below = [source[s][layers[0], mid, :] for s in range(2)]
            values = [source[s][layers[0] + 1, mid, :] for s in range(2)]
            for k in layers:
                above = [source[s][k + 2, mid, :] for s in range(2)]
                rights = [roll(values[s], 127, 1) for s in range(2)]
                lefts = [roll(values[s], 1, 1) for s in range(2)]
                for s in range(2):
                    right = jnp.where(last, rights[1 - s], rights[s])
                    left = jnp.where(first, lefts[1 - s], lefts[s])
                    total = faces[s][0] * source[s][k + 1, up, :] + faces[s][1] * source[s][k + 1, down, :]
                    total = total + (faces[s][2] * right + faces[s][3] * left)
                    total = (total + VERT * (below[s] + above[s])) + top.B[s][k, rows, :]
                    if residual:
                        value = total - top.D[s][kind(k), rows, :] * values[s]
                    else:
                        value = (1.0 - RELAX) * values[s] + top.W[s][kind(k), rows, :] * total
                    target[s][k + 1, mid, :] = value
                below, values = values, above

    over_layers(body, NZ)


def table_gather(read_row, count, components, hi, lo):
    picked = [jnp.zeros((8, 128), F32) for _ in range(components)]
    for j in range(count):
        mask = hi == j
        for c in range(components):
            row = jnp.broadcast_to(read_row(c, j), (8, 128))
            picked[c] = jnp.where(mask, lane_gather(row, lo), picked[c])
    return picked


CHANNELS = (4, 4, 1, 1, 1)


def scratch_plan():
    def vmem(*shape, dtype=F32):
        return pltpu.VMEM(shape, dtype)

    def pair(*shape):
        return [vmem(*shape), vmem(*shape)]

    def sems(count):
        return [pltpu.SemaphoreType.DMA((count,)), pltpu.SemaphoreType.DMA((count,))]

    def level(rows):
        return dict(
            V=vmem(NZ + 2, rows + 2 * PAD, 128),
            U=vmem(NZ + 2, rows + 2 * PAD, 128),
            B=vmem(NZ, rows, 128),
            T=vmem(NZ, rows, 128),
            C=vmem(4, rows, 128),
            W=vmem(2, rows, 128),
            D=vmem(2, rows, 128),
            E=vmem(rows, 128),
        )

    return dict(
        V=pair(NZ + 2, 48 + 2 * PAD, 128),
        U=pair(NZ + 2, 48 + 2 * PAD, 128),
        B=pair(NZ, 48, 128),
        C=pair(4, 48, 128),
        W=pair(2, 48, 128),
        D=pair(2, 48, 128),
        E=pair(48, 128),
        levels=[level(24), level(16), level(32), level(16)],
        M1=vmem(24, 128),
        first=vmem(5, 16, 128),
        final=vmem(5, 16, 128),
        strips=vmem(6, 5, 16, 128),
        P=pair(5, 4, 128),
        N=pair(3, 3, 5, 4, 128),
        P3=pair(3, 2, 128),
        G=pair(16, 3, 3, 2, 128),
        near=pair(2, 9, 8, 128),
        sides=pair(6, 2, 8, 128),
        mine=pair(9, 8, 128),
        left=pair(2, 8, 128),
        right=pair(2, 8, 128),
        HI=vmem(FACES * ROWS, 128, dtype=I32),
        LO=vmem(FACES * ROWS, 128, dtype=I32),
        SI=vmem(8, 128, dtype=I32),
        TQ=vmem(4 * EXT, 128),
        TS=vmem(4 * EXT, 128),
        TP=[vmem(EXT, 128) for _ in range(3)],
        CS=[vmem(n, 8, 128) for n in CHANNELS],
        CR=[vmem(4, n, 8, 128) for n in CHANNELS],
        FRAC=vmem(ROWS, 128),
        DIV=vmem(ROWS, 128),
        IWS=vmem(ROWS, 128),
        COR=vmem(3 * ROWS, 128),
        INV=vmem(2 * ROWS, 128, dtype=I32),
        S=vmem(256, 128),
        RB=vmem(256, 128),
        neighbour=vmem(FACES * ROWS, 128, dtype=I32),
        slot=vmem(4, 1, 1, 192, dtype=I32),
        normal=vmem(3 * FACES * ROWS, 128),
        weight=vmem(FACES * ROWS, 128),
        step=vmem(ROWS, 128),
        height=vmem(ROWS, 128),
        blend=vmem(ROWS, 128),
        corner=vmem(ROWS, 128, dtype=I32),
        stencil=vmem(32 * ROWS, 128),
        receive=vmem(ROWS, 128, dtype=I32),
        load=pltpu.SemaphoreType.DMA((20,)),
        s_tile=sems(6),
        s_strip=sems(6),
        s_deep=[sems(48), sems(48)],
        s_near=[sems(8), sems(8)],
        s_second=[sems(9), sems(9)],
        s_all=sems(32),
        s_cfd=[sems(4) for _ in range(5)],
    )


def kernel(*refs):
    (source_in, depth_in, start_in, velocity_in, fraction_in, pressure_in, neighbour_in, slot_in, normal_in,
     weight_in, step_in, height_in, blend_in, corner_in, stencil_in, receive_in,
     potential_out, velocity_out, fraction_out, pressure_out) = refs[:20]
    plan = scratch_plan()
    r = SimpleNamespace(**jax.tree_util.tree_unflatten(jax.tree_util.tree_structure(plan), refs[20:]))
    levels = [None] + [
        SimpleNamespace(R=rows, **fields) for rows, fields in zip((24, 16, 32, 16), r.levels)
    ]
    x, y = lax.axis_index("px"), lax.axis_index("py")

    def at(dx, dy):
        return (lax.rem(x + dx + NPX, NPX), lax.rem(y + dy + NPY, NPY))

    def send(source, target, semaphores, slot, where):
        copy = pltpu.make_async_remote_copy(
            src_ref=source,
            dst_ref=target,
            send_sem=semaphores[0].at[slot],
            recv_sem=semaphores[1].at[slot],
            device_id=where,
            device_id_type=MESH,
        )
        copy.start()
        return copy

    sent = []

    barrier = pltpu.get_barrier_semaphore()
    partners = [(dx, 0) for dx in range(1, NPX)]
    partners += [(dx, dy) for dx in range(-REACH, REACH + 1) for dy in (-1, 1)]
    for dx, dy in partners:
        pl.semaphore_signal(barrier, inc=1, device_id=at(dx, dy), device_id_type=MESH)

    middle = pl.ds(PAD + 16, 16)
    moves = [(velocity_in.at[pl.ds(c * ROWS, ROWS), :], r.TQ.at[pl.ds(c * EXT, ROWS), :]) for c in range(3)]
    moves += [
        (fraction_in, r.TQ.at[pl.ds(3 * EXT, ROWS), :]),
        (slot_in, r.slot),
        (start_in, r.V[0].at[pl.ds(1, NZ), middle, :]),
        (source_in, r.B[0].at[:, pl.ds(16, 16), :]),
        (depth_in, r.E[0].at[pl.ds(16, 16), :]),
        (receive_in, r.receive),
        (neighbour_in, r.neighbour),
        (normal_in, r.normal),
        (step_in, r.step),
        (pressure_in, r.TS.at[pl.ds(3 * EXT, ROWS), :]),
        (weight_in, r.weight),
        (corner_in, r.corner),
        (stencil_in, r.stencil),
        (height_in, r.height),
        (blend_in, r.blend),
    ]
    loads = [pltpu.make_async_copy(a, b, r.load.at[i]) for i, (a, b) in enumerate(moves)]
    for load in loads:
        load.start()

    def loaded(first, last):
        for load in loads[first:last]:
            load.wait()

    for rows, refs_of in [(48, r.V + r.U)] + [(level.R, [level.V, level.U]) for level in levels[1:]]:
        for ref in refs_of:
            ref[0] = jnp.zeros((rows + 2 * PAD, 128), F32)
            ref[NZ + 1] = jnp.zeros((rows + 2 * PAD, 128), F32)
            ref[1 : NZ + 1, 0:PAD, :] = jnp.zeros((NZ, PAD, 128), F32)
            ref[1 : NZ + 1, PAD + rows : 2 * PAD + rows, :] = jnp.zeros((NZ, PAD, 128), F32)
    for cycle in range(2):
        r.G[cycle][0] = jnp.zeros((3, 3, 2, 128), F32)

    loaded(0, 5)
    r.SI[...] = jnp.zeros((8, 128), I32)
    for b in range(4):
        r.SI[b : b + 1, :] = r.slot[b, 0, :, 0:128]
        r.SI[4 + b : 5 + b, 0:64] = r.slot[b, 0, :, 128:192]
    send_hi, send_lo = r.SI[...] >> 7, r.SI[...] & 127

    def reader(table):
        return lambda c, j: table[c * EXT + j : c * EXT + j + 1, :]

    def cfd_send(i, table):
        values = table_gather(reader(table), ROWS, CHANNELS[i], send_hi, send_lo)
        for c in range(CHANNELS[i]):
            r.CS[i][c] = values[c]

    def cfd_start(i):
        copies = []
        for slot, (dx, dy) in enumerate(((1, 0), (-1, 0), (0, 1), (0, -1))):
            copies.append(send(r.CS[i], r.CR[i].at[slot], r.s_cfd[i], slot, at(dx, dy)))
        return copies

    there = (x > 0, x < NPX - 1, y > 0, y < NPY - 1)
    block = (1, 0, 3, 2)

    def cfd_wait(i, table, copies):
        for copy in copies:
            copy.wait_recv()
        sent.extend(copies)
        for c in range(CHANNELS[i]):
            for b in range(4):
                for h in range(2):
                    row = r.CR[i][b, c, block[b] + 4 * h : block[b] + 4 * h + 1, :]
                    place = c * EXT + ROWS + 2 * b + h
                    table[place : place + 1, :] = jnp.where(there[b], row, 0.0)

    cfd_send(0, r.TQ)

    loaded(5, 8)
    lane16 = lane_iota(16)
    groups_f = [jnp.zeros((16, 128), F32) for _ in range(5)]
    groups_l = [jnp.zeros((16, 128), F32) for _ in range(5)]
    for t in range(2 * NZ + 1):
        if t < NZ:
            tile = r.V[0][t + 1, PAD + 16 : PAD + 32, :]
        elif t < 2 * NZ:
            tile = r.B[0][t - NZ, 16:32, :]
        else:
            tile = r.E[0][16:32, :]
        g, q = t // 8, t % 8
        own = (lane16 >= 16 * q) & (lane16 < 16 * q + 16)
        groups_f[g] = jnp.where(own, roll(tile, 16 * q, 1), groups_f[g])
        groups_l[g] = jnp.where(own, roll(tile, 16 * q + 16, 1), groups_l[g])
    for g in range(5):
        r.first[g] = groups_f[g]
        r.final[g] = groups_l[g]

    pl.semaphore_wait(barrier, len(partners))

    copies0 = cfd_start(0)
    strips = []
    for dx in (-1, 0, 1):
        slot = 2 * (1 - dx)
        strips.append(send(r.final, r.strips.at[slot], r.s_strip, slot, at(dx, 1)))
        strips.append(send(r.first, r.strips.at[slot + 1], r.s_strip, slot + 1, at(dx, -1)))
    tiles = []
    for s, (dx, row) in enumerate(((1, 0), (-1, 32))):
        padded = pl.ds(PAD + row, 16)
        rows = pl.ds(row, 16)
        tiles.append(send(start_in, r.V[0].at[pl.ds(1, NZ), padded, :], r.s_tile, 3 * s, at(dx, 0)))
        tiles.append(send(source_in, r.B[0].at[:, rows, :], r.s_tile, 3 * s + 1, at(dx, 0)))
        tiles.append(send(depth_in, r.E[0].at[rows, :], r.s_tile, 3 * s + 2, at(dx, 0)))

    loaded(8, 10)
    cells = r.receive[...]
    hi_of, lo_of = cells >> 7, cells & 127
    inverse = jnp.zeros((2 * ROWS, 128), F32)
    for chunk in range(4):
        lefts, rights = [], []
        for o in range(8 * chunk, 8 * chunk + 8):
            match = row_iota(ROWS) == jnp.broadcast_to(hi_of[o : o + 1, :], (ROWS, 128))
            lanes = lane_iota(ROWS).astype(F32)
            lefts.append(
                jnp.concatenate([jnp.where(match, F32(o + 1), 0.0), jnp.where(match, lanes, 0.0)], axis=0)
            )
            low = row_iota(128) == jnp.broadcast_to(lo_of[o : o + 1, :], (128, 128))
            rights.append(jnp.where(low, F32(1.0), 0.0))
        left = jnp.concatenate(lefts, axis=1).astype(jnp.bfloat16)
        right = jnp.concatenate(rights, axis=1).astype(jnp.bfloat16)
        inverse = inverse + lax.dot_general(
            left, right, (((1,), (1,)), ((), ())), preferred_element_type=F32
        )
    r.INV[...] = inverse.astype(I32)

    index = r.neighbour[...]
    for edge in (4288, 4480, 4672, 4864):
        index = index + jnp.where(r.neighbour[...] >= edge, 64, 0)
    r.HI[...] = index >> 7
    r.LO[...] = index & 127

    cfd_wait(0, r.TQ, copies0)
    loaded(10, 13)

    def part(f, quarter):
        return pl.ds(pl.multiple_of(f * ROWS + 8 * quarter, 8), 8)

    def cells_of(base, quarter):
        return pl.ds(pl.multiple_of(base + 8 * quarter, 8), 8)

    def beside_of(table, components, f, quarter):
        rows = part(f, quarter)
        return table_gather(reader(table), EXT, components, r.HI[rows, :], r.LO[rows, :])

    def normal_of(c, f, quarter):
        return r.normal[part(c * FACES + f, quarter), :]

    zero = jnp.zeros((8, 128), F32)

    @pl.loop(0, 4)
    def _(quarter):
        mine = [r.TQ[cells_of(c * EXT, quarter), :] for c in range(4)]

        def face(f, totals):
            beside = beside_of(r.TQ, 4, f, quarter)
            flux = normal_of(0, f, quarter) * (mine[0] + beside[0])
            for c in (1, 2):
                flux = flux + normal_of(c, f, quarter) * (mine[c] + beside[c])
            flux = 0.5 * flux
            out, into = jnp.maximum(flux, 0.0), jnp.minimum(flux, 0.0)
            return tuple(totals[c] + (out * mine[c] + into * beside[c]) for c in range(4))

        totals = lax.fori_loop(0, FACES, face, (zero,) * 4)
        scale = r.step[cells_of(0, quarter), :]
        for c in range(3):
            r.TS[cells_of(c * EXT, quarter), :] = mine[c] - scale * totals[c]
        r.FRAC[cells_of(0, quarter), :] = mine[3] - scale * totals[3]

    cfd_send(1, r.TS)
    copies1 = cfd_start(1)

    for copy in tiles + strips:
        copy.wait_recv()
    sent.extend(tiles + strips)
    for block_row in range(3):
        rows = slice(16 * block_row, 16 * block_row + 16)
        padded = slice(PAD + 16 * block_row, PAD + 16 * block_row + 16)
        for t in range(2 * NZ + 1):
            g, q = t // 8, t % 8
            lower = r.strips[2 * block_row, g]
            upper = r.strips[2 * block_row + 1, g]
            value = jnp.where(
                lane16 < 16,
                roll(upper, -16 * q, 1),
                jnp.where(lane16 >= 112, roll(lower, 112 - 16 * q, 1), 0.0),
            )
            if t < NZ:
                r.V[1][t + 1, padded, :] = value
            elif t < 2 * NZ:
                r.B[1][t - NZ, rows, :] = value
            else:
                r.E[1][rows, :] = value

    fine_rows = row_iota(48) + 16 * (x - 1)
    inside_a = (fine_rows >= 0) & (fine_rows < 16 * NPX)
    side_ok = jnp.where(lane_iota(48) < 64, jnp.where(y < NPY - 1, 1, 0), jnp.where(y > 0, 1, 0)) > 0
    insides = [inside_a, inside_a & side_ok]
    data = slice(PAD, PAD + 48)

    def mask_start(k):
        for s in range(2):
            r.V[s][k + 1, data, :] = jnp.where(insides[s], r.V[s][k + 1, data, :], 0.0)

    each_layer(mask_start)

    depths = [jnp.where(insides[s], r.E[s][...], 0.0) for s in range(2)]
    lane48 = lane_iota(48)
    for s in range(2):
        depth, other = depths[s], depths[1 - s]
        r.E[s][...] = depth
        right = jnp.where(lane48 == 127, roll(other, 127, 1), roll(depth, 127, 1))
        left = jnp.where(lane48 == 0, roll(other, 1, 1), roll(depth, 1, 1))
        faces = (
            0.5 * (depth + roll(depth, 47, 0)),
            0.5 * (depth + roll(depth, 1, 0)),
            0.5 * (depth + right),
            0.5 * (depth + left),
        )
        total = faces[0] + faces[1] + faces[2] + faces[3]
        for i, face in enumerate(faces):
            r.C[s][i] = face
        for i, extra in enumerate((VERT, 2 * VERT)):
            r.D[s][i] = total + extra
            r.W[s][i] = jnp.where(insides[s], RELAX / (total + extra), 0.0)

    def fine_sweep(source, target, lo=0, hi=48):
        fine_operate(r, source, target, False, lo, hi)

    lane24 = lane_iota(24)
    down24 = (2 * lane24) & 127

    def fine_pair(a_even, a_odd, b_even, b_odd):
        mean_a = lane_gather(pair_mean_rows(a_even, a_odd), down24)
        mean_b = lane_gather(pair_mean_rows(b_even, b_odd), down24)
        return jnp.where(lane24 < 64, mean_a, mean_b)

    even24, odd24 = pl.ds(0, 24, stride=2), pl.ds(1, 24, stride=2)
    even_pad, odd_pad = pl.ds(PAD, 24, stride=2), pl.ds(PAD + 1, 24, stride=2)
    inside_1 = inside_of(x, y, 24, 8 * (x - 1), 96, 64, 8 * NPX, 64 * NPY)
    r.M1[...] = jnp.where(inside_1, F32(1.0), 0.0)
    depth_1 = fine_pair(r.E[0][even24, :], r.E[0][odd24, :], r.E[1][even24, :], r.E[1][odd24, :])
    depth_1 = jnp.where(inside_1, depth_1, 0.0)
    levels[1].E[...] = depth_1
    set_coefficients(levels[1], depth_1, inside_1, 0.25)

    def fine_coarsen(k):
        levels[1].B[k] = fine_pair(
            r.U[0][k + 1, even_pad, :], r.U[0][k + 1, odd_pad, :],
            r.U[1][k + 1, even_pad, :], r.U[1][k + 1, odd_pad, :],
        )

    lane8 = lane_iota(8)

    lane4 = lane_iota(4)

    def pack_second(cycle):
        count = NZ + 1 if cycle == 0 else NZ
        even, odd = pl.ds(8, 4, stride=2), pl.ds(9, 4, stride=2)
        for g in range(5):
            packed = jnp.zeros((4, 128), F32)
            for q in range(4):
                k = 4 * g + q
                if k >= count:
                    continue
                if k < NZ:
                    mean = pair_mean_rows(levels[1].T[k, even, :], levels[1].T[k, odd, :])
                else:
                    mean = pair_mean_rows(levels[1].E[even, :], levels[1].E[odd, :])
                own = (lane4 >= 32 * q) & (lane4 < 32 * q + 32)
                packed = jnp.where(own, lane_gather(mean, (2 * lane4 + 64 * (q % 2)) & 127), packed)
            r.P[cycle][g] = packed
            r.N[cycle][1, 1, g] = packed

    def start_second(cycle):
        copies = []
        for dx in (-1, 0, 1):
            for dy in (-1, 0, 1):
                if dx or dy:
                    d, j = 1 - dx, 1 - dy
                    copies.append(send(r.P[cycle], r.N[cycle].at[d, j], r.s_second[cycle], 3 * d + j, at(dx, dy)))
        return copies

    def unpack_second(cycle):
        got = r.N[cycle]
        for m, pair in enumerate(((0, 1), (2, 2))):
            rows = slice(8 * m, 8 * m + 8)
            for g in range(5):
                tiles_of = [jnp.concatenate([got[d, j, g] for d in pair], axis=0) for j in range(3)]
                for q in range(4):
                    k = 4 * g + q
                    if k > NZ or (k == NZ and cycle > 0):
                        continue
                    value = jnp.where(
                        lane8 < 32,
                        roll(tiles_of[1], -32 * q, 1),
                        jnp.where(
                            lane8 < 64,
                            roll(tiles_of[2], 32 - 32 * q, 1),
                            roll(tiles_of[0], 96 - 32 * q, 1),
                        ),
                    )
                    if k < NZ:
                        levels[2].B[k, rows, :] = value
                    else:
                        levels[2].E[rows, :] = value

    lane2 = lane_iota(2)

    def pack_deep(cycle):
        count = NZ + 1 if cycle == 0 else NZ
        even, odd = pl.ds(4, 2, stride=2), pl.ds(5, 2, stride=2)
        for g in range(3):
            packed = jnp.zeros((2, 128), F32)
            for q in range(8):
                k = 8 * g + q
                if k >= count:
                    continue
                if k < NZ:
                    mean = pair_mean_rows(levels[2].T[k, even, :], levels[2].T[k, odd, :])
                else:
                    mean = pair_mean_rows(levels[2].E[even, :], levels[2].E[odd, :])
                own = (lane2 >= 16 * q) & (lane2 < 16 * q + 16)
                packed = jnp.where(own, lane_gather(mean, (2 * lane2 + 96 * q) & 127), packed)
            r.P3[cycle][g] = packed
            r.G[cycle][8, 1, g] = packed

    def start_deep(cycle):
        copies = []
        for dx in range(-REACH, REACH + 1):
            for dy in (-1, 0, 1):
                if dx == 0 and dy == 0:
                    continue
                d, j = 8 - dx, 1 - dy
                copies.append(send(r.P3[cycle], r.G[cycle].at[d, j], r.s_deep[cycle], 3 * d + j, at(dx, dy)))
        return copies

    def unpack_deep(cycle):
        grid_of = r.G[cycle]

        @pl.loop(0, 4)
        def _(m):
            rows = pl.ds(pl.multiple_of(8 * m, 8), 8)
            for g in range(3):
                tiles_of = [
                    jnp.concatenate([grid_of[4 * m + i, j, g] for i in range(4)], axis=0) for j in range(3)
                ]
                for q in range(8):
                    k = 8 * g + q
                    if k > NZ or (k == NZ and cycle > 0):
                        continue
                    value = jnp.where(
                        lane8 < 16,
                        roll(tiles_of[1], -16 * q, 1),
                        jnp.where(
                            lane8 < 64,
                            roll(tiles_of[2], 16 - 16 * q, 1),
                            roll(tiles_of[0], 112 - 16 * q, 1),
                        ),
                    )
                    if k < NZ:
                        levels[3].B[k, rows, :] = value
                    else:
                        levels[3].E[rows, :] = value

    def deep_coefficients(level):
        here = levels[level]
        rows = here.R
        first, tile, width = {2: (-1, 4, 32), 3: (-8, 2, 16), 4: (-8, 1, 8)}[level]
        inside = inside_of(x, y, rows, tile * (x + first), 64, width, tile * NPX, width * NPY)
        if level > 3:
            above = levels[level - 1].E
            mean = pair_mean_rows(above[pl.ds(0, rows, stride=2), :], above[pl.ds(1, rows, stride=2), :])
            depth = lane_gather(mean, (2 * lane_iota(rows)) & 127)
        else:
            depth = here.E[...]
        depth = jnp.where(inside, depth, 0.0)
        here.E[...] = depth
        set_coefficients(here, depth, inside, 0.25**level)

    def descend(here):
        point_step(here)
        sweep_step(here, here.V, here.U)
        operate(here, here.U, here.T, True)

    def solve_deep():
        descend(levels[3])
        coarsen_step(levels[3], levels[4])
        last = levels[4]
        point_step(last)
        sweep_step(last, last.V, last.U)
        sweep_step(last, last.U, last.V)
        sweep_step(last, last.V, last.U)
        for level, first, split in ((3, 0, 64), (2, 14, 64), (1, 0, 96)):
            here = levels[level]
            refine_add(levels[level + 1].U, first, here, here.U, split)
            sweep_step(here, here.U, here.V)
            sweep_step(here, here.V, here.U)

    def down(lo, hi):
        fine_operate(r, r.V, r.U, True, lo, hi)
        each_layer(fine_coarsen)
        descend(levels[1])

    def start_near(cycle):
        own = slice(PAD + 8, PAD + 16)
        values = [levels[1].U[k + 1, own, :] for k in range(NZ)]
        for pair in range(9):
            value = values[2 * pair]
            if 2 * pair + 1 < NZ:
                value = jnp.where(lane8 < 64, value, roll(values[2 * pair + 1], 64, 1))
            r.mine[cycle][pair] = value
        for g in range(2):
            left, right = jnp.zeros((8, 128), F32), jnp.zeros((8, 128), F32)
            for q in range(16):
                if 16 * g + q < NZ:
                    columns = (lane8 >= 8 * q) & (lane8 < 8 * q + 8)
                    left = jnp.where(columns, roll(values[16 * g + q], 8 * q, 1), left)
                    right = jnp.where(columns, roll(values[16 * g + q], 8 * q - 56, 1), right)
            r.left[cycle][g] = left
            r.right[cycle][g] = right
        copies = []
        for s, dx in enumerate((1, -1)):
            copies.append(send(r.mine[cycle], r.near[cycle].at[s], r.s_near[cycle], s, at(dx, 0)))
        for dx in (-1, 0, 1):
            slot = 2 * (1 - dx)
            copies.append(send(r.right[cycle], r.sides[cycle].at[slot], r.s_near[cycle], 2 + slot, at(dx, 1)))
            copies.append(send(r.left[cycle], r.sides[cycle].at[slot + 1], r.s_near[cycle], 3 + slot, at(dx, -1)))
        return copies

    def add_near(cycle):
        half_lane = lane24 >> 1
        for k in range(NZ):
            pair, odd, g, q = k // 2, k % 2, k // 16, k % 16
            for block_row in range(3):
                middle = r.mine[cycle][pair] if block_row == 1 else r.near[cycle][block_row // 2, pair]
                lower, upper = r.sides[cycle][2 * block_row, g], r.sides[cycle][2 * block_row + 1, g]
                aside = jnp.where(lane8 < 96, roll(upper, 64 - 8 * q, 1), roll(lower, 120 - 8 * q, 1))
                value = jnp.where(lane8 < 64, roll(middle, 64 * odd, 1), aside)
                levels[1].T[k, 8 * block_row : 8 * block_row + 8, :] = value

        def body(k):
            value = levels[1].T[k] * r.M1[...]
            for s, lanes in ((0, half_lane), (1, half_lane + 64)):
                spread = lane_gather(value, lanes)
                r.U[s][k + 1, even_pad, :] = spread
                r.U[s][k + 1, odd_pad, :] = spread
                r.V[s][k + 1, data, :] = r.V[s][k + 1, data, :] + r.U[s][k + 1, data, :]

        each_layer(body)

    fine_sweep(r.V, r.U)
    fine_sweep(r.U, r.V)
    down(0, 48)
    pack_second(0)
    second0 = start_second(0)

    cfd_wait(1, r.TS, copies1)
    loaded(13, 14)

    def divergence(quarter):
        mine = [r.TS[cells_of(c * EXT, quarter), :] for c in range(3)]

        def face(f, carry):
            flow, pull, weights = carry
            beside = beside_of(r.TS, 4, f, quarter)
            for c in range(3):
                flow = flow + normal_of(c, f, quarter) * (mine[c] + beside[c])
            weight = r.weight[part(f, quarter), :]
            return flow, pull + weight * beside[3], weights + weight

        flow, pull, weights = lax.fori_loop(0, FACES, face, (zero,) * 3)
        here = cells_of(0, quarter)
        flow, inverse_sum = 0.5 * flow, 1.0 / weights
        r.DIV[here, :] = flow
        r.IWS[here, :] = inverse_sum
        r.TP[0][here, :] = (pull - flow) * inverse_sum

    def descend_second(cycle, copies):
        for copy in copies:
            copy.wait_recv()
        sent.extend(copies)
        unpack_second(cycle)
        if cycle == 0:
            deep_coefficients(2)
        descend(levels[2])
        pack_deep(cycle)
        return start_deep(cycle)

    pl.loop(0, 2)(divergence)
    deep0 = descend_second(0, second0)
    pl.loop(2, 4)(divergence)
    cfd_send(2, r.TP[0])
    copies2 = cfd_start(2)

    for copy in deep0:
        copy.wait_recv()
    sent.extend(deep0)
    unpack_deep(0)
    deep_coefficients(3)
    deep_coefficients(4)
    solve_deep()
    near0 = start_near(0)

    def pressure_sweep(before, after):
        @pl.loop(0, 4)
        def _(quarter):
            pull = zero
            for f in range(FACES):
                pull = pull + r.weight[part(f, quarter), :] * beside_of(before, 1, f, quarter)[0]
            here = cells_of(0, quarter)
            after[here, :] = (pull - r.DIV[here, :]) * r.IWS[here, :]

    cfd_wait(2, r.TP[0], copies2)
    pressure_sweep(r.TP[0], r.TP[1])
    cfd_send(3, r.TP[1])
    copies3 = cfd_start(3)

    for copy in near0:
        copy.wait_recv()
    sent.extend(near0)
    add_near(0)
    fine_sweep(r.V, r.U)
    fine_sweep(r.U, r.V)
    fine_sweep(r.V, r.U)
    fine_sweep(r.U, r.V)
    down(8, 40)
    pack_second(1)
    second1 = start_second(1)

    cfd_wait(3, r.TP[1], copies3)
    pressure_sweep(r.TP[1], r.TP[2])
    cfd_send(4, r.TP[2])
    copies4 = cfd_start(4)
    pressure_copy = pltpu.make_async_copy(r.TP[2].at[pl.ds(0, ROWS), :], pressure_out, r.load.at[18])
    pressure_copy.start()
    deep1 = descend_second(1, second1)

    for copy in deep1:
        copy.wait_recv()
    sent.extend(deep1)
    unpack_deep(1)
    solve_deep()
    near1 = start_near(1)

    cfd_wait(4, r.TP[2], copies4)

    @pl.loop(0, 4)
    def _(quarter):
        here = cells_of(0, quarter)
        pressure = r.TP[2][here, :]
        totals = [zero] * 3
        for f in range(FACES):
            difference = beside_of(r.TP[2], 1, f, quarter)[0] - pressure
            totals = [totals[c] + normal_of(c, f, quarter) * difference for c in range(3)]
        for c in range(3):
            r.COR[cells_of(c * ROWS, quarter), :] = r.TS[cells_of(c * EXT, quarter), :] - r.step[here, :] * (
                0.5 * totals[c]
            )

    for copy in near1:
        copy.wait_recv()
    sent.extend(near1)
    add_near(1)
    fine_sweep(r.V, r.U, 8, 40)
    fine_sweep(r.U, r.V, 8, 40)

    loaded(14, 18)

    own_rows = pl.ds(pl.multiple_of(x * 8, 8), 8)

    def interpolate(quarter):
        corner = r.corner[cells_of(0, quarter), :]
        column = corner & 127
        point_row = (corner >> 7) & 15
        point_layer = corner >> 11

        def layer(k, picks):
            found = []
            for lanes in (column, column + 1):
                low, high = zero, zero
                before = None
                for i in range(16):
                    row = jnp.broadcast_to(r.V[0][k + 1, PAD + 16 + i : PAD + 17 + i, :], (8, 128))
                    value = lane_gather(row, lanes)
                    here = point_row == i
                    if i < 15:
                        low = jnp.where(here, value, low)
                    if before is not None:
                        high = jnp.where(before, value, high)
                    before = here
                found.append((low, high))
            found = (found[0][0], found[1][0], found[0][1], found[1][1])
            lower, upper = point_layer == k, point_layer == k - 1
            return tuple(jnp.where(lower, found[i], picks[i]) for i in range(4)) + tuple(
                jnp.where(upper, found[i], picks[4 + i]) for i in range(4)
            )

        def layers(step, picks):
            for i in range(4):
                picks = layer(4 * step + i, picks)
            return picks

        picks = layer(NZ - 1, lax.fori_loop(0, NZ // 4, layers, (zero,) * 8))
        for quantity in range(4):
            total = zero
            for p in range(8):
                total = total + r.stencil[cells_of((quantity * 8 + p) * ROWS, quarter), :] * picks[p]
            for i in range(8):
                r.S[pl.ds(64 * quarter + 8 * i + quantity, 1), :] = total[i : i + 1, :]

    potential_copy = pltpu.make_async_copy(r.V[0].at[pl.ds(1, NZ), middle, :], potential_out, r.load.at[19])
    potential_copy.start()

    everyone = []
    for away in (2, 1, 3, 0):
        quarter = lax.rem(x // 8 + away, 4)
        interpolate(quarter)
        for i in range(0 if away else 1, 8):
            there_x = quarter * 8 + (i if away else lax.rem(x + i, 8))
            rows = pl.ds(pl.multiple_of(there_x * 8, 8), 8)
            slot = lax.rem(there_x - x + NPX, NPX)
            everyone.append(send(r.S.at[rows, :], r.RB.at[own_rows, :], r.s_all, slot, (there_x, y)))
    r.RB[own_rows, :] = r.S[own_rows, :]
    for o in range(1, NPX):
        pltpu.make_async_remote_copy(
            src_ref=r.S.at[0:8, :],
            dst_ref=r.RB.at[0:8, :],
            send_sem=r.s_all[0].at[o],
            recv_sem=r.s_all[1].at[o],
            device_id=at(o, 0),
            device_id_type=MESH,
        ).wait_recv()
    sent.extend(everyone)

    @pl.loop(0, 4)
    def _(quarter):
        here = cells_of(0, quarter)
        slot_hi, slot_lo = r.INV[here, :] - 1, r.INV[cells_of(ROWS, quarter), :]
        targets = table_gather(lambda c, j: r.RB[8 * j + c : 8 * j + c + 1, :], NPX, 4, slot_hi, slot_lo)
        strength = jnp.where(slot_hi >= 0, r.blend[here, :], 0.0)
        for c in range(3):
            velocity = r.COR[cells_of(c * ROWS, quarter), :]
            velocity_out[cells_of(c * ROWS, quarter), :] = velocity - strength * (velocity - targets[c])
        level_target = jax.nn.sigmoid(4.0 * (targets[3] - r.height[here, :]))
        fraction = r.FRAC[here, :]
        fraction_out[here, :] = fraction - strength * (fraction - level_target)

    pressure_copy.wait()
    potential_copy.wait()
    for copy in sent:
        copy.wait_send()


def hand_over(*refs):
    given, results, held, arrive, leave = refs[0:4], refs[4:8], refs[8:12], refs[12], refs[13]
    ins = [pltpu.make_async_copy(given[i], held[i], arrive.at[i]) for i in range(4)]
    outs = [pltpu.make_async_copy(held[i], results[i], leave.at[i]) for i in range(4)]
    for copy in ins:
        copy.start()
    for i in range(4):
        ins[i].wait()
        outs[i].start()
    for copy in outs:
        copy.wait()


def on_device(
    source, water_depth, potential_start, velocity, fraction, pressure, neighbour, send_slot,
    face_normal, face_weight, step_scale, height, blend_weight, corner, stencil_weight, receive_cell,
):
    def lanes(array):
        return array.reshape(-1, 128)

    args = (
        source, water_depth, potential_start, lanes(velocity), lanes(fraction), lanes(pressure), lanes(neighbour),
        send_slot, lanes(face_normal), lanes(face_weight), lanes(step_scale), lanes(height),
        lanes(blend_weight), lanes(corner), lanes(stencil_weight), lanes(receive_cell),
    )
    shapes = ((NZ, 16, 128), (3 * ROWS, 128), (ROWS, 128), (ROWS, 128))
    results = pl.pallas_call(
        kernel,
        name="step",
        out_shape=[jax.ShapeDtypeStruct(shape, F32) for shape in shapes],
        in_specs=[pl.BlockSpec(memory_space=pltpu.HBM)] * len(args),
        out_specs=[pl.BlockSpec(memory_space=space) for space in (pltpu.HBM, pltpu.VMEM, pltpu.VMEM, pltpu.HBM)],
        scratch_shapes=jax.tree_util.tree_leaves(scratch_plan()),
        compiler_params=pltpu.CompilerParams(
            collective_id=0, has_side_effects=True, vmem_limit_bytes=67043328
        ),
    )(*args)
    dma = pltpu.SemaphoreType.DMA
    results = pl.pallas_call(
        hand_over,
        name="hand_over",
        out_shape=[jax.ShapeDtypeStruct(shape, F32) for shape in shapes],
        in_specs=[pl.BlockSpec(memory_space=pltpu.HBM)] * len(shapes),
        out_specs=[pl.BlockSpec(memory_space=pltpu.HBM)] * len(shapes),
        scratch_shapes=[pltpu.VMEM(shape, F32) for shape in shapes] + [dma((4,)), dma((4,))],
        compiler_params=pltpu.CompilerParams(vmem_limit_bytes=67043328),
    )(*results)
    potential, velocity_out, fraction_out, pressure_out = results
    return (
        potential,
        velocity_out.reshape(3, 1, 1, -1),
        fraction_out.reshape(1, 1, -1),
        pressure_out.reshape(1, 1, -1),
    )


def solution(mesh):
    in_specs = (
        P(None, "px", "py"),
        P("px", "py"),
        P(None, "px", "py"),
        P(None, "px", "py", None),
        P("px", "py", None),
        P("px", "py", None),
        P(None, "px", "py", None),
        P(None, "px", "py", None),
        P(None, None, "px", "py", None),
        P(None, "px", "py", None),
        P("px", "py", None),
        P("px", "py", None),
        P("px", "py", None),
        P("px", "py", None),
        P(None, None, "px", "py", None),
        P("px", "py", None),
    )
    out_specs = (
        P(None, "px", "py"),
        P(None, "px", "py", None),
        P("px", "py", None),
        P("px", "py", None),
    )
    return jax.shard_map(on_device, mesh=mesh, in_specs=in_specs, out_specs=out_specs, check_vma=False)
```

```python
from types import SimpleNamespace

import jax
import jax.numpy as jnp
from jax import lax
from jax.experimental import pallas as pl
from jax.experimental.pallas import tpu as pltpu
from jax.sharding import PartitionSpec as P

F32 = jnp.float32
I32 = jnp.int32
MESH = pl.DeviceIdType.MESH
NPX, NPY = 32, 8
NZ = 17
FACES = 6
ROWS = 32
EXT = 40
PAD = 8
VERT = 0.01
RELAX = 0.8
REACH = 6

GATHER_DIMS = lax.GatherDimensionNumbers(
    offset_dims=(),
    collapsed_slice_dims=(1,),
    start_index_map=(1,),
    operand_batching_dims=(0,),
    start_indices_batching_dims=(0,),
)


def lane_gather(values, lanes):
    return lax.gather(
        values,
        lanes[..., None],
        GATHER_DIMS,
        slice_sizes=(1, 1),
        mode=lax.GatherScatterMode.PROMISE_IN_BOUNDS,
    )


def lane_iota(rows):
    return lax.broadcasted_iota(I32, (rows, 128), 1)


def row_iota(rows):
    return lax.broadcasted_iota(I32, (rows, 128), 0)


def roll(values, shift, axis):
    shift = shift % values.shape[axis]
    return values if shift == 0 else pltpu.roll(values, shift, axis)


def over_layers(body, chunk=4):
    whole = NZ // chunk
    if whole > 1:

        @pl.loop(0, whole)
        def _(step):
            body([step * chunk + j for j in range(chunk)])

    rest = list(range(whole * chunk if whole > 1 else 0, NZ))
    if rest:
        body(rest)


def each_layer(body, chunk=4):
    def bodies(layers):
        for k in layers:
            body(k)

    over_layers(bodies, chunk)


def kind(k):
    return min(k, 1) if isinstance(k, int) else jnp.minimum(k, 1)


def inside_of(x, y, rows, row_first, lane_split, width, height, depth):
    row = row_iota(rows) + row_first
    lane = lane_iota(rows)
    column = jnp.where(lane < lane_split, lane, lane - 128) + y * width
    return (row >= 0) & (row < height) & (column >= 0) & (column < depth)


def set_coefficients(level, depth, inside, scale):
    rows = depth.shape[0]
    half = 0.5 * scale
    faces = (
        half * (depth + roll(depth, rows - 1, 0)),
        half * (depth + roll(depth, 1, 0)),
        half * (depth + roll(depth, 127, 1)),
        half * (depth + roll(depth, 1, 1)),
    )
    total = faces[0] + faces[1] + faces[2] + faces[3]
    for i, face in enumerate(faces):
        level.C[i] = face
    for i, extra in enumerate((VERT, 2 * VERT)):
        diagonal = total + extra
        level.D[i] = diagonal
        level.W[i] = jnp.where(inside, RELAX / diagonal, 0.0)


def point_step(level):
    def body(k):
        level.V[k + 1, PAD : PAD + level.R, :] = level.W[kind(k)] * level.B[k]

    each_layer(body)


def operate(level, source, target, residual, lo, hi):
    def body(layers):
        for start in range(lo, hi, 8):
            rows, mid = slice(start, start + 8), slice(PAD + start, PAD + start + 8)
            up, down = slice(PAD + start + 1, PAD + start + 9), slice(PAD + start - 1, PAD + start + 7)
            faces = [level.C[i, rows, :] for i in range(4)]
            below, values = source[layers[0], mid, :], source[layers[0] + 1, mid, :]
            for k in layers:
                above = source[k + 2, mid, :]
                total = faces[0] * source[k + 1, up, :] + faces[1] * source[k + 1, down, :]
                total = total + (faces[2] * roll(values, 127, 1) + faces[3] * roll(values, 1, 1))
                total = (total + VERT * (below + above)) + level.B[k, rows, :]
                if residual:
                    target[k, rows, :] = total - level.D[kind(k), rows, :] * values
                else:
                    target[k + 1, mid, :] = (1.0 - RELAX) * values + level.W[kind(k), rows, :] * total
                below, values = values, above

    over_layers(body, NZ)


def sweep_step(level, source, target, lo=0, hi=None):
    operate(level, source, target, False, lo, level.R if hi is None else hi)


def pair_mean_rows(even, odd):
    total = even + odd
    return 0.25 * (total + roll(total, 127, 1))


def coarsen_step(fine, coarse):
    half = coarse.R
    lanes = (2 * lane_iota(half)) & 127

    def body(k):
        total = pair_mean_rows(fine.T[k, pl.ds(0, half, stride=2), :], fine.T[k, pl.ds(1, half, stride=2), :])
        coarse.B[k] = lane_gather(total, lanes)

    each_layer(body)


def refine_add(correction, first, fine, target, lane_split):
    rows = fine.R
    half = rows // 2
    lane = lane_iota(half)
    lanes = jnp.where(lane < lane_split, lane >> 1, (lane >> 1) + 64)

    def body(k):
        spread = lane_gather(correction[k + 1, PAD + first : PAD + first + half, :], lanes)
        fine.T[k, pl.ds(0, half, stride=2), :] = spread
        fine.T[k, pl.ds(1, half, stride=2), :] = spread
        target[k + 1, PAD : PAD + rows, :] = target[k + 1, PAD : PAD + rows, :] + fine.T[k]

    each_layer(body)


def fine_operate(top, source, target, residual, lo, hi, halves=(0, 1)):
    lane = lane_iota(8)
    first, last = lane == 0, lane == 127

    def body(layers):
        for start in range(lo, hi, 8):
            rows, mid = slice(start, start + 8), slice(PAD + start, PAD + start + 8)
            up, down = slice(PAD + start + 1, PAD + start + 9), slice(PAD + start - 1, PAD + start + 7)
            faces = [[top.C[s][i, rows, :] for i in range(4)] for s in range(2)]
            below = [source[s][layers[0], mid, :] for s in range(2)]
            values = [source[s][layers[0] + 1, mid, :] for s in range(2)]
            for k in layers:
                above = [source[s][k + 2, mid, :] for s in range(2)]
                rights = [roll(values[s], 127, 1) for s in range(2)]
                lefts = [roll(values[s], 1, 1) for s in range(2)]
                for s in halves:
                    right = jnp.where(last, rights[1 - s], rights[s])
                    left = jnp.where(first, lefts[1 - s], lefts[s])
                    total = faces[s][0] * source[s][k + 1, up, :] + faces[s][1] * source[s][k + 1, down, :]
                    total = total + (faces[s][2] * right + faces[s][3] * left)
                    total = (total + VERT * (below[s] + above[s])) + top.B[s][k, rows, :]
                    if residual:
                        value = total - top.D[s][kind(k), rows, :] * values[s]
                    else:
                        value = (1.0 - RELAX) * values[s] + top.W[s][kind(k), rows, :] * total
                    target[s][k + 1, mid, :] = value
                below, values = values, above

    over_layers(body, NZ)


def table_gather(read_row, count, components, hi, lo):
    picked = [jnp.zeros((8, 128), F32) for _ in range(components)]
    for j in range(count):
        mask = hi == j
        for c in range(components):
            row = jnp.broadcast_to(read_row(c, j), (8, 128))
            picked[c] = jnp.where(mask, lane_gather(row, lo), picked[c])
    return picked


CHANNELS = (4, 4, 1, 1, 1)


def scratch_plan():
    def vmem(*shape, dtype=F32):
        return pltpu.VMEM(shape, dtype)

    def pair(*shape):
        return [vmem(*shape), vmem(*shape)]

    def sems(count):
        return [pltpu.SemaphoreType.DMA((count,)), pltpu.SemaphoreType.DMA((count,))]

    def level(rows):
        return dict(
            V=vmem(NZ + 2, rows + 2 * PAD, 128),
            U=vmem(NZ + 2, rows + 2 * PAD, 128),
            B=vmem(NZ, rows, 128),
            T=vmem(NZ, rows, 128),
            C=vmem(4, rows, 128),
            W=vmem(2, rows, 128),
            D=vmem(2, rows, 128),
            E=vmem(rows, 128),
        )

    return dict(
        V=pair(NZ + 2, 48 + 2 * PAD, 128),
        U=pair(NZ + 2, 48 + 2 * PAD, 128),
        B=pair(NZ, 48, 128),
        C=pair(4, 48, 128),
        W=pair(2, 48, 128),
        D=pair(2, 48, 128),
        E=pair(48, 128),
        levels=[level(24), level(16), level(32), level(16)],
        M1=vmem(24, 128),
        first=vmem(5, 16, 128),
        final=vmem(5, 16, 128),
        strips=vmem(6, 5, 16, 128),
        P=pair(5, 4, 128),
        N=pair(3, 3, 5, 4, 128),
        P3=pair(3, 2, 128),
        G=pair(16, 3, 3, 2, 128),
        near=pair(2, 9, 8, 128),
        sides=pair(6, 2, 8, 128),
        mine=pair(9, 8, 128),
        left=pair(2, 8, 128),
        right=pair(2, 8, 128),
        HI=vmem(FACES * ROWS, 128, dtype=I32),
        LO=vmem(FACES * ROWS, 128, dtype=I32),
        SI=vmem(8, 128, dtype=I32),
        TQ=vmem(4 * EXT, 128),
        TS=vmem(4 * EXT, 128),
        TP=[vmem(EXT, 128) for _ in range(3)],
        CS=[vmem(n, 8, 128) for n in CHANNELS],
        CR=[vmem(4, n, 8, 128) for n in CHANNELS],
        FRAC=vmem(ROWS, 128),
        DIV=vmem(ROWS, 128),
        IWS=vmem(ROWS, 128),
        COR=vmem(3 * ROWS, 128),
        INV=vmem(2 * ROWS, 128, dtype=I32),
        S=vmem(256, 128),
        RB=vmem(256, 128),
        neighbour=vmem(FACES * ROWS, 128, dtype=I32),
        slot=vmem(4, 1, 1, 192, dtype=I32),
        normal=vmem(3 * FACES * ROWS, 128),
        weight=vmem(FACES * ROWS, 128),
        step=vmem(ROWS, 128),
        height=vmem(ROWS, 128),
        blend=vmem(ROWS, 128),
        corner=vmem(ROWS, 128, dtype=I32),
        stencil=vmem(32 * ROWS, 128),
        receive=vmem(ROWS, 128, dtype=I32),
        load=pltpu.SemaphoreType.DMA((20,)),
        s_tile=sems(6),
        s_strip=sems(6),
        s_deep=[sems(48), sems(48)],
        s_near=[sems(8), sems(8)],
        s_second=[sems(9), sems(9)],
        s_all=sems(32),
        s_cfd=[sems(4) for _ in range(5)],
    )


def kernel(*refs):
    (source_in, depth_in, start_in, velocity_in, fraction_in, pressure_in, neighbour_in, slot_in, normal_in,
     weight_in, step_in, height_in, blend_in, corner_in, stencil_in, receive_in,
     potential_out, velocity_out, fraction_out, pressure_out) = refs[:20]
    plan = scratch_plan()
    r = SimpleNamespace(**jax.tree_util.tree_unflatten(jax.tree_util.tree_structure(plan), refs[20:]))
    levels = [None] + [
        SimpleNamespace(R=rows, **fields) for rows, fields in zip((24, 16, 32, 16), r.levels)
    ]
    x, y = lax.axis_index("px"), lax.axis_index("py")

    def at(dx, dy):
        return (lax.rem(x + dx + NPX, NPX), lax.rem(y + dy + NPY, NPY))

    def send(source, target, semaphores, slot, where):
        copy = pltpu.make_async_remote_copy(
            src_ref=source,
            dst_ref=target,
            send_sem=semaphores[0].at[slot],
            recv_sem=semaphores[1].at[slot],
            device_id=where,
            device_id_type=MESH,
        )
        copy.start()
        return copy

    sent = []

    barrier = pltpu.get_barrier_semaphore()
    partners = [(dx, 0) for dx in range(1, NPX)]
    partners += [(dx, dy) for dx in range(-REACH, REACH + 1) for dy in (-1, 1)]
    for dx, dy in partners:
        pl.semaphore_signal(barrier, inc=1, device_id=at(dx, dy), device_id_type=MESH)

    middle = pl.ds(PAD + 16, 16)
    moves = [(velocity_in.at[pl.ds(c * ROWS, ROWS), :], r.TQ.at[pl.ds(c * EXT, ROWS), :]) for c in range(3)]
    moves += [
        (fraction_in, r.TQ.at[pl.ds(3 * EXT, ROWS), :]),
        (slot_in, r.slot),
        (start_in, r.V[0].at[pl.ds(1, NZ), middle, :]),
        (source_in, r.B[0].at[:, pl.ds(16, 16), :]),
        (depth_in, r.E[0].at[pl.ds(16, 16), :]),
        (receive_in, r.receive),
        (neighbour_in, r.neighbour),
        (normal_in, r.normal),
        (step_in, r.step),
        (pressure_in, r.TS.at[pl.ds(3 * EXT, ROWS), :]),
        (weight_in, r.weight),
        (corner_in, r.corner),
        (stencil_in, r.stencil),
        (height_in, r.height),
        (blend_in, r.blend),
    ]
    loads = [pltpu.make_async_copy(a, b, r.load.at[i]) for i, (a, b) in enumerate(moves)]
    for load in loads:
        load.start()

    def loaded(first, last):
        for load in loads[first:last]:
            load.wait()

    for rows, refs_of in [(48, r.V + r.U)] + [(level.R, [level.V, level.U]) for level in levels[1:]]:
        for ref in refs_of:
            ref[0] = jnp.zeros((rows + 2 * PAD, 128), F32)
            ref[NZ + 1] = jnp.zeros((rows + 2 * PAD, 128), F32)
            ref[1 : NZ + 1, 0:PAD, :] = jnp.zeros((NZ, PAD, 128), F32)
            ref[1 : NZ + 1, PAD + rows : 2 * PAD + rows, :] = jnp.zeros((NZ, PAD, 128), F32)
    for cycle in range(2):
        for d in (0, 1, 15):
            r.G[cycle][d] = jnp.zeros((3, 3, 2, 128), F32)

    loaded(0, 5)
    r.SI[...] = jnp.zeros((8, 128), I32)
    for b in range(4):
        r.SI[b : b + 1, :] = r.slot[b, 0, :, 0:128]
        r.SI[4 + b : 5 + b, 0:64] = r.slot[b, 0, :, 128:192]
    send_hi, send_lo = r.SI[...] >> 7, r.SI[...] & 127

    def reader(table):
        return lambda c, j: table[c * EXT + j : c * EXT + j + 1, :]

    def cfd_send(i, table):
        values = table_gather(reader(table), ROWS, CHANNELS[i], send_hi, send_lo)
        for c in range(CHANNELS[i]):
            r.CS[i][c] = values[c]

    def cfd_start(i):
        copies = []
        for slot, (dx, dy) in enumerate(((1, 0), (-1, 0), (0, 1), (0, -1))):
            copies.append(send(r.CS[i], r.CR[i].at[slot], r.s_cfd[i], slot, at(dx, dy)))
        return copies

    there = (x > 0, x < NPX - 1, y > 0, y < NPY - 1)
    block = (1, 0, 3, 2)

    def cfd_wait(i, table, copies):
        for copy in copies:
            copy.wait_recv()
        sent.extend(copies)
        for c in range(CHANNELS[i]):
            for b in range(4):
                for h in range(2):
                    row = r.CR[i][b, c, block[b] + 4 * h : block[b] + 4 * h + 1, :]
                    place = c * EXT + ROWS + 2 * b + h
                    table[place : place + 1, :] = jnp.where(there[b], row, 0.0)

    cfd_send(0, r.TQ)

    loaded(5, 8)
    lane16 = lane_iota(16)
    groups_f = [jnp.zeros((16, 128), F32) for _ in range(5)]
    groups_l = [jnp.zeros((16, 128), F32) for _ in range(5)]
    for t in range(2 * NZ + 1):
        if t < NZ:
            tile = r.V[0][t + 1, PAD + 16 : PAD + 32, :]
        elif t < 2 * NZ:
            tile = r.B[0][t - NZ, 16:32, :]
        else:
            tile = r.E[0][16:32, :]
        g, q = t // 8, t % 8
        own = (lane16 >= 16 * q) & (lane16 < 16 * q + 16)
        groups_f[g] = jnp.where(own, roll(tile, 16 * q, 1), groups_f[g])
        groups_l[g] = jnp.where(own, roll(tile, 16 * q + 16, 1), groups_l[g])
    for g in range(5):
        r.first[g] = groups_f[g]
        r.final[g] = groups_l[g]

    pl.semaphore_wait(barrier, len(partners))

    copies0 = cfd_start(0)
    strips = []
    for dx in (-1, 0, 1):
        slot = 2 * (1 - dx)
        strips.append(send(r.final, r.strips.at[slot], r.s_strip, slot, at(dx, 1)))
        strips.append(send(r.first, r.strips.at[slot + 1], r.s_strip, slot + 1, at(dx, -1)))
    tiles = []
    for s, (dx, row) in enumerate(((1, 0), (-1, 32))):
        padded = pl.ds(PAD + row, 16)
        rows = pl.ds(row, 16)
        tiles.append(send(start_in, r.V[0].at[pl.ds(1, NZ), padded, :], r.s_tile, 3 * s, at(dx, 0)))
        tiles.append(send(source_in, r.B[0].at[:, rows, :], r.s_tile, 3 * s + 1, at(dx, 0)))
        tiles.append(send(depth_in, r.E[0].at[rows, :], r.s_tile, 3 * s + 2, at(dx, 0)))

    loaded(8, 10)
    cells = r.receive[...]
    hi_of, lo_of = cells >> 7, cells & 127
    inverse = jnp.zeros((2 * ROWS, 128), F32)
    for chunk in range(4):
        lefts, rights = [], []
        for o in range(8 * chunk, 8 * chunk + 8):
            match = row_iota(ROWS) == jnp.broadcast_to(hi_of[o : o + 1, :], (ROWS, 128))
            lanes = lane_iota(ROWS).astype(F32)
            lefts.append(
                jnp.concatenate([jnp.where(match, F32(o + 1), 0.0), jnp.where(match, lanes, 0.0)], axis=0)
            )
            low = row_iota(128) == jnp.broadcast_to(lo_of[o : o + 1, :], (128, 128))
            rights.append(jnp.where(low, F32(1.0), 0.0))
        left = jnp.concatenate(lefts, axis=1).astype(jnp.bfloat16)
        right = jnp.concatenate(rights, axis=1).astype(jnp.bfloat16)
        inverse = inverse + lax.dot_general(
            left, right, (((1,), (1,)), ((), ())), preferred_element_type=F32
        )
    r.INV[...] = inverse.astype(I32)

    index = r.neighbour[...]
    for edge in (4288, 4480, 4672, 4864):
        index = index + jnp.where(r.neighbour[...] >= edge, 64, 0)
    r.HI[...] = index >> 7
    r.LO[...] = index & 127

    cfd_wait(0, r.TQ, copies0)
    loaded(10, 13)

    def part(f, quarter):
        return pl.ds(pl.multiple_of(f * ROWS + 8 * quarter, 8), 8)

    def cells_of(base, quarter):
        return pl.ds(pl.multiple_of(base + 8 * quarter, 8), 8)

    def beside_of(table, components, f, quarter):
        rows = part(f, quarter)
        return table_gather(reader(table), EXT, components, r.HI[rows, :], r.LO[rows, :])

    def normal_of(c, f, quarter):
        return r.normal[part(c * FACES + f, quarter), :]

    zero = jnp.zeros((8, 128), F32)

    @pl.loop(0, 4)
    def _(quarter):
        mine = [r.TQ[cells_of(c * EXT, quarter), :] for c in range(4)]

        def face(f, totals):
            beside = beside_of(r.TQ, 4, f, quarter)
            flux = normal_of(0, f, quarter) * (mine[0] + beside[0])
            for c in (1, 2):
                flux = flux + normal_of(c, f, quarter) * (mine[c] + beside[c])
            flux = 0.5 * flux
            out, into = jnp.maximum(flux, 0.0), jnp.minimum(flux, 0.0)
            return tuple(totals[c] + (out * mine[c] + into * beside[c]) for c in range(4))

        totals = lax.fori_loop(0, FACES, face, (zero,) * 4)
        scale = r.step[cells_of(0, quarter), :]
        for c in range(3):
            r.TS[cells_of(c * EXT, quarter), :] = mine[c] - scale * totals[c]
        r.FRAC[cells_of(0, quarter), :] = mine[3] - scale * totals[3]

    cfd_send(1, r.TS)
    copies1 = cfd_start(1)

    for copy in tiles + strips:
        copy.wait_recv()
    sent.extend(tiles + strips)
    for block_row in range(3):
        rows = slice(16 * block_row, 16 * block_row + 16)
        padded = slice(PAD + 16 * block_row, PAD + 16 * block_row + 16)
        for t in range(2 * NZ + 1):
            g, q = t // 8, t % 8
            lower = r.strips[2 * block_row, g]
            upper = r.strips[2 * block_row + 1, g]
            value = jnp.where(
                lane16 < 16,
                roll(upper, -16 * q, 1),
                jnp.where(lane16 >= 112, roll(lower, 112 - 16 * q, 1), 0.0),
            )
            if t < NZ:
                r.V[1][t + 1, padded, :] = value
            elif t < 2 * NZ:
                r.B[1][t - NZ, rows, :] = value
            else:
                r.E[1][rows, :] = value

    fine_rows = row_iota(48) + 16 * (x - 1)
    inside_a = (fine_rows >= 0) & (fine_rows < 16 * NPX)
    side_ok = jnp.where(lane_iota(48) < 64, jnp.where(y < NPY - 1, 1, 0), jnp.where(y > 0, 1, 0)) > 0
    insides = [inside_a, inside_a & side_ok]
    data = slice(PAD, PAD + 48)

    def mask_start(k):
        for s in range(2):
            r.V[s][k + 1, data, :] = jnp.where(insides[s], r.V[s][k + 1, data, :], 0.0)

    each_layer(mask_start)

    depths = [jnp.where(insides[s], r.E[s][...], 0.0) for s in range(2)]
    lane48 = lane_iota(48)
    for s in range(2):
        depth, other = depths[s], depths[1 - s]
        r.E[s][...] = depth
        right = jnp.where(lane48 == 127, roll(other, 127, 1), roll(depth, 127, 1))
        left = jnp.where(lane48 == 0, roll(other, 1, 1), roll(depth, 1, 1))
        faces = (
            0.5 * (depth + roll(depth, 47, 0)),
            0.5 * (depth + roll(depth, 1, 0)),
            0.5 * (depth + right),
            0.5 * (depth + left),
        )
        total = faces[0] + faces[1] + faces[2] + faces[3]
        for i, face in enumerate(faces):
            r.C[s][i] = face
        for i, extra in enumerate((VERT, 2 * VERT)):
            r.D[s][i] = total + extra
            r.W[s][i] = jnp.where(insides[s], RELAX / (total + extra), 0.0)

    def fine_sweep(source, target, lo=0, hi=48, halves=(0, 1)):
        fine_operate(r, source, target, False, lo, hi, halves)

    lane24 = lane_iota(24)
    down24 = (2 * lane24) & 127

    def fine_pair(a_even, a_odd, b_even, b_odd):
        mean_a = lane_gather(pair_mean_rows(a_even, a_odd), down24)
        mean_b = lane_gather(pair_mean_rows(b_even, b_odd), down24)
        return jnp.where(lane24 < 64, mean_a, mean_b)

    even24, odd24 = pl.ds(0, 24, stride=2), pl.ds(1, 24, stride=2)
    even_pad, odd_pad = pl.ds(PAD, 24, stride=2), pl.ds(PAD + 1, 24, stride=2)
    inside_1 = inside_of(x, y, 24, 8 * (x - 1), 96, 64, 8 * NPX, 64 * NPY)
    r.M1[...] = jnp.where(inside_1, F32(1.0), 0.0)
    depth_1 = fine_pair(r.E[0][even24, :], r.E[0][odd24, :], r.E[1][even24, :], r.E[1][odd24, :])
    depth_1 = jnp.where(inside_1, depth_1, 0.0)
    levels[1].E[...] = depth_1
    set_coefficients(levels[1], depth_1, inside_1, 0.25)

    def fine_coarsen(k):
        levels[1].B[k] = fine_pair(
            r.U[0][k + 1, even_pad, :], r.U[0][k + 1, odd_pad, :],
            r.U[1][k + 1, even_pad, :], r.U[1][k + 1, odd_pad, :],
        )

    lane8 = lane_iota(8)

    lane4 = lane_iota(4)

    def pack_second(cycle):
        count = NZ + 1 if cycle == 0 else NZ
        even, odd = pl.ds(8, 4, stride=2), pl.ds(9, 4, stride=2)
        for g in range(5):
            packed = jnp.zeros((4, 128), F32)
            for q in range(4):
                k = 4 * g + q
                if k >= count:
                    continue
                if k < NZ:
                    mean = pair_mean_rows(levels[1].T[k, even, :], levels[1].T[k, odd, :])
                else:
                    mean = pair_mean_rows(levels[1].E[even, :], levels[1].E[odd, :])
                own = (lane4 >= 32 * q) & (lane4 < 32 * q + 32)
                packed = jnp.where(own, lane_gather(mean, (2 * lane4 + 64 * (q % 2)) & 127), packed)
            r.P[cycle][g] = packed
            r.N[cycle][1, 1, g] = packed

    def start_second(cycle):
        copies = []
        for dx in (-1, 0, 1):
            for dy in (-1, 0, 1):
                if dx or dy:
                    d, j = 1 - dx, 1 - dy
                    copies.append(send(r.P[cycle], r.N[cycle].at[d, j], r.s_second[cycle], 3 * d + j, at(dx, dy)))
        return copies

    def unpack_second(cycle):
        got = r.N[cycle]
        for m, pair in enumerate(((0, 1), (2, 2))):
            rows = slice(8 * m, 8 * m + 8)
            for g in range(5):
                tiles_of = [jnp.concatenate([got[d, j, g] for d in pair], axis=0) for j in range(3)]
                for q in range(4):
                    k = 4 * g + q
                    if k > NZ or (k == NZ and cycle > 0):
                        continue
                    value = jnp.where(
                        lane8 < 32,
                        roll(tiles_of[1], -32 * q, 1),
                        jnp.where(
                            lane8 < 64,
                            roll(tiles_of[2], 32 - 32 * q, 1),
                            roll(tiles_of[0], 96 - 32 * q, 1),
                        ),
                    )
                    if k < NZ:
                        levels[2].B[k, rows, :] = value
                    else:
                        levels[2].E[rows, :] = value

    lane2 = lane_iota(2)

    def pack_deep(cycle):
        count = NZ + 1 if cycle == 0 else NZ
        even, odd = pl.ds(4, 2, stride=2), pl.ds(5, 2, stride=2)
        for g in range(3):
            packed = jnp.zeros((2, 128), F32)
            for q in range(8):
                k = 8 * g + q
                if k >= count:
                    continue
                if k < NZ:
                    mean = pair_mean_rows(levels[2].T[k, even, :], levels[2].T[k, odd, :])
                else:
                    mean = pair_mean_rows(levels[2].E[even, :], levels[2].E[odd, :])
                own = (lane2 >= 16 * q) & (lane2 < 16 * q + 16)
                packed = jnp.where(own, lane_gather(mean, (2 * lane2 + 96 * q) & 127), packed)
            r.P3[cycle][g] = packed
            r.G[cycle][8, 1, g] = packed

    def start_deep(cycle):
        copies = []
        for dx in range(-REACH, REACH + 1):
            for dy in (-1, 0, 1):
                if dx == 0 and dy == 0:
                    continue
                d, j = 8 - dx, 1 - dy
                copies.append(send(r.P3[cycle], r.G[cycle].at[d, j], r.s_deep[cycle], 3 * d + j, at(dx, dy)))
        return copies

    def unpack_deep(cycle):
        grid_of = r.G[cycle]

        @pl.loop(0, 4)
        def _(m):
            rows = pl.ds(pl.multiple_of(8 * m, 8), 8)
            for g in range(3):
                tiles_of = [
                    jnp.concatenate([grid_of[4 * m + i, j, g] for i in range(4)], axis=0) for j in range(3)
                ]
                for q in range(8):
                    k = 8 * g + q
                    if k > NZ or (k == NZ and cycle > 0):
                        continue
                    value = jnp.where(
                        lane8 < 16,
                        roll(tiles_of[1], -16 * q, 1),
                        jnp.where(
                            lane8 < 64,
                            roll(tiles_of[2], 16 - 16 * q, 1),
                            roll(tiles_of[0], 112 - 16 * q, 1),
                        ),
                    )
                    if k < NZ:
                        levels[3].B[k, rows, :] = value
                    else:
                        levels[3].E[rows, :] = value

    def deep_coefficients(level):
        here = levels[level]
        rows = here.R
        first, tile, width = {2: (-1, 4, 32), 3: (-8, 2, 16), 4: (-8, 1, 8)}[level]
        inside = inside_of(x, y, rows, tile * (x + first), 64, width, tile * NPX, width * NPY)
        if level > 3:
            above = levels[level - 1].E
            mean = pair_mean_rows(above[pl.ds(0, rows, stride=2), :], above[pl.ds(1, rows, stride=2), :])
            depth = lane_gather(mean, (2 * lane_iota(rows)) & 127)
        else:
            depth = here.E[...]
        depth = jnp.where(inside, depth, 0.0)
        here.E[...] = depth
        set_coefficients(here, depth, inside, 0.25**level)

    def descend(here, lo, hi):
        point_step(here)
        sweep_step(here, here.V, here.U)
        operate(here, here.U, here.T, True, lo, hi)

    def solve_deep():
        descend(levels[3], 0, 32)
        coarsen_step(levels[3], levels[4])
        last = levels[4]
        point_step(last)
        sweep_step(last, last.V, last.U)
        sweep_step(last, last.U, last.V)
        sweep_step(last, last.V, last.U)
        for level, first, split, before, after in (
            (3, 0, 64, (8, 24), (8, 24)), (2, 14, 64, (0, 16), (0, 16)), (1, 0, 96, (0, 24), (8, 16)),
        ):
            here = levels[level]
            refine_add(levels[level + 1].U, first, here, here.U, split)
            sweep_step(here, here.U, here.V, *before)
            sweep_step(here, here.V, here.U, *after)

    def down(lo, hi):
        fine_operate(r, r.V, r.U, True, lo, hi)
        each_layer(fine_coarsen)
        descend(levels[1], 8, 16)

    def start_near(cycle):
        own = slice(PAD + 8, PAD + 16)
        values = [levels[1].U[k + 1, own, :] for k in range(NZ)]
        for pair in range(9):
            value = values[2 * pair]
            if 2 * pair + 1 < NZ:
                value = jnp.where(lane8 < 64, value, roll(values[2 * pair + 1], 64, 1))
            r.mine[cycle][pair] = value
        for g in range(2):
            left, right = jnp.zeros((8, 128), F32), jnp.zeros((8, 128), F32)
            for q in range(16):
                if 16 * g + q < NZ:
                    columns = (lane8 >= 8 * q) & (lane8 < 8 * q + 8)
                    left = jnp.where(columns, roll(values[16 * g + q], 8 * q, 1), left)
                    right = jnp.where(columns, roll(values[16 * g + q], 8 * q - 56, 1), right)
            r.left[cycle][g] = left
            r.right[cycle][g] = right
        copies = []
        for s, dx in enumerate((1, -1)):
            copies.append(send(r.mine[cycle], r.near[cycle].at[s], r.s_near[cycle], s, at(dx, 0)))
        for dx in (-1, 0, 1):
            slot = 2 * (1 - dx)
            copies.append(send(r.right[cycle], r.sides[cycle].at[slot], r.s_near[cycle], 2 + slot, at(dx, 1)))
            copies.append(send(r.left[cycle], r.sides[cycle].at[slot + 1], r.s_near[cycle], 3 + slot, at(dx, -1)))
        return copies

    def add_near(cycle):
        half_lane = lane24 >> 1
        for k in range(NZ):
            pair, odd, g, q = k // 2, k % 2, k // 16, k % 16
            for block_row in range(3):
                middle = r.mine[cycle][pair] if block_row == 1 else r.near[cycle][block_row // 2, pair]
                lower, upper = r.sides[cycle][2 * block_row, g], r.sides[cycle][2 * block_row + 1, g]
                aside = jnp.where(lane8 < 96, roll(upper, 64 - 8 * q, 1), roll(lower, 120 - 8 * q, 1))
                value = jnp.where(lane8 < 64, roll(middle, 64 * odd, 1), aside)
                levels[1].T[k, 8 * block_row : 8 * block_row + 8, :] = value

        def body(k):
            value = levels[1].T[k] * r.M1[...]
            for s, lanes in ((0, half_lane), (1, half_lane + 64)):
                spread = lane_gather(value, lanes)
                r.U[s][k + 1, even_pad, :] = spread
                r.U[s][k + 1, odd_pad, :] = spread
                r.V[s][k + 1, data, :] = r.V[s][k + 1, data, :] + r.U[s][k + 1, data, :]

        each_layer(body)

    fine_sweep(r.V, r.U)
    fine_sweep(r.U, r.V)
    down(8, 40)
    pack_second(0)
    second0 = start_second(0)

    cfd_wait(1, r.TS, copies1)
    loaded(13, 14)

    def divergence(quarter):
        mine = [r.TS[cells_of(c * EXT, quarter), :] for c in range(3)]

        def face(f, carry):
            flow, pull, weights = carry
            beside = beside_of(r.TS, 4, f, quarter)
            for c in range(3):
                flow = flow + normal_of(c, f, quarter) * (mine[c] + beside[c])
            weight = r.weight[part(f, quarter), :]
            return flow, pull + weight * beside[3], weights + weight

        flow, pull, weights = lax.fori_loop(0, FACES, face, (zero,) * 3)
        here = cells_of(0, quarter)
        flow, inverse_sum = 0.5 * flow, 1.0 / weights
        r.DIV[here, :] = flow
        r.IWS[here, :] = inverse_sum
        r.TP[0][here, :] = (pull - flow) * inverse_sum

    def descend_second(cycle, copies):
        for copy in copies:
            copy.wait_recv()
        sent.extend(copies)
        unpack_second(cycle)
        if cycle == 0:
            deep_coefficients(2)
        descend(levels[2], 0, 8)
        pack_deep(cycle)
        return start_deep(cycle)

    pl.loop(0, 2)(divergence)
    deep0 = descend_second(0, second0)
    pl.loop(2, 4)(divergence)
    cfd_send(2, r.TP[0])
    copies2 = cfd_start(2)

    for copy in deep0:
        copy.wait_recv()
    sent.extend(deep0)
    unpack_deep(0)
    deep_coefficients(3)
    deep_coefficients(4)
    solve_deep()
    near0 = start_near(0)

    def pressure_sweep(before, after):
        @pl.loop(0, 4)
        def _(quarter):
            pull = zero
            for f in range(FACES):
                pull = pull + r.weight[part(f, quarter), :] * beside_of(before, 1, f, quarter)[0]
            here = cells_of(0, quarter)
            after[here, :] = (pull - r.DIV[here, :]) * r.IWS[here, :]

    cfd_wait(2, r.TP[0], copies2)
    pressure_sweep(r.TP[0], r.TP[1])
    cfd_send(3, r.TP[1])
    copies3 = cfd_start(3)

    for copy in near0:
        copy.wait_recv()
    sent.extend(near0)
    add_near(0)
    fine_sweep(r.V, r.U)
    fine_sweep(r.U, r.V)
    fine_sweep(r.V, r.U, 8, 40)
    fine_sweep(r.U, r.V, 8, 40)
    down(8, 40)
    pack_second(1)
    second1 = start_second(1)

    cfd_wait(3, r.TP[1], copies3)
    pressure_sweep(r.TP[1], r.TP[2])
    cfd_send(4, r.TP[2])
    copies4 = cfd_start(4)
    pressure_copy = pltpu.make_async_copy(r.TP[2].at[pl.ds(0, ROWS), :], pressure_out, r.load.at[18])
    pressure_copy.start()
    deep1 = descend_second(1, second1)

    for copy in deep1:
        copy.wait_recv()
    sent.extend(deep1)
    unpack_deep(1)
    solve_deep()
    near1 = start_near(1)

    cfd_wait(4, r.TP[2], copies4)

    @pl.loop(0, 4)
    def _(quarter):
        here = cells_of(0, quarter)
        pressure = r.TP[2][here, :]
        totals = [zero] * 3
        for f in range(FACES):
            difference = beside_of(r.TP[2], 1, f, quarter)[0] - pressure
            totals = [totals[c] + normal_of(c, f, quarter) * difference for c in range(3)]
        for c in range(3):
            r.COR[cells_of(c * ROWS, quarter), :] = r.TS[cells_of(c * EXT, quarter), :] - r.step[here, :] * (
                0.5 * totals[c]
            )

    for copy in near1:
        copy.wait_recv()
    sent.extend(near1)
    add_near(1)
    fine_sweep(r.V, r.U, 8, 40)
    fine_sweep(r.U, r.V, 16, 32, (0,))

    loaded(14, 18)

    own_rows = pl.ds(pl.multiple_of(x * 8, 8), 8)

    def interpolate(quarter):
        corner = r.corner[cells_of(0, quarter), :]
        column = corner & 127
        point_row = (corner >> 7) & 15
        point_layer = corner >> 11

        def layer(k, picks):
            found = []
            for lanes in (column, column + 1):
                low, high = zero, zero
                before = None
                for i in range(16):
                    row = jnp.broadcast_to(r.V[0][k + 1, PAD + 16 + i : PAD + 17 + i, :], (8, 128))
                    value = lane_gather(row, lanes)
                    here = point_row == i
                    if i < 15:
                        low = jnp.where(here, value, low)
                    if before is not None:
                        high = jnp.where(before, value, high)
                    before = here
                found.append((low, high))
            found = (found[0][0], found[1][0], found[0][1], found[1][1])
            lower, upper = point_layer == k, point_layer == k - 1
            return tuple(jnp.where(lower, found[i], picks[i]) for i in range(4)) + tuple(
                jnp.where(upper, found[i], picks[4 + i]) for i in range(4)
            )

        picks = (zero,) * 8
        for k in range(NZ):
            picks = layer(k, picks)
        for quantity in range(4):
            total = zero
            for p in range(8):
                total = total + r.stencil[cells_of((quantity * 8 + p) * ROWS, quarter), :] * picks[p]
            for i in range(8):
                r.S[pl.ds(64 * quarter + 8 * i + quantity, 1), :] = total[i : i + 1, :]

    potential_copy = pltpu.make_async_copy(r.V[0].at[pl.ds(1, NZ), middle, :], potential_out, r.load.at[19])
    potential_copy.start()

    everyone = []
    for away in (2, 1, 3, 0):
        quarter = lax.rem(x // 8 + away, 4)
        interpolate(quarter)
        for i in range(0 if away else 1, 8):
            there_x = quarter * 8 + (i if away else lax.rem(x + i, 8))
            rows = pl.ds(pl.multiple_of(there_x * 8, 8), 8)
            slot = lax.rem(there_x - x + NPX, NPX)
            everyone.append(send(r.S.at[rows, :], r.RB.at[own_rows, :], r.s_all, slot, (there_x, y)))
    r.RB[own_rows, :] = r.S[own_rows, :]
    for o in range(1, NPX):
        pltpu.make_async_remote_copy(
            src_ref=r.S.at[0:8, :],
            dst_ref=r.RB.at[0:8, :],
            send_sem=r.s_all[0].at[o],
            recv_sem=r.s_all[1].at[o],
            device_id=at(o, 0),
            device_id_type=MESH,
        ).wait_recv()
    sent.extend(everyone)

    @pl.loop(0, 4)
    def _(quarter):
        here = cells_of(0, quarter)
        slot_hi, slot_lo = r.INV[here, :] - 1, r.INV[cells_of(ROWS, quarter), :]
        targets = table_gather(lambda c, j: r.RB[8 * j + c : 8 * j + c + 1, :], NPX, 4, slot_hi, slot_lo)
        strength = jnp.where(slot_hi >= 0, r.blend[here, :], 0.0)
        for c in range(3):
            velocity = r.COR[cells_of(c * ROWS, quarter), :]
            velocity_out[cells_of(c * ROWS, quarter), :] = velocity - strength * (velocity - targets[c])
        level_target = jax.nn.sigmoid(4.0 * (targets[3] - r.height[here, :]))
        fraction = r.FRAC[here, :]
        fraction_out[here, :] = fraction - strength * (fraction - level_target)

    pressure_copy.wait()
    potential_copy.wait()
    for copy in sent:
        copy.wait_send()


def hand_over(*refs):
    given, results, held, arrive, leave = refs[0:4], refs[4:8], refs[8:12], refs[12], refs[13]
    ins = [pltpu.make_async_copy(given[i], held[i], arrive.at[i]) for i in range(4)]
    outs = [pltpu.make_async_copy(held[i], results[i], leave.at[i]) for i in range(4)]
    for copy in ins:
        copy.start()
    for i in range(4):
        ins[i].wait()
        outs[i].start()
    for copy in outs:
        copy.wait()


def on_device(
    source, water_depth, potential_start, velocity, fraction, pressure, neighbour, send_slot,
    face_normal, face_weight, step_scale, height, blend_weight, corner, stencil_weight, receive_cell,
):
    def lanes(array):
        return array.reshape(-1, 128)

    args = (
        source, water_depth, potential_start, lanes(velocity), lanes(fraction), lanes(pressure), lanes(neighbour),
        send_slot, lanes(face_normal), lanes(face_weight), lanes(step_scale), lanes(height),
        lanes(blend_weight), lanes(corner), lanes(stencil_weight), lanes(receive_cell),
    )
    shapes = ((NZ, 16, 128), (3 * ROWS, 128), (ROWS, 128), (ROWS, 128))
    results = pl.pallas_call(
        kernel,
        name="step",
        out_shape=[jax.ShapeDtypeStruct(shape, F32) for shape in shapes],
        in_specs=[pl.BlockSpec(memory_space=pltpu.HBM)] * len(args),
        out_specs=[pl.BlockSpec(memory_space=space) for space in (pltpu.HBM, pltpu.VMEM, pltpu.VMEM, pltpu.HBM)],
        scratch_shapes=jax.tree_util.tree_leaves(scratch_plan()),
        compiler_params=pltpu.CompilerParams(
            collective_id=0, has_side_effects=True, vmem_limit_bytes=67043328
        ),
    )(*args)
    dma = pltpu.SemaphoreType.DMA
    results = pl.pallas_call(
        hand_over,
        name="hand_over",
        out_shape=[jax.ShapeDtypeStruct(shape, F32) for shape in shapes],
        in_specs=[pl.BlockSpec(memory_space=pltpu.HBM)] * len(shapes),
        out_specs=[pl.BlockSpec(memory_space=pltpu.HBM)] * len(shapes),
        scratch_shapes=[pltpu.VMEM(shape, F32) for shape in shapes] + [dma((4,)), dma((4,))],
        compiler_params=pltpu.CompilerParams(vmem_limit_bytes=67043328),
    )(*results)
    potential, velocity_out, fraction_out, pressure_out = results
    return (
        potential,
        velocity_out.reshape(3, 1, 1, -1),
        fraction_out.reshape(1, 1, -1),
        pressure_out.reshape(1, 1, -1),
    )


def solution(mesh):
    in_specs = (
        P(None, "px", "py"),
        P("px", "py"),
        P(None, "px", "py"),
        P(None, "px", "py", None),
        P("px", "py", None),
        P("px", "py", None),
        P(None, "px", "py", None),
        P(None, "px", "py", None),
        P(None, None, "px", "py", None),
        P(None, "px", "py", None),
        P("px", "py", None),
        P("px", "py", None),
        P("px", "py", None),
        P("px", "py", None),
        P(None, None, "px", "py", None),
        P("px", "py", None),
    )
    out_specs = (
        P(None, "px", "py"),
        P(None, "px", "py", None),
        P("px", "py", None),
        P("px", "py", None),
    )
    return jax.shard_map(on_device, mesh=mesh, in_specs=in_specs, out_specs=out_specs, check_vma=False)
```

```python
from types import SimpleNamespace

import jax
import jax.numpy as jnp
from jax import lax
from jax.experimental import pallas as pl
from jax.experimental.pallas import tpu as pltpu
from jax.sharding import PartitionSpec as P

F32 = jnp.float32
I32 = jnp.int32
MESH = pl.DeviceIdType.MESH
NPX, NPY = 32, 8
NZ = 17
FACES = 6
ROWS = 32
EXT = 40
PAD = 8
VERT = 0.01
RELAX = 0.8
REACH = 6

GATHER_DIMS = lax.GatherDimensionNumbers(
    offset_dims=(),
    collapsed_slice_dims=(1,),
    start_index_map=(1,),
    operand_batching_dims=(0,),
    start_indices_batching_dims=(0,),
)


def lane_gather(values, lanes):
    return lax.gather(
        values,
        lanes[..., None],
        GATHER_DIMS,
        slice_sizes=(1, 1),
        mode=lax.GatherScatterMode.PROMISE_IN_BOUNDS,
    )


def lane_iota(rows):
    return lax.broadcasted_iota(I32, (rows, 128), 1)


def row_iota(rows):
    return lax.broadcasted_iota(I32, (rows, 128), 0)


def roll(values, shift, axis):
    shift = shift % values.shape[axis]
    return values if shift == 0 else pltpu.roll(values, shift, axis)


def over_layers(body, chunk=4):
    whole = NZ // chunk
    if whole > 1:

        @pl.loop(0, whole)
        def _(step):
            body([step * chunk + j for j in range(chunk)])

    rest = list(range(whole * chunk if whole > 1 else 0, NZ))
    if rest:
        body(rest)


def each_layer(body, chunk=4):
    def bodies(layers):
        for k in layers:
            body(k)

    over_layers(bodies, chunk)


def kind(k):
    return min(k, 1) if isinstance(k, int) else jnp.minimum(k, 1)


def inside_of(x, y, rows, row_first, lane_split, width, height, depth):
    row = row_iota(rows) + row_first
    lane = lane_iota(rows)
    column = jnp.where(lane < lane_split, lane, lane - 128) + y * width
    return (row >= 0) & (row < height) & (column >= 0) & (column < depth)


def set_coefficients(level, depth, inside, scale):
    rows = depth.shape[0]
    half = 0.5 * scale
    faces = (
        half * (depth + roll(depth, rows - 1, 0)),
        half * (depth + roll(depth, 1, 0)),
        half * (depth + roll(depth, 127, 1)),
        half * (depth + roll(depth, 1, 1)),
    )
    total = faces[0] + faces[1] + faces[2] + faces[3]
    for i, face in enumerate(faces):
        level.C[i] = face
    for i, extra in enumerate((VERT, 2 * VERT)):
        diagonal = total + extra
        level.D[i] = diagonal
        level.W[i] = jnp.where(inside, RELAX / diagonal, 0.0)


def point_step(level):
    def body(k):
        level.V[k + 1, PAD : PAD + level.R, :] = level.W[kind(k)] * level.B[k]

    each_layer(body)


def operate(level, source, target, residual, lo, hi):
    def body(layers):
        for start in range(lo, hi, 8):
            rows, mid = slice(start, start + 8), slice(PAD + start, PAD + start + 8)
            up, down = slice(PAD + start + 1, PAD + start + 9), slice(PAD + start - 1, PAD + start + 7)
            faces = [level.C[i, rows, :] for i in range(4)]
            below, values = source[layers[0], mid, :], source[layers[0] + 1, mid, :]
            for k in layers:
                above = source[k + 2, mid, :]
                total = faces[0] * source[k + 1, up, :] + faces[1] * source[k + 1, down, :]
                total = total + (faces[2] * roll(values, 127, 1) + faces[3] * roll(values, 1, 1))
                total = (total + VERT * (below + above)) + level.B[k, rows, :]
                if residual:
                    target[k, rows, :] = total - level.D[kind(k), rows, :] * values
                else:
                    target[k + 1, mid, :] = (1.0 - RELAX) * values + level.W[kind(k), rows, :] * total
                below, values = values, above

    over_layers(body, NZ)


def sweep_step(level, source, target, lo=0, hi=None):
    operate(level, source, target, False, lo, level.R if hi is None else hi)


def pair_mean_rows(even, odd):
    total = even + odd
    return 0.25 * (total + roll(total, 127, 1))


def coarsen_step(fine, coarse):
    half = coarse.R
    lanes = (2 * lane_iota(half)) & 127

    def body(k):
        total = pair_mean_rows(fine.T[k, pl.ds(0, half, stride=2), :], fine.T[k, pl.ds(1, half, stride=2), :])
        coarse.B[k] = lane_gather(total, lanes)

    each_layer(body)


def refine_add(correction, first, fine, target, lane_split):
    rows = fine.R
    half = rows // 2
    lane = lane_iota(half)
    lanes = jnp.where(lane < lane_split, lane >> 1, (lane >> 1) + 64)

    def body(k):
        spread = lane_gather(correction[k + 1, PAD + first : PAD + first + half, :], lanes)
        fine.T[k, pl.ds(0, half, stride=2), :] = spread
        fine.T[k, pl.ds(1, half, stride=2), :] = spread
        target[k + 1, PAD : PAD + rows, :] = target[k + 1, PAD : PAD + rows, :] + fine.T[k]

    each_layer(body)


def fine_operate(top, source, target, residual, lo, hi, halves=(0, 1)):
    lane = lane_iota(8)
    first, last = lane == 0, lane == 127

    def body(layers):
        for start in range(lo, hi, 8):
            rows, mid = slice(start, start + 8), slice(PAD + start, PAD + start + 8)
            up, down = slice(PAD + start + 1, PAD + start + 9), slice(PAD + start - 1, PAD + start + 7)
            faces = [[top.C[s][i, rows, :] for i in range(4)] for s in range(2)]
            below = [source[s][layers[0], mid, :] for s in range(2)]
            values = [source[s][layers[0] + 1, mid, :] for s in range(2)]
            for k in layers:
                above = [source[s][k + 2, mid, :] for s in range(2)]
                rights = [roll(values[s], 127, 1) for s in range(2)]
                lefts = [roll(values[s], 1, 1) for s in range(2)]
                for s in halves:
                    right = jnp.where(last, rights[1 - s], rights[s])
                    left = jnp.where(first, lefts[1 - s], lefts[s])
                    total = faces[s][0] * source[s][k + 1, up, :] + faces[s][1] * source[s][k + 1, down, :]
                    total = total + (faces[s][2] * right + faces[s][3] * left)
                    total = (total + VERT * (below[s] + above[s])) + top.B[s][k, rows, :]
                    if residual:
                        value = total - top.D[s][kind(k), rows, :] * values[s]
                    else:
                        value = (1.0 - RELAX) * values[s] + top.W[s][kind(k), rows, :] * total
                    target[s][k + 1, mid, :] = value
                below, values = values, above

    over_layers(body, NZ)


def table_gather(read_row, count, components, hi, lo):
    picked = [jnp.zeros((8, 128), F32) for _ in range(components)]
    for j in range(count):
        mask = hi == j
        for c in range(components):
            row = jnp.broadcast_to(read_row(c, j), (8, 128))
            picked[c] = jnp.where(mask, lane_gather(row, lo), picked[c])
    return picked


CHANNELS = (4, 4, 1, 1, 1)


def scratch_plan():
    def vmem(*shape, dtype=F32):
        return pltpu.VMEM(shape, dtype)

    def pair(*shape):
        return [vmem(*shape), vmem(*shape)]

    def sems(count):
        return [pltpu.SemaphoreType.DMA((count,)), pltpu.SemaphoreType.DMA((count,))]

    def level(rows):
        return dict(
            V=vmem(NZ + 2, rows + 2 * PAD, 128),
            U=vmem(NZ + 2, rows + 2 * PAD, 128),
            B=vmem(NZ, rows, 128),
            T=vmem(NZ, rows, 128),
            C=vmem(4, rows, 128),
            W=vmem(2, rows, 128),
            D=vmem(2, rows, 128),
            E=vmem(rows, 128),
        )

    return dict(
        V=pair(NZ + 2, 48 + 2 * PAD, 128),
        U=pair(NZ + 2, 48 + 2 * PAD, 128),
        B=pair(NZ, 48, 128),
        C=pair(4, 48, 128),
        W=pair(2, 48, 128),
        D=pair(2, 48, 128),
        E=pair(48, 128),
        levels=[level(24), level(16), level(32), level(16)],
        M1=vmem(24, 128),
        first=vmem(5, 16, 128),
        final=vmem(5, 16, 128),
        strips=vmem(6, 5, 16, 128),
        P=pair(5, 4, 128),
        N=pair(3, 3, 5, 4, 128),
        P3=pair(3, 2, 128),
        G=pair(16, 3, 3, 2, 128),
        near=pair(2, 9, 8, 128),
        sides=pair(6, 2, 8, 128),
        mine=pair(9, 8, 128),
        left=pair(2, 8, 128),
        right=pair(2, 8, 128),
        HI=vmem(FACES * ROWS, 128, dtype=I32),
        LO=vmem(FACES * ROWS, 128, dtype=I32),
        SI=vmem(8, 128, dtype=I32),
        TQ=vmem(4 * EXT, 128),
        TS=vmem(4 * EXT, 128),
        TP=[vmem(EXT, 128) for _ in range(3)],
        CS=[vmem(n, 8, 128) for n in CHANNELS],
        CR=[vmem(4, n, 8, 128) for n in CHANNELS],
        FRAC=vmem(ROWS, 128),
        DIV=vmem(ROWS, 128),
        IWS=vmem(ROWS, 128),
        COR=vmem(3 * ROWS, 128),
        INV=vmem(2 * ROWS, 128, dtype=I32),
        S=vmem(256, 128),
        RB=vmem(256, 128),
        neighbour=vmem(FACES * ROWS, 128, dtype=I32),
        slot=vmem(4, 1, 1, 192, dtype=I32),
        normal=vmem(3 * FACES * ROWS, 128),
        weight=vmem(FACES * ROWS, 128),
        step=vmem(ROWS, 128),
        height=vmem(ROWS, 128),
        blend=vmem(ROWS, 128),
        corner=vmem(ROWS, 128, dtype=I32),
        stencil=vmem(32 * ROWS, 128),
        receive=vmem(ROWS, 128, dtype=I32),
        load=pltpu.SemaphoreType.DMA((20,)),
        s_tile=sems(6),
        s_strip=sems(6),
        s_deep=[sems(48), sems(48)],
        s_near=[sems(8), sems(8)],
        s_second=[sems(9), sems(9)],
        s_all=sems(32),
        s_cfd=[sems(4) for _ in range(5)],
    )


def kernel(*refs):
    (source_in, depth_in, start_in, velocity_in, fraction_in, pressure_in, neighbour_in, slot_in, normal_in,
     weight_in, step_in, height_in, blend_in, corner_in, stencil_in, receive_in,
     potential_out, velocity_out, fraction_out, pressure_out) = refs[:20]
    plan = scratch_plan()
    r = SimpleNamespace(**jax.tree_util.tree_unflatten(jax.tree_util.tree_structure(plan), refs[20:]))
    levels = [None] + [
        SimpleNamespace(R=rows, **fields) for rows, fields in zip((24, 16, 32, 16), r.levels)
    ]
    x, y = lax.axis_index("px"), lax.axis_index("py")

    def at(dx, dy):
        return (lax.rem(x + dx + NPX, NPX), lax.rem(y + dy + NPY, NPY))

    def send(source, target, semaphores, slot, where):
        copy = pltpu.make_async_remote_copy(
            src_ref=source,
            dst_ref=target,
            send_sem=semaphores[0].at[slot],
            recv_sem=semaphores[1].at[slot],
            device_id=where,
            device_id_type=MESH,
        )
        copy.start()
        return copy

    sent = []

    barrier = pltpu.get_barrier_semaphore()
    partners = [(dx, 0) for dx in range(1, NPX)]
    partners += [(dx, dy) for dx in range(-REACH, REACH + 1) for dy in (-1, 1)]
    for dx, dy in partners:
        pl.semaphore_signal(barrier, inc=1, device_id=at(dx, dy), device_id_type=MESH)

    middle = pl.ds(PAD + 16, 16)
    moves = [(velocity_in.at[pl.ds(c * ROWS, ROWS), :], r.TQ.at[pl.ds(c * EXT, ROWS), :]) for c in range(3)]
    moves += [
        (fraction_in, r.TQ.at[pl.ds(3 * EXT, ROWS), :]),
        (slot_in, r.slot),
        (start_in, r.V[0].at[pl.ds(1, NZ), middle, :]),
        (source_in, r.B[0].at[:, pl.ds(16, 16), :]),
        (depth_in, r.E[0].at[pl.ds(16, 16), :]),
        (receive_in, r.receive),
        (neighbour_in, r.neighbour),
        (normal_in, r.normal),
        (step_in, r.step),
        (pressure_in, r.TS.at[pl.ds(3 * EXT, ROWS), :]),
        (weight_in, r.weight),
        (corner_in, r.corner),
        (stencil_in, r.stencil),
        (height_in, r.height),
        (blend_in, r.blend),
    ]
    loads = [pltpu.make_async_copy(a, b, r.load.at[i]) for i, (a, b) in enumerate(moves)]
    for load in loads:
        load.start()

    def loaded(first, last):
        for load in loads[first:last]:
            load.wait()

    for rows, refs_of in [(48, r.V + r.U)] + [(level.R, [level.V, level.U]) for level in levels[1:]]:
        for ref in refs_of:
            ref[0] = jnp.zeros((rows + 2 * PAD, 128), F32)
            ref[NZ + 1] = jnp.zeros((rows + 2 * PAD, 128), F32)
            ref[1 : NZ + 1, 0:PAD, :] = jnp.zeros((NZ, PAD, 128), F32)
            ref[1 : NZ + 1, PAD + rows : 2 * PAD + rows, :] = jnp.zeros((NZ, PAD, 128), F32)
    for cycle in range(2):
        for d in (0, 1, 15):
            r.G[cycle][d] = jnp.zeros((3, 3, 2, 128), F32)

    loaded(0, 5)
    r.SI[...] = jnp.zeros((8, 128), I32)
    for b in range(4):
        r.SI[b : b + 1, :] = r.slot[b, 0, :, 0:128]
        r.SI[4 + b : 5 + b, 0:64] = r.slot[b, 0, :, 128:192]
    send_hi, send_lo = r.SI[...] >> 7, r.SI[...] & 127

    def reader(table):
        return lambda c, j: table[c * EXT + j : c * EXT + j + 1, :]

    def cfd_send(i, table):
        values = table_gather(reader(table), ROWS, CHANNELS[i], send_hi, send_lo)
        for c in range(CHANNELS[i]):
            r.CS[i][c] = values[c]

    def cfd_start(i):
        copies = []
        for slot, (dx, dy) in enumerate(((1, 0), (-1, 0), (0, 1), (0, -1))):
            copies.append(send(r.CS[i], r.CR[i].at[slot], r.s_cfd[i], slot, at(dx, dy)))
        return copies

    there = (x > 0, x < NPX - 1, y > 0, y < NPY - 1)
    block = (1, 0, 3, 2)

    def cfd_wait(i, table, copies):
        for copy in copies:
            copy.wait_recv()
        sent.extend(copies)
        for c in range(CHANNELS[i]):
            for b in range(4):
                for h in range(2):
                    row = r.CR[i][b, c, block[b] + 4 * h : block[b] + 4 * h + 1, :]
                    place = c * EXT + ROWS + 2 * b + h
                    table[place : place + 1, :] = jnp.where(there[b], row, 0.0)

    cfd_send(0, r.TQ)

    loaded(5, 8)
    lane16 = lane_iota(16)
    groups_f = [jnp.zeros((16, 128), F32) for _ in range(5)]
    groups_l = [jnp.zeros((16, 128), F32) for _ in range(5)]
    for t in range(2 * NZ + 1):
        if t < NZ:
            tile = r.V[0][t + 1, PAD + 16 : PAD + 32, :]
        elif t < 2 * NZ:
            tile = r.B[0][t - NZ, 16:32, :]
        else:
            tile = r.E[0][16:32, :]
        g, q = t // 8, t % 8
        own = (lane16 >= 16 * q) & (lane16 < 16 * q + 16)
        groups_f[g] = jnp.where(own, roll(tile, 16 * q, 1), groups_f[g])
        groups_l[g] = jnp.where(own, roll(tile, 16 * q + 16, 1), groups_l[g])
    for g in range(5):
        r.first[g] = groups_f[g]
        r.final[g] = groups_l[g]

    pl.semaphore_wait(barrier, len(partners))

    copies0 = cfd_start(0)
    strips = []
    for s, (dx, row) in enumerate(((1, 0), (-1, 32))):
        strips.append(send(depth_in, r.E[0].at[pl.ds(row, 16), :], r.s_tile, 4 + s, at(dx, 0)))
    for dx in (-1, 0, 1):
        slot = 2 * (1 - dx)
        strips.append(send(r.final, r.strips.at[slot], r.s_strip, slot, at(dx, 1)))
        strips.append(send(r.first, r.strips.at[slot + 1], r.s_strip, slot + 1, at(dx, -1)))
    tiles = []
    for s, (dx, row) in enumerate(((1, 0), (-1, 32))):
        padded = pl.ds(PAD + row, 16)
        rows = pl.ds(row, 16)
        tiles.append(send(start_in, r.V[0].at[pl.ds(1, NZ), padded, :], r.s_tile, 2 * s, at(dx, 0)))
        tiles.append(send(source_in, r.B[0].at[:, rows, :], r.s_tile, 2 * s + 1, at(dx, 0)))

    loaded(8, 10)
    cells = r.receive[...]
    hi_of, lo_of = cells >> 7, cells & 127
    inverse = jnp.zeros((2 * ROWS, 128), F32)
    for chunk in range(4):
        lefts, rights = [], []
        for o in range(8 * chunk, 8 * chunk + 8):
            match = row_iota(ROWS) == jnp.broadcast_to(hi_of[o : o + 1, :], (ROWS, 128))
            lanes = lane_iota(ROWS).astype(F32)
            lefts.append(
                jnp.concatenate([jnp.where(match, F32(o + 1), 0.0), jnp.where(match, lanes, 0.0)], axis=0)
            )
            low = row_iota(128) == jnp.broadcast_to(lo_of[o : o + 1, :], (128, 128))
            rights.append(jnp.where(low, F32(1.0), 0.0))
        left = jnp.concatenate(lefts, axis=1).astype(jnp.bfloat16)
        right = jnp.concatenate(rights, axis=1).astype(jnp.bfloat16)
        inverse = inverse + lax.dot_general(
            left, right, (((1,), (1,)), ((), ())), preferred_element_type=F32
        )
    r.INV[...] = inverse.astype(I32)

    index = r.neighbour[...]
    for edge in (4288, 4480, 4672, 4864):
        index = index + jnp.where(r.neighbour[...] >= edge, 64, 0)
    r.HI[...] = index >> 7
    r.LO[...] = index & 127

    cfd_wait(0, r.TQ, copies0)
    loaded(10, 13)

    def part(f, quarter):
        return pl.ds(pl.multiple_of(f * ROWS + 8 * quarter, 8), 8)

    def cells_of(base, quarter):
        return pl.ds(pl.multiple_of(base + 8 * quarter, 8), 8)

    def beside_of(table, components, f, quarter):
        rows = part(f, quarter)
        return table_gather(reader(table), EXT, components, r.HI[rows, :], r.LO[rows, :])

    def normal_of(c, f, quarter):
        return r.normal[part(c * FACES + f, quarter), :]

    zero = jnp.zeros((8, 128), F32)

    @pl.loop(0, 4)
    def _(quarter):
        mine = [r.TQ[cells_of(c * EXT, quarter), :] for c in range(4)]

        def face(f, totals):
            beside = beside_of(r.TQ, 4, f, quarter)
            flux = normal_of(0, f, quarter) * (mine[0] + beside[0])
            for c in (1, 2):
                flux = flux + normal_of(c, f, quarter) * (mine[c] + beside[c])
            flux = 0.5 * flux
            out, into = jnp.maximum(flux, 0.0), jnp.minimum(flux, 0.0)
            return tuple(totals[c] + (out * mine[c] + into * beside[c]) for c in range(4))

        totals = lax.fori_loop(0, FACES, face, (zero,) * 4)
        scale = r.step[cells_of(0, quarter), :]
        for c in range(3):
            r.TS[cells_of(c * EXT, quarter), :] = mine[c] - scale * totals[c]
        r.FRAC[cells_of(0, quarter), :] = mine[3] - scale * totals[3]

    cfd_send(1, r.TS)
    copies1 = cfd_start(1)

    for copy in strips:
        copy.wait_recv()
    sent.extend(strips)
    for block_row in range(3):
        rows = slice(16 * block_row, 16 * block_row + 16)
        padded = slice(PAD + 16 * block_row, PAD + 16 * block_row + 16)
        for t in range(2 * NZ + 1):
            g, q = t // 8, t % 8
            lower = r.strips[2 * block_row, g]
            upper = r.strips[2 * block_row + 1, g]
            value = jnp.where(
                lane16 < 16,
                roll(upper, -16 * q, 1),
                jnp.where(lane16 >= 112, roll(lower, 112 - 16 * q, 1), 0.0),
            )
            if t < NZ:
                r.V[1][t + 1, padded, :] = value
            elif t < 2 * NZ:
                r.B[1][t - NZ, rows, :] = value
            else:
                r.E[1][rows, :] = value

    fine_rows = row_iota(48) + 16 * (x - 1)
    inside_a = (fine_rows >= 0) & (fine_rows < 16 * NPX)
    side_ok = jnp.where(lane_iota(48) < 64, jnp.where(y < NPY - 1, 1, 0), jnp.where(y > 0, 1, 0)) > 0
    insides = [inside_a, inside_a & side_ok]
    data = slice(PAD, PAD + 48)

    def mask_start(k):
        for s in range(2):
            r.V[s][k + 1, data, :] = jnp.where(insides[s], r.V[s][k + 1, data, :], 0.0)

    depths = [jnp.where(insides[s], r.E[s][...], 0.0) for s in range(2)]
    lane48 = lane_iota(48)
    for s in range(2):
        depth, other = depths[s], depths[1 - s]
        r.E[s][...] = depth
        right = jnp.where(lane48 == 127, roll(other, 127, 1), roll(depth, 127, 1))
        left = jnp.where(lane48 == 0, roll(other, 1, 1), roll(depth, 1, 1))
        faces = (
            0.5 * (depth + roll(depth, 47, 0)),
            0.5 * (depth + roll(depth, 1, 0)),
            0.5 * (depth + right),
            0.5 * (depth + left),
        )
        total = faces[0] + faces[1] + faces[2] + faces[3]
        for i, face in enumerate(faces):
            r.C[s][i] = face
        for i, extra in enumerate((VERT, 2 * VERT)):
            r.D[s][i] = total + extra
            r.W[s][i] = jnp.where(insides[s], RELAX / (total + extra), 0.0)

    def fine_sweep(source, target, lo=0, hi=48, halves=(0, 1)):
        fine_operate(r, source, target, False, lo, hi, halves)

    lane24 = lane_iota(24)
    down24 = (2 * lane24) & 127

    def fine_pair(a_even, a_odd, b_even, b_odd):
        mean_a = lane_gather(pair_mean_rows(a_even, a_odd), down24)
        mean_b = lane_gather(pair_mean_rows(b_even, b_odd), down24)
        return jnp.where(lane24 < 64, mean_a, mean_b)

    even24, odd24 = pl.ds(0, 24, stride=2), pl.ds(1, 24, stride=2)
    even_pad, odd_pad = pl.ds(PAD, 24, stride=2), pl.ds(PAD + 1, 24, stride=2)
    inside_1 = inside_of(x, y, 24, 8 * (x - 1), 96, 64, 8 * NPX, 64 * NPY)
    r.M1[...] = jnp.where(inside_1, F32(1.0), 0.0)
    depth_1 = fine_pair(r.E[0][even24, :], r.E[0][odd24, :], r.E[1][even24, :], r.E[1][odd24, :])
    depth_1 = jnp.where(inside_1, depth_1, 0.0)
    levels[1].E[...] = depth_1
    set_coefficients(levels[1], depth_1, inside_1, 0.25)

    def fine_coarsen(k):
        levels[1].B[k] = fine_pair(
            r.U[0][k + 1, even_pad, :], r.U[0][k + 1, odd_pad, :],
            r.U[1][k + 1, even_pad, :], r.U[1][k + 1, odd_pad, :],
        )

    lane8 = lane_iota(8)

    lane4 = lane_iota(4)

    def pack_second(cycle):
        count = NZ + 1 if cycle == 0 else NZ
        even, odd = pl.ds(8, 4, stride=2), pl.ds(9, 4, stride=2)
        for g in range(5):
            packed = jnp.zeros((4, 128), F32)
            for q in range(4):
                k = 4 * g + q
                if k >= count:
                    continue
                if k < NZ:
                    mean = pair_mean_rows(levels[1].T[k, even, :], levels[1].T[k, odd, :])
                else:
                    mean = pair_mean_rows(levels[1].E[even, :], levels[1].E[odd, :])
                own = (lane4 >= 32 * q) & (lane4 < 32 * q + 32)
                packed = jnp.where(own, lane_gather(mean, (2 * lane4 + 64 * (q % 2)) & 127), packed)
            r.P[cycle][g] = packed
            r.N[cycle][1, 1, g] = packed

    def start_second(cycle):
        copies = []
        for dx in (-1, 0, 1):
            for dy in (-1, 0, 1):
                if dx or dy:
                    d, j = 1 - dx, 1 - dy
                    copies.append(send(r.P[cycle], r.N[cycle].at[d, j], r.s_second[cycle], 3 * d + j, at(dx, dy)))
        return copies

    def unpack_second(cycle):
        got = r.N[cycle]
        for m, pair in enumerate(((0, 1), (2, 2))):
            rows = slice(8 * m, 8 * m + 8)
            for g in range(5):
                tiles_of = [jnp.concatenate([got[d, j, g] for d in pair], axis=0) for j in range(3)]
                for q in range(4):
                    k = 4 * g + q
                    if k > NZ or (k == NZ and cycle > 0):
                        continue
                    value = jnp.where(
                        lane8 < 32,
                        roll(tiles_of[1], -32 * q, 1),
                        jnp.where(
                            lane8 < 64,
                            roll(tiles_of[2], 32 - 32 * q, 1),
                            roll(tiles_of[0], 96 - 32 * q, 1),
                        ),
                    )
                    if k < NZ:
                        levels[2].B[k, rows, :] = value
                    else:
                        levels[2].E[rows, :] = value

    lane2 = lane_iota(2)

    def pack_deep(cycle):
        count = NZ + 1 if cycle == 0 else NZ
        even, odd = pl.ds(4, 2, stride=2), pl.ds(5, 2, stride=2)
        for g in range(3):
            packed = jnp.zeros((2, 128), F32)
            for q in range(8):
                k = 8 * g + q
                if k >= count:
                    continue
                if k < NZ:
                    mean = pair_mean_rows(levels[2].T[k, even, :], levels[2].T[k, odd, :])
                else:
                    mean = pair_mean_rows(levels[2].E[even, :], levels[2].E[odd, :])
                own = (lane2 >= 16 * q) & (lane2 < 16 * q + 16)
                packed = jnp.where(own, lane_gather(mean, (2 * lane2 + 96 * q) & 127), packed)
            r.P3[cycle][g] = packed
            r.G[cycle][8, 1, g] = packed

    def start_deep(cycle):
        copies = []
        for dx in range(-REACH, REACH + 1):
            for dy in (-1, 0, 1):
                if dx == 0 and dy == 0:
                    continue
                d, j = 8 - dx, 1 - dy
                copies.append(send(r.P3[cycle], r.G[cycle].at[d, j], r.s_deep[cycle], 3 * d + j, at(dx, dy)))
        return copies

    def unpack_deep(cycle):
        grid_of = r.G[cycle]

        @pl.loop(0, 4)
        def _(m):
            rows = pl.ds(pl.multiple_of(8 * m, 8), 8)
            for g in range(3):
                tiles_of = [
                    jnp.concatenate([grid_of[4 * m + i, j, g] for i in range(4)], axis=0) for j in range(3)
                ]
                for q in range(8):
                    k = 8 * g + q
                    if k > NZ or (k == NZ and cycle > 0):
                        continue
                    value = jnp.where(
                        lane8 < 16,
                        roll(tiles_of[1], -16 * q, 1),
                        jnp.where(
                            lane8 < 64,
                            roll(tiles_of[2], 16 - 16 * q, 1),
                            roll(tiles_of[0], 112 - 16 * q, 1),
                        ),
                    )
                    if k < NZ:
                        levels[3].B[k, rows, :] = value
                    else:
                        levels[3].E[rows, :] = value

    def deep_coefficients(level):
        here = levels[level]
        rows = here.R
        first, tile, width = {2: (-1, 4, 32), 3: (-8, 2, 16), 4: (-8, 1, 8)}[level]
        inside = inside_of(x, y, rows, tile * (x + first), 64, width, tile * NPX, width * NPY)
        if level > 3:
            above = levels[level - 1].E
            mean = pair_mean_rows(above[pl.ds(0, rows, stride=2), :], above[pl.ds(1, rows, stride=2), :])
            depth = lane_gather(mean, (2 * lane_iota(rows)) & 127)
        else:
            depth = here.E[...]
        depth = jnp.where(inside, depth, 0.0)
        here.E[...] = depth
        set_coefficients(here, depth, inside, 0.25**level)

    def descend(here, lo, hi):
        point_step(here)
        sweep_step(here, here.V, here.U)
        operate(here, here.U, here.T, True, lo, hi)

    def solve_deep():
        descend(levels[3], 0, 32)
        coarsen_step(levels[3], levels[4])
        last = levels[4]
        point_step(last)
        sweep_step(last, last.V, last.U)
        sweep_step(last, last.U, last.V)
        sweep_step(last, last.V, last.U)
        for level, first, split, before, after in (
            (3, 0, 64, (8, 24), (8, 24)), (2, 14, 64, (0, 16), (0, 16)), (1, 0, 96, (0, 24), (8, 16)),
        ):
            here = levels[level]
            refine_add(levels[level + 1].U, first, here, here.U, split)
            sweep_step(here, here.U, here.V, *before)
            sweep_step(here, here.V, here.U, *after)

    def down(lo, hi):
        fine_operate(r, r.V, r.U, True, lo, hi)
        each_layer(fine_coarsen)
        descend(levels[1], 8, 16)

    def start_near(cycle):
        own = slice(PAD + 8, PAD + 16)
        values = [levels[1].U[k + 1, own, :] for k in range(NZ)]
        for pair in range(9):
            value = values[2 * pair]
            if 2 * pair + 1 < NZ:
                value = jnp.where(lane8 < 64, value, roll(values[2 * pair + 1], 64, 1))
            r.mine[cycle][pair] = value
        for g in range(2):
            left, right = jnp.zeros((8, 128), F32), jnp.zeros((8, 128), F32)
            for q in range(16):
                if 16 * g + q < NZ:
                    columns = (lane8 >= 8 * q) & (lane8 < 8 * q + 8)
                    left = jnp.where(columns, roll(values[16 * g + q], 8 * q, 1), left)
                    right = jnp.where(columns, roll(values[16 * g + q], 8 * q - 56, 1), right)
            r.left[cycle][g] = left
            r.right[cycle][g] = right
        copies = []
        for s, dx in enumerate((1, -1)):
            copies.append(send(r.mine[cycle], r.near[cycle].at[s], r.s_near[cycle], s, at(dx, 0)))
        for dx in (-1, 0, 1):
            slot = 2 * (1 - dx)
            copies.append(send(r.right[cycle], r.sides[cycle].at[slot], r.s_near[cycle], 2 + slot, at(dx, 1)))
            copies.append(send(r.left[cycle], r.sides[cycle].at[slot + 1], r.s_near[cycle], 3 + slot, at(dx, -1)))
        return copies

    def add_near(cycle, lo=0, hi=24):
        half_lane = lane_iota(hi - lo) >> 1
        even, odd_rows = pl.ds(PAD + 2 * lo, hi - lo, stride=2), pl.ds(PAD + 2 * lo + 1, hi - lo, stride=2)
        fine = slice(PAD + 2 * lo, PAD + 2 * hi)
        for k in range(NZ):
            pair, odd, g, q = k // 2, k % 2, k // 16, k % 16
            for block_row in range(3):
                middle = r.mine[cycle][pair] if block_row == 1 else r.near[cycle][block_row // 2, pair]
                lower, upper = r.sides[cycle][2 * block_row, g], r.sides[cycle][2 * block_row + 1, g]
                aside = jnp.where(lane8 < 96, roll(upper, 64 - 8 * q, 1), roll(lower, 120 - 8 * q, 1))
                value = jnp.where(lane8 < 64, roll(middle, 64 * odd, 1), aside)
                levels[1].T[k, 8 * block_row : 8 * block_row + 8, :] = value

        def body(k):
            value = levels[1].T[k, lo:hi, :] * r.M1[lo:hi, :]
            for s, lanes in ((0, half_lane), (1, half_lane + 64)):
                spread = lane_gather(value, lanes)
                r.U[s][k + 1, even, :] = spread
                r.U[s][k + 1, odd_rows, :] = spread
                r.V[s][k + 1, fine, :] = r.V[s][k + 1, fine, :] + r.U[s][k + 1, fine, :]

        each_layer(body)

    for copy in tiles:
        copy.wait_recv()
    sent.extend(tiles)
    each_layer(mask_start)
    fine_sweep(r.V, r.U)
    fine_sweep(r.U, r.V)
    down(8, 40)
    pack_second(0)
    second0 = start_second(0)

    cfd_wait(1, r.TS, copies1)
    loaded(13, 14)

    def divergence(quarter):
        mine = [r.TS[cells_of(c * EXT, quarter), :] for c in range(3)]

        def face(f, carry):
            flow, pull, weights = carry
            beside = beside_of(r.TS, 4, f, quarter)
            for c in range(3):
                flow = flow + normal_of(c, f, quarter) * (mine[c] + beside[c])
            weight = r.weight[part(f, quarter), :]
            return flow, pull + weight * beside[3], weights + weight

        flow, pull, weights = lax.fori_loop(0, FACES, face, (zero,) * 3)
        here = cells_of(0, quarter)
        flow, inverse_sum = 0.5 * flow, 1.0 / weights
        r.DIV[here, :] = flow
        r.IWS[here, :] = inverse_sum
        r.TP[0][here, :] = (pull - flow) * inverse_sum

    def descend_second(cycle, copies):
        for copy in copies:
            copy.wait_recv()
        sent.extend(copies)
        unpack_second(cycle)
        if cycle == 0:
            deep_coefficients(2)
        descend(levels[2], 0, 8)
        pack_deep(cycle)
        return start_deep(cycle)

    pl.loop(0, 2)(divergence)
    deep0 = descend_second(0, second0)
    pl.loop(2, 4)(divergence)
    cfd_send(2, r.TP[0])
    copies2 = cfd_start(2)

    for copy in deep0:
        copy.wait_recv()
    sent.extend(deep0)
    unpack_deep(0)
    deep_coefficients(3)
    deep_coefficients(4)
    solve_deep()
    near0 = start_near(0)

    def pressure_sweep(before, after):
        @pl.loop(0, 4)
        def _(quarter):
            pull = zero
            for f in range(FACES):
                pull = pull + r.weight[part(f, quarter), :] * beside_of(before, 1, f, quarter)[0]
            here = cells_of(0, quarter)
            after[here, :] = (pull - r.DIV[here, :]) * r.IWS[here, :]

    cfd_wait(2, r.TP[0], copies2)
    pressure_sweep(r.TP[0], r.TP[1])
    cfd_send(3, r.TP[1])
    copies3 = cfd_start(3)

    for copy in near0:
        copy.wait_recv()
    sent.extend(near0)
    add_near(0)
    fine_sweep(r.V, r.U)
    fine_sweep(r.U, r.V)
    fine_sweep(r.V, r.U, 8, 40)
    fine_sweep(r.U, r.V, 8, 40)
    down(8, 40)
    pack_second(1)
    second1 = start_second(1)

    cfd_wait(3, r.TP[1], copies3)
    pressure_sweep(r.TP[1], r.TP[2])
    cfd_send(4, r.TP[2])
    copies4 = cfd_start(4)
    pressure_copy = pltpu.make_async_copy(r.TP[2].at[pl.ds(0, ROWS), :], pressure_out, r.load.at[18])
    pressure_copy.start()
    deep1 = descend_second(1, second1)

    for copy in deep1:
        copy.wait_recv()
    sent.extend(deep1)
    unpack_deep(1)
    solve_deep()
    near1 = start_near(1)

    cfd_wait(4, r.TP[2], copies4)

    @pl.loop(0, 4)
    def _(quarter):
        here = cells_of(0, quarter)
        pressure = r.TP[2][here, :]
        totals = [zero] * 3
        for f in range(FACES):
            difference = beside_of(r.TP[2], 1, f, quarter)[0] - pressure
            totals = [totals[c] + normal_of(c, f, quarter) * difference for c in range(3)]
        for c in range(3):
            r.COR[cells_of(c * ROWS, quarter), :] = r.TS[cells_of(c * EXT, quarter), :] - r.step[here, :] * (
                0.5 * totals[c]
            )

    for copy in near1:
        copy.wait_recv()
    sent.extend(near1)
    add_near(1, 4, 20)
    fine_sweep(r.V, r.U, 8, 40)
    fine_sweep(r.U, r.V, 16, 32, (0,))

    loaded(14, 18)

    own_rows = pl.ds(pl.multiple_of(x * 8, 8), 8)

    def interpolate(quarter):
        corner = r.corner[cells_of(0, quarter), :]
        column = corner & 127
        point_row = (corner >> 7) & 15
        point_layer = corner >> 11

        def layer(k, picks):
            found = []
            for lanes in (column, column + 1):
                low, high = zero, zero
                before = None
                for i in range(16):
                    row = jnp.broadcast_to(r.V[0][k + 1, PAD + 16 + i : PAD + 17 + i, :], (8, 128))
                    value = lane_gather(row, lanes)
                    here = point_row == i
                    if i < 15:
                        low = jnp.where(here, value, low)
                    if before is not None:
                        high = jnp.where(before, value, high)
                    before = here
                found.append((low, high))
            found = (found[0][0], found[1][0], found[0][1], found[1][1])
            lower, upper = point_layer == k, point_layer == k - 1
            return tuple(jnp.where(lower, found[i], picks[i]) for i in range(4)) + tuple(
                jnp.where(upper, found[i], picks[4 + i]) for i in range(4)
            )

        picks = (zero,) * 8
        for k in range(NZ):
            picks = layer(k, picks)
        for quantity in range(4):
            total = zero
            for p in range(8):
                total = total + r.stencil[cells_of((quantity * 8 + p) * ROWS, quarter), :] * picks[p]
            for i in range(8):
                r.S[pl.ds(64 * quarter + 8 * i + quantity, 1), :] = total[i : i + 1, :]

    potential_copy = pltpu.make_async_copy(r.V[0].at[pl.ds(1, NZ), middle, :], potential_out, r.load.at[19])
    potential_copy.start()

    everyone = []
    for away in (2, 1, 3, 0):
        quarter = lax.rem(x // 8 + away, 4)
        interpolate(quarter)
        for i in range(0 if away else 1, 8):
            there_x = quarter * 8 + (i if away else lax.rem(x + i, 8))
            rows = pl.ds(pl.multiple_of(there_x * 8, 8), 8)
            slot = lax.rem(there_x - x + NPX, NPX)
            everyone.append(send(r.S.at[rows, :], r.RB.at[own_rows, :], r.s_all, slot, (there_x, y)))
    r.RB[own_rows, :] = r.S[own_rows, :]
    for o in range(1, NPX):
        pltpu.make_async_remote_copy(
            src_ref=r.S.at[0:8, :],
            dst_ref=r.RB.at[0:8, :],
            send_sem=r.s_all[0].at[o],
            recv_sem=r.s_all[1].at[o],
            device_id=at(o, 0),
            device_id_type=MESH,
        ).wait_recv()
    sent.extend(everyone)

    @pl.loop(0, 4)
    def _(quarter):
        here = cells_of(0, quarter)
        slot_hi, slot_lo = r.INV[here, :] - 1, r.INV[cells_of(ROWS, quarter), :]
        targets = table_gather(lambda c, j: r.RB[8 * j + c : 8 * j + c + 1, :], NPX, 4, slot_hi, slot_lo)
        strength = jnp.where(slot_hi >= 0, r.blend[here, :], 0.0)
        for c in range(3):
            velocity = r.COR[cells_of(c * ROWS, quarter), :]
            velocity_out[cells_of(c * ROWS, quarter), :] = velocity - strength * (velocity - targets[c])
        level_target = jax.nn.sigmoid(4.0 * (targets[3] - r.height[here, :]))
        fraction = r.FRAC[here, :]
        fraction_out[here, :] = fraction - strength * (fraction - level_target)

    pressure_copy.wait()
    potential_copy.wait()
    for copy in sent:
        copy.wait_send()


def hand_over(*refs):
    given, results, held, arrive, leave = refs[0:4], refs[4:8], refs[8:12], refs[12], refs[13]
    ins = [pltpu.make_async_copy(given[i], held[i], arrive.at[i]) for i in range(4)]
    outs = [pltpu.make_async_copy(held[i], results[i], leave.at[i]) for i in range(4)]
    for copy in ins:
        copy.start()
    for i in range(4):
        ins[i].wait()
        outs[i].start()
    for copy in outs:
        copy.wait()


def on_device(
    source, water_depth, potential_start, velocity, fraction, pressure, neighbour, send_slot,
    face_normal, face_weight, step_scale, height, blend_weight, corner, stencil_weight, receive_cell,
):
    def lanes(array):
        return array.reshape(-1, 128)

    args = (
        source, water_depth, potential_start, lanes(velocity), lanes(fraction), lanes(pressure), lanes(neighbour),
        send_slot, lanes(face_normal), lanes(face_weight), lanes(step_scale), lanes(height),
        lanes(blend_weight), lanes(corner), lanes(stencil_weight), lanes(receive_cell),
    )
    shapes = ((NZ, 16, 128), (3 * ROWS, 128), (ROWS, 128), (ROWS, 128))
    results = pl.pallas_call(
        kernel,
        name="step",
        out_shape=[jax.ShapeDtypeStruct(shape, F32) for shape in shapes],
        in_specs=[pl.BlockSpec(memory_space=pltpu.HBM)] * len(args),
        out_specs=[pl.BlockSpec(memory_space=space) for space in (pltpu.HBM, pltpu.VMEM, pltpu.VMEM, pltpu.HBM)],
        scratch_shapes=jax.tree_util.tree_leaves(scratch_plan()),
        compiler_params=pltpu.CompilerParams(
            collective_id=0, has_side_effects=True, vmem_limit_bytes=67043328
        ),
    )(*args)
    dma = pltpu.SemaphoreType.DMA
    results = pl.pallas_call(
        hand_over,
        name="hand_over",
        out_shape=[jax.ShapeDtypeStruct(shape, F32) for shape in shapes],
        in_specs=[pl.BlockSpec(memory_space=pltpu.HBM)] * len(shapes),
        out_specs=[pl.BlockSpec(memory_space=pltpu.HBM)] * len(shapes),
        scratch_shapes=[pltpu.VMEM(shape, F32) for shape in shapes] + [dma((4,)), dma((4,))],
        compiler_params=pltpu.CompilerParams(vmem_limit_bytes=67043328),
    )(*results)
    potential, velocity_out, fraction_out, pressure_out = results
    return (
        potential,
        velocity_out.reshape(3, 1, 1, -1),
        fraction_out.reshape(1, 1, -1),
        pressure_out.reshape(1, 1, -1),
    )


def solution(mesh):
    in_specs = (
        P(None, "px", "py"),
        P("px", "py"),
        P(None, "px", "py"),
        P(None, "px", "py", None),
        P("px", "py", None),
        P("px", "py", None),
        P(None, "px", "py", None),
        P(None, "px", "py", None),
        P(None, None, "px", "py", None),
        P(None, "px", "py", None),
        P("px", "py", None),
        P("px", "py", None),
        P("px", "py", None),
        P("px", "py", None),
        P(None, None, "px", "py", None),
        P("px", "py", None),
    )
    out_specs = (
        P(None, "px", "py"),
        P(None, "px", "py", None),
        P("px", "py", None),
        P("px", "py", None),
    )
    return jax.shard_map(on_device, mesh=mesh, in_specs=in_specs, out_specs=out_specs, check_vma=False)
```

```python
from types import SimpleNamespace

import jax
import jax.numpy as jnp
from jax import lax
from jax.experimental import pallas as pl
from jax.experimental.pallas import tpu as pltpu
from jax.sharding import PartitionSpec as P

F32 = jnp.float32
I32 = jnp.int32
MESH = pl.DeviceIdType.MESH
NPX, NPY = 32, 8
NZ = 17
FACES = 6
ROWS = 32
EXT = 40
PAD = 8
VERT = 0.01
RELAX = 0.8
REACH = 6

GATHER_DIMS = lax.GatherDimensionNumbers(
    offset_dims=(),
    collapsed_slice_dims=(1,),
    start_index_map=(1,),
    operand_batching_dims=(0,),
    start_indices_batching_dims=(0,),
)


def lane_gather(values, lanes):
    return lax.gather(
        values,
        lanes[..., None],
        GATHER_DIMS,
        slice_sizes=(1, 1),
        mode=lax.GatherScatterMode.PROMISE_IN_BOUNDS,
    )


def lane_iota(rows):
    return lax.broadcasted_iota(I32, (rows, 128), 1)


def row_iota(rows):
    return lax.broadcasted_iota(I32, (rows, 128), 0)


def roll(values, shift, axis):
    shift = shift % values.shape[axis]
    return values if shift == 0 else pltpu.roll(values, shift, axis)


def over_layers(body, chunk=4):
    whole = NZ // chunk
    if whole > 1:

        @pl.loop(0, whole)
        def _(step):
            body([step * chunk + j for j in range(chunk)])

    rest = list(range(whole * chunk if whole > 1 else 0, NZ))
    if rest:
        body(rest)


def each_layer(body, chunk=4):
    def bodies(layers):
        for k in layers:
            body(k)

    over_layers(bodies, chunk)


def kind(k):
    return min(k, 1) if isinstance(k, int) else jnp.minimum(k, 1)


def inside_of(x, y, rows, row_first, lane_split, width, height, depth):
    row = row_iota(rows) + row_first
    lane = lane_iota(rows)
    column = jnp.where(lane < lane_split, lane, lane - 128) + y * width
    return (row >= 0) & (row < height) & (column >= 0) & (column < depth)


def set_coefficients(level, depth, inside, scale):
    rows = depth.shape[0]
    half = 0.5 * scale
    faces = (
        half * (depth + roll(depth, rows - 1, 0)),
        half * (depth + roll(depth, 1, 0)),
        half * (depth + roll(depth, 127, 1)),
        half * (depth + roll(depth, 1, 1)),
    )
    total = faces[0] + faces[1] + faces[2] + faces[3]
    for i, face in enumerate(faces):
        level.C[i] = face
    for i, extra in enumerate((VERT, 2 * VERT)):
        diagonal = total + extra
        level.D[i] = diagonal
        level.W[i] = jnp.where(inside, RELAX / diagonal, 0.0)


def point_step(level):
    def body(k):
        level.V[k + 1, PAD : PAD + level.R, :] = level.W[kind(k)] * level.B[k]

    each_layer(body)


def operate(level, source, target, residual, lo, hi):
    def body(layers):
        for start in range(lo, hi, 8):
            rows, mid = slice(start, start + 8), slice(PAD + start, PAD + start + 8)
            up, down = slice(PAD + start + 1, PAD + start + 9), slice(PAD + start - 1, PAD + start + 7)
            faces = [level.C[i, rows, :] for i in range(4)]
            below, values = source[layers[0], mid, :], source[layers[0] + 1, mid, :]
            for k in layers:
                above = source[k + 2, mid, :]
                total = faces[0] * source[k + 1, up, :] + faces[1] * source[k + 1, down, :]
                total = total + (faces[2] * roll(values, 127, 1) + faces[3] * roll(values, 1, 1))
                total = (total + VERT * (below + above)) + level.B[k, rows, :]
                if residual:
                    target[k, rows, :] = total - level.D[kind(k), rows, :] * values
                else:
                    target[k + 1, mid, :] = (1.0 - RELAX) * values + level.W[kind(k), rows, :] * total
                below, values = values, above

    over_layers(body, NZ)


def sweep_step(level, source, target, lo=0, hi=None):
    operate(level, source, target, False, lo, level.R if hi is None else hi)


def pair_mean_rows(even, odd):
    total = even + odd
    return 0.25 * (total + roll(total, 127, 1))


def coarsen_step(fine, coarse):
    half = coarse.R
    lanes = (2 * lane_iota(half)) & 127

    def body(k):
        total = pair_mean_rows(fine.T[k, pl.ds(0, half, stride=2), :], fine.T[k, pl.ds(1, half, stride=2), :])
        coarse.B[k] = lane_gather(total, lanes)

    each_layer(body)


def refine_add(correction, first, fine, target, lane_split):
    rows = fine.R
    half = rows // 2
    lane = lane_iota(half)
    lanes = jnp.where(lane < lane_split, lane >> 1, (lane >> 1) + 64)

    def body(k):
        spread = lane_gather(correction[k + 1, PAD + first : PAD + first + half, :], lanes)
        fine.T[k, pl.ds(0, half, stride=2), :] = spread
        fine.T[k, pl.ds(1, half, stride=2), :] = spread
        target[k + 1, PAD : PAD + rows, :] = target[k + 1, PAD : PAD + rows, :] + fine.T[k]

    each_layer(body)


def fine_operate(top, source, target, residual, lo, hi, halves=(0, 1)):
    lane = lane_iota(8)
    first, last = lane == 0, lane == 127

    def body(layers):
        for start in range(lo, hi, 8):
            rows, mid = slice(start, start + 8), slice(PAD + start, PAD + start + 8)
            up, down = slice(PAD + start + 1, PAD + start + 9), slice(PAD + start - 1, PAD + start + 7)
            faces = [[top.C[s][i, rows, :] for i in range(4)] for s in range(2)]
            below = [source[s][layers[0], mid, :] for s in range(2)]
            values = [source[s][layers[0] + 1, mid, :] for s in range(2)]
            for k in layers:
                above = [source[s][k + 2, mid, :] for s in range(2)]
                rights = [roll(values[s], 127, 1) for s in range(2)]
                lefts = [roll(values[s], 1, 1) for s in range(2)]
                for s in halves:
                    right = jnp.where(last, rights[1 - s], rights[s])
                    left = jnp.where(first, lefts[1 - s], lefts[s])
                    total = faces[s][0] * source[s][k + 1, up, :] + faces[s][1] * source[s][k + 1, down, :]
                    total = total + (faces[s][2] * right + faces[s][3] * left)
                    total = (total + VERT * (below[s] + above[s])) + top.B[s][k, rows, :]
                    if residual:
                        value = total - top.D[s][kind(k), rows, :] * values[s]
                    else:
                        value = (1.0 - RELAX) * values[s] + top.W[s][kind(k), rows, :] * total
                    target[s][k + 1, mid, :] = value
                below, values = values, above

    over_layers(body, NZ)


def table_gather(read_row, count, components, hi, lo):
    picked = [jnp.zeros((8, 128), F32) for _ in range(components)]
    for j in range(count):
        mask = hi == j
        for c in range(components):
            row = jnp.broadcast_to(read_row(c, j), (8, 128))
            picked[c] = jnp.where(mask, lane_gather(row, lo), picked[c])
    return picked


CHANNELS = (4, 4, 1, 1, 1)


def scratch_plan():
    def vmem(*shape, dtype=F32):
        return pltpu.VMEM(shape, dtype)

    def pair(*shape):
        return [vmem(*shape), vmem(*shape)]

    def sems(count):
        return [pltpu.SemaphoreType.DMA((count,)), pltpu.SemaphoreType.DMA((count,))]

    def level(rows):
        return dict(
            V=vmem(NZ + 2, rows + 2 * PAD, 128),
            U=vmem(NZ + 2, rows + 2 * PAD, 128),
            B=vmem(NZ, rows, 128),
            T=vmem(NZ, rows, 128),
            C=vmem(4, rows, 128),
            W=vmem(2, rows, 128),
            D=vmem(2, rows, 128),
            E=vmem(rows, 128),
        )

    return dict(
        V=pair(NZ + 2, 48 + 2 * PAD, 128),
        U=pair(NZ + 2, 48 + 2 * PAD, 128),
        B=pair(NZ, 48, 128),
        C=pair(4, 48, 128),
        W=pair(2, 48, 128),
        D=pair(2, 48, 128),
        E=pair(48, 128),
        levels=[level(24), level(16), level(32), level(16)],
        M1=vmem(24, 128),
        first=vmem(5, 16, 128),
        final=vmem(5, 16, 128),
        strips=vmem(6, 5, 16, 128),
        P=pair(5, 4, 128),
        N=pair(3, 3, 5, 4, 128),
        P3=pair(3, 2, 128),
        G=pair(16, 3, 3, 2, 128),
        near=pair(2, 9, 8, 128),
        sides=pair(6, 2, 8, 128),
        mine=pair(9, 8, 128),
        left=pair(2, 8, 128),
        right=pair(2, 8, 128),
        HI=vmem(FACES * ROWS, 128, dtype=I32),
        LO=vmem(FACES * ROWS, 128, dtype=I32),
        SI=vmem(8, 128, dtype=I32),
        TQ=vmem(4 * EXT, 128),
        TS=vmem(4 * EXT, 128),
        TP=[vmem(EXT, 128) for _ in range(3)],
        CS=[vmem(n, 8, 128) for n in CHANNELS],
        CR=[vmem(4, n, 8, 128) for n in CHANNELS],
        FRAC=vmem(ROWS, 128),
        DIV=vmem(ROWS, 128),
        IWS=vmem(ROWS, 128),
        COR=vmem(3 * ROWS, 128),
        INV=vmem(2 * ROWS, 128, dtype=I32),
        S=vmem(256, 128),
        RB=vmem(256, 128),
        neighbour=vmem(FACES * ROWS, 128, dtype=I32),
        slot=vmem(4, 1, 1, 192, dtype=I32),
        normal=vmem(3 * FACES * ROWS, 128),
        weight=vmem(FACES * ROWS, 128),
        step=vmem(ROWS, 128),
        height=vmem(ROWS, 128),
        blend=vmem(ROWS, 128),
        corner=vmem(ROWS, 128, dtype=I32),
        stencil=vmem(32 * ROWS, 128),
        receive=vmem(ROWS, 128, dtype=I32),
        load=pltpu.SemaphoreType.DMA((20,)),
        s_tile=sems(6),
        s_strip=sems(6),
        s_deep=[sems(48), sems(48)],
        s_near=[sems(8), sems(8)],
        s_second=[sems(9), sems(9)],
        s_all=sems(32),
        s_cfd=[sems(4) for _ in range(5)],
    )


def kernel(*refs):
    (source_in, depth_in, start_in, velocity_in, fraction_in, pressure_in, neighbour_in, slot_in, normal_in,
     weight_in, step_in, height_in, blend_in, corner_in, stencil_in, receive_in,
     potential_out, velocity_out, fraction_out, pressure_out) = refs[:20]
    plan = scratch_plan()
    r = SimpleNamespace(**jax.tree_util.tree_unflatten(jax.tree_util.tree_structure(plan), refs[20:]))
    levels = [None] + [
        SimpleNamespace(R=rows, **fields) for rows, fields in zip((24, 16, 32, 16), r.levels)
    ]
    x, y = lax.axis_index("px"), lax.axis_index("py")

    def at(dx, dy):
        return (lax.rem(x + dx + NPX, NPX), lax.rem(y + dy + NPY, NPY))

    def send(source, target, semaphores, slot, where):
        copy = pltpu.make_async_remote_copy(
            src_ref=source,
            dst_ref=target,
            send_sem=semaphores[0].at[slot],
            recv_sem=semaphores[1].at[slot],
            device_id=where,
            device_id_type=MESH,
        )
        copy.start()
        return copy

    sent = []

    barrier = pltpu.get_barrier_semaphore()
    partners = [(dx, 0) for dx in range(1, NPX)]
    partners += [(dx, dy) for dx in range(-REACH, REACH + 1) for dy in (-1, 1)]
    for dx, dy in partners:
        pl.semaphore_signal(barrier, inc=1, device_id=at(dx, dy), device_id_type=MESH)

    middle = pl.ds(PAD + 16, 16)
    moves = [(velocity_in.at[pl.ds(c * ROWS, ROWS), :], r.TQ.at[pl.ds(c * EXT, ROWS), :]) for c in range(3)]
    moves += [
        (fraction_in, r.TQ.at[pl.ds(3 * EXT, ROWS), :]),
        (slot_in, r.slot),
        (start_in, r.V[0].at[pl.ds(1, NZ), middle, :]),
        (source_in, r.B[0].at[:, pl.ds(16, 16), :]),
        (depth_in, r.E[0].at[pl.ds(16, 16), :]),
        (receive_in, r.receive),
        (neighbour_in, r.neighbour),
        (normal_in, r.normal),
        (step_in, r.step),
        (pressure_in, r.TS.at[pl.ds(3 * EXT, ROWS), :]),
        (weight_in, r.weight),
        (corner_in, r.corner),
        (stencil_in, r.stencil),
        (height_in, r.height),
        (blend_in, r.blend),
    ]
    loads = [pltpu.make_async_copy(a, b, r.load.at[i]) for i, (a, b) in enumerate(moves)]
    for load in loads:
        load.start()

    def loaded(first, last):
        for load in loads[first:last]:
            load.wait()

    for rows, refs_of in [(48, r.V + r.U)] + [(level.R, [level.V, level.U]) for level in levels[1:]]:
        for ref in refs_of:
            ref[0] = jnp.zeros((rows + 2 * PAD, 128), F32)
            ref[NZ + 1] = jnp.zeros((rows + 2 * PAD, 128), F32)
            ref[1 : NZ + 1, 0:PAD, :] = jnp.zeros((NZ, PAD, 128), F32)
            ref[1 : NZ + 1, PAD + rows : 2 * PAD + rows, :] = jnp.zeros((NZ, PAD, 128), F32)
    for cycle in range(2):
        for d in (0, 1, 15):
            r.G[cycle][d] = jnp.zeros((3, 3, 2, 128), F32)

    loaded(0, 5)
    r.SI[...] = jnp.zeros((8, 128), I32)
    for b in range(4):
        r.SI[b : b + 1, :] = r.slot[b, 0, :, 0:128]
        r.SI[4 + b : 5 + b, 0:64] = r.slot[b, 0, :, 128:192]
    send_hi, send_lo = r.SI[...] >> 7, r.SI[...] & 127

    def reader(table):
        return lambda c, j: table[c * EXT + j : c * EXT + j + 1, :]

    def cfd_send(i, table):
        values = table_gather(reader(table), ROWS, CHANNELS[i], send_hi, send_lo)
        for c in range(CHANNELS[i]):
            r.CS[i][c] = values[c]

    def cfd_start(i):
        copies = []
        for slot, (dx, dy) in enumerate(((1, 0), (-1, 0), (0, 1), (0, -1))):
            copies.append(send(r.CS[i], r.CR[i].at[slot], r.s_cfd[i], slot, at(dx, dy)))
        return copies

    there = (x > 0, x < NPX - 1, y > 0, y < NPY - 1)
    block = (1, 0, 3, 2)

    def cfd_wait(i, table, copies):
        for copy in copies:
            copy.wait_recv()
        sent.extend(copies)
        for c in range(CHANNELS[i]):
            for b in range(4):
                for h in range(2):
                    row = r.CR[i][b, c, block[b] + 4 * h : block[b] + 4 * h + 1, :]
                    place = c * EXT + ROWS + 2 * b + h
                    table[place : place + 1, :] = jnp.where(there[b], row, 0.0)

    cfd_send(0, r.TQ)

    loaded(5, 8)
    lane16 = lane_iota(16)
    groups_f = [jnp.zeros((16, 128), F32) for _ in range(5)]
    groups_l = [jnp.zeros((16, 128), F32) for _ in range(5)]
    for t in range(2 * NZ + 1):
        if t < NZ:
            tile = r.V[0][t + 1, PAD + 16 : PAD + 32, :]
        elif t < 2 * NZ:
            tile = r.B[0][t - NZ, 16:32, :]
        else:
            tile = r.E[0][16:32, :]
        g, q = t // 8, t % 8
        own = (lane16 >= 16 * q) & (lane16 < 16 * q + 16)
        groups_f[g] = jnp.where(own, roll(tile, 16 * q, 1), groups_f[g])
        groups_l[g] = jnp.where(own, roll(tile, 16 * q + 16, 1), groups_l[g])
    for g in range(5):
        r.first[g] = groups_f[g]
        r.final[g] = groups_l[g]

    pl.semaphore_wait(barrier, len(partners))

    copies0 = cfd_start(0)
    strips = []
    for s, (dx, row) in enumerate(((1, 0), (-1, 32))):
        strips.append(send(depth_in, r.E[0].at[pl.ds(row, 16), :], r.s_tile, 4 + s, at(dx, 0)))
    for dx in (-1, 0, 1):
        slot = 2 * (1 - dx)
        strips.append(send(r.final, r.strips.at[slot], r.s_strip, slot, at(dx, 1)))
        strips.append(send(r.first, r.strips.at[slot + 1], r.s_strip, slot + 1, at(dx, -1)))
    tiles = []
    for s, (dx, row) in enumerate(((1, 0), (-1, 32))):
        padded = pl.ds(PAD + row, 16)
        rows = pl.ds(row, 16)
        tiles.append(send(start_in, r.V[0].at[pl.ds(1, NZ), padded, :], r.s_tile, 2 * s, at(dx, 0)))
        tiles.append(send(source_in, r.B[0].at[:, rows, :], r.s_tile, 2 * s + 1, at(dx, 0)))

    loaded(8, 10)
    cells = r.receive[...]
    hi_of, lo_of = cells >> 7, cells & 127
    inverse = jnp.zeros((2 * ROWS, 128), F32)
    for chunk in range(4):
        lefts, rights = [], []
        for o in range(8 * chunk, 8 * chunk + 8):
            match = row_iota(ROWS) == jnp.broadcast_to(hi_of[o : o + 1, :], (ROWS, 128))
            lanes = lane_iota(ROWS).astype(F32)
            lefts.append(
                jnp.concatenate([jnp.where(match, F32(o + 1), 0.0), jnp.where(match, lanes, 0.0)], axis=0)
            )
            low = row_iota(128) == jnp.broadcast_to(lo_of[o : o + 1, :], (128, 128))
            rights.append(jnp.where(low, F32(1.0), 0.0))
        left = jnp.concatenate(lefts, axis=1).astype(jnp.bfloat16)
        right = jnp.concatenate(rights, axis=1).astype(jnp.bfloat16)
        inverse = inverse + lax.dot_general(
            left, right, (((1,), (1,)), ((), ())), preferred_element_type=F32
        )
    r.INV[...] = inverse.astype(I32)

    index = r.neighbour[...]
    for edge in (4288, 4480, 4672, 4864):
        index = index + jnp.where(r.neighbour[...] >= edge, 64, 0)
    r.HI[...] = index >> 7
    r.LO[...] = index & 127

    cfd_wait(0, r.TQ, copies0)
    loaded(10, 13)

    def part(f, quarter):
        return pl.ds(pl.multiple_of(f * ROWS + 8 * quarter, 8), 8)

    def cells_of(base, quarter):
        return pl.ds(pl.multiple_of(base + 8 * quarter, 8), 8)

    def beside_of(table, components, f, quarter):
        rows = part(f, quarter)
        return table_gather(reader(table), EXT, components, r.HI[rows, :], r.LO[rows, :])

    def normal_of(c, f, quarter):
        return r.normal[part(c * FACES + f, quarter), :]

    zero = jnp.zeros((8, 128), F32)

    @pl.loop(0, 4)
    def _(quarter):
        mine = [r.TQ[cells_of(c * EXT, quarter), :] for c in range(4)]

        def face(f, totals):
            beside = beside_of(r.TQ, 4, f, quarter)
            flux = normal_of(0, f, quarter) * (mine[0] + beside[0])
            for c in (1, 2):
                flux = flux + normal_of(c, f, quarter) * (mine[c] + beside[c])
            flux = 0.5 * flux
            out, into = jnp.maximum(flux, 0.0), jnp.minimum(flux, 0.0)
            return tuple(totals[c] + (out * mine[c] + into * beside[c]) for c in range(4))

        totals = lax.fori_loop(0, FACES // 2, lambda i, t: face(2 * i + 1, face(2 * i, t)), (zero,) * 4)
        scale = r.step[cells_of(0, quarter), :]
        for c in range(3):
            r.TS[cells_of(c * EXT, quarter), :] = mine[c] - scale * totals[c]
        r.FRAC[cells_of(0, quarter), :] = mine[3] - scale * totals[3]

    cfd_send(1, r.TS)
    copies1 = cfd_start(1)

    for copy in strips:
        copy.wait_recv()
    sent.extend(strips)
    for block_row in range(3):
        rows = slice(16 * block_row, 16 * block_row + 16)
        padded = slice(PAD + 16 * block_row, PAD + 16 * block_row + 16)
        for t in range(2 * NZ + 1):
            g, q = t // 8, t % 8
            lower = r.strips[2 * block_row, g]
            upper = r.strips[2 * block_row + 1, g]
            value = jnp.where(
                lane16 < 16,
                roll(upper, -16 * q, 1),
                jnp.where(lane16 >= 112, roll(lower, 112 - 16 * q, 1), 0.0),
            )
            if t < NZ:
                r.V[1][t + 1, padded, :] = value
            elif t < 2 * NZ:
                r.B[1][t - NZ, rows, :] = value
            else:
                r.E[1][rows, :] = value

    fine_rows = row_iota(48) + 16 * (x - 1)
    inside_a = (fine_rows >= 0) & (fine_rows < 16 * NPX)
    side_ok = jnp.where(lane_iota(48) < 64, jnp.where(y < NPY - 1, 1, 0), jnp.where(y > 0, 1, 0)) > 0
    insides = [inside_a, inside_a & side_ok]
    data = slice(PAD, PAD + 48)

    def mask_start(k):
        for s in range(2):
            r.V[s][k + 1, data, :] = jnp.where(insides[s], r.V[s][k + 1, data, :], 0.0)

    depths = [jnp.where(insides[s], r.E[s][...], 0.0) for s in range(2)]
    lane48 = lane_iota(48)
    for s in range(2):
        depth, other = depths[s], depths[1 - s]
        r.E[s][...] = depth
        right = jnp.where(lane48 == 127, roll(other, 127, 1), roll(depth, 127, 1))
        left = jnp.where(lane48 == 0, roll(other, 1, 1), roll(depth, 1, 1))
        faces = (
            0.5 * (depth + roll(depth, 47, 0)),
            0.5 * (depth + roll(depth, 1, 0)),
            0.5 * (depth + right),
            0.5 * (depth + left),
        )
        total = faces[0] + faces[1] + faces[2] + faces[3]
        for i, face in enumerate(faces):
            r.C[s][i] = face
        for i, extra in enumerate((VERT, 2 * VERT)):
            r.D[s][i] = total + extra
            r.W[s][i] = jnp.where(insides[s], RELAX / (total + extra), 0.0)

    def fine_sweep(source, target, lo=0, hi=48, halves=(0, 1)):
        fine_operate(r, source, target, False, lo, hi, halves)

    lane24 = lane_iota(24)
    down24 = (2 * lane24) & 127

    def fine_pair(a_even, a_odd, b_even, b_odd):
        mean_a = lane_gather(pair_mean_rows(a_even, a_odd), down24)
        mean_b = lane_gather(pair_mean_rows(b_even, b_odd), down24)
        return jnp.where(lane24 < 64, mean_a, mean_b)

    even24, odd24 = pl.ds(0, 24, stride=2), pl.ds(1, 24, stride=2)
    even_pad, odd_pad = pl.ds(PAD, 24, stride=2), pl.ds(PAD + 1, 24, stride=2)
    inside_1 = inside_of(x, y, 24, 8 * (x - 1), 96, 64, 8 * NPX, 64 * NPY)
    r.M1[...] = jnp.where(inside_1, F32(1.0), 0.0)
    depth_1 = fine_pair(r.E[0][even24, :], r.E[0][odd24, :], r.E[1][even24, :], r.E[1][odd24, :])
    depth_1 = jnp.where(inside_1, depth_1, 0.0)
    levels[1].E[...] = depth_1
    set_coefficients(levels[1], depth_1, inside_1, 0.25)

    def fine_coarsen(k):
        levels[1].B[k] = fine_pair(
            r.U[0][k + 1, even_pad, :], r.U[0][k + 1, odd_pad, :],
            r.U[1][k + 1, even_pad, :], r.U[1][k + 1, odd_pad, :],
        )

    lane8 = lane_iota(8)

    lane4 = lane_iota(4)

    def pack_second(cycle):
        count = NZ + 1 if cycle == 0 else NZ
        even, odd = pl.ds(8, 4, stride=2), pl.ds(9, 4, stride=2)
        for g in range(5):
            packed = jnp.zeros((4, 128), F32)
            for q in range(4):
                k = 4 * g + q
                if k >= count:
                    continue
                if k < NZ:
                    mean = pair_mean_rows(levels[1].T[k, even, :], levels[1].T[k, odd, :])
                else:
                    mean = pair_mean_rows(levels[1].E[even, :], levels[1].E[odd, :])
                own = (lane4 >= 32 * q) & (lane4 < 32 * q + 32)
                packed = jnp.where(own, lane_gather(mean, (2 * lane4 + 64 * (q % 2)) & 127), packed)
            r.P[cycle][g] = packed
            r.N[cycle][1, 1, g] = packed

    def start_second(cycle):
        copies = []
        for dx in (-1, 0, 1):
            for dy in (-1, 0, 1):
                if dx or dy:
                    d, j = 1 - dx, 1 - dy
                    copies.append(send(r.P[cycle], r.N[cycle].at[d, j], r.s_second[cycle], 3 * d + j, at(dx, dy)))
        return copies

    def unpack_second(cycle):
        got = r.N[cycle]
        for m, pair in enumerate(((0, 1), (2, 2))):
            rows = slice(8 * m, 8 * m + 8)
            for g in range(5):
                tiles_of = [jnp.concatenate([got[d, j, g] for d in pair], axis=0) for j in range(3)]
                for q in range(4):
                    k = 4 * g + q
                    if k > NZ or (k == NZ and cycle > 0):
                        continue
                    value = jnp.where(
                        lane8 < 32,
                        roll(tiles_of[1], -32 * q, 1),
                        jnp.where(
                            lane8 < 64,
                            roll(tiles_of[2], 32 - 32 * q, 1),
                            roll(tiles_of[0], 96 - 32 * q, 1),
                        ),
                    )
                    if k < NZ:
                        levels[2].B[k, rows, :] = value
                    else:
                        levels[2].E[rows, :] = value

    lane2 = lane_iota(2)

    def pack_deep(cycle):
        count = NZ + 1 if cycle == 0 else NZ
        even, odd = pl.ds(4, 2, stride=2), pl.ds(5, 2, stride=2)
        for g in range(3):
            packed = jnp.zeros((2, 128), F32)
            for q in range(8):
                k = 8 * g + q
                if k >= count:
                    continue
                if k < NZ:
                    mean = pair_mean_rows(levels[2].T[k, even, :], levels[2].T[k, odd, :])
                else:
                    mean = pair_mean_rows(levels[2].E[even, :], levels[2].E[odd, :])
                own = (lane2 >= 16 * q) & (lane2 < 16 * q + 16)
                packed = jnp.where(own, lane_gather(mean, (2 * lane2 + 96 * q) & 127), packed)
            r.P3[cycle][g] = packed
            r.G[cycle][8, 1, g] = packed

    def start_deep(cycle):
        copies = []
        for dx in range(-REACH, REACH + 1):
            for dy in (-1, 0, 1):
                if dx == 0 and dy == 0:
                    continue
                d, j = 8 - dx, 1 - dy
                copies.append(send(r.P3[cycle], r.G[cycle].at[d, j], r.s_deep[cycle], 3 * d + j, at(dx, dy)))
        return copies

    def unpack_deep(cycle):
        grid_of = r.G[cycle]

        @pl.loop(0, 4)
        def _(m):
            rows = pl.ds(pl.multiple_of(8 * m, 8), 8)
            for g in range(3):
                tiles_of = [
                    jnp.concatenate([grid_of[4 * m + i, j, g] for i in range(4)], axis=0) for j in range(3)
                ]
                for q in range(8):
                    k = 8 * g + q
                    if k > NZ or (k == NZ and cycle > 0):
                        continue
                    value = jnp.where(
                        lane8 < 16,
                        roll(tiles_of[1], -16 * q, 1),
                        jnp.where(
                            lane8 < 64,
                            roll(tiles_of[2], 16 - 16 * q, 1),
                            roll(tiles_of[0], 112 - 16 * q, 1),
                        ),
                    )
                    if k < NZ:
                        levels[3].B[k, rows, :] = value
                    else:
                        levels[3].E[rows, :] = value

    def deep_coefficients(level):
        here = levels[level]
        rows = here.R
        first, tile, width = {2: (-1, 4, 32), 3: (-8, 2, 16), 4: (-8, 1, 8)}[level]
        inside = inside_of(x, y, rows, tile * (x + first), 64, width, tile * NPX, width * NPY)
        if level > 3:
            above = levels[level - 1].E
            mean = pair_mean_rows(above[pl.ds(0, rows, stride=2), :], above[pl.ds(1, rows, stride=2), :])
            depth = lane_gather(mean, (2 * lane_iota(rows)) & 127)
        else:
            depth = here.E[...]
        depth = jnp.where(inside, depth, 0.0)
        here.E[...] = depth
        set_coefficients(here, depth, inside, 0.25**level)

    def descend(here, lo, hi):
        point_step(here)
        sweep_step(here, here.V, here.U)
        operate(here, here.U, here.T, True, lo, hi)

    def solve_deep():
        descend(levels[3], 0, 32)
        coarsen_step(levels[3], levels[4])
        last = levels[4]
        point_step(last)
        sweep_step(last, last.V, last.U)
        sweep_step(last, last.U, last.V)
        sweep_step(last, last.V, last.U)
        for level, first, split, before, after in (
            (3, 0, 64, (8, 24), (8, 24)), (2, 14, 64, (0, 16), (0, 16)), (1, 0, 96, (0, 24), (8, 16)),
        ):
            here = levels[level]
            refine_add(levels[level + 1].U, first, here, here.U, split)
            sweep_step(here, here.U, here.V, *before)
            sweep_step(here, here.V, here.U, *after)

    def down(lo, hi):
        fine_operate(r, r.V, r.U, True, lo, hi)
        each_layer(fine_coarsen)
        descend(levels[1], 8, 16)

    def start_near(cycle):
        own = slice(PAD + 8, PAD + 16)
        values = [levels[1].U[k + 1, own, :] for k in range(NZ)]
        for pair in range(9):
            value = values[2 * pair]
            if 2 * pair + 1 < NZ:
                value = jnp.where(lane8 < 64, value, roll(values[2 * pair + 1], 64, 1))
            r.mine[cycle][pair] = value
        for g in range(2):
            left, right = jnp.zeros((8, 128), F32), jnp.zeros((8, 128), F32)
            for q in range(16):
                if 16 * g + q < NZ:
                    columns = (lane8 >= 8 * q) & (lane8 < 8 * q + 8)
                    left = jnp.where(columns, roll(values[16 * g + q], 8 * q, 1), left)
                    right = jnp.where(columns, roll(values[16 * g + q], 8 * q - 56, 1), right)
            r.left[cycle][g] = left
            r.right[cycle][g] = right
        copies = []
        for s, dx in enumerate((1, -1)):
            copies.append(send(r.mine[cycle], r.near[cycle].at[s], r.s_near[cycle], s, at(dx, 0)))
        for dx in (-1, 0, 1):
            slot = 2 * (1 - dx)
            copies.append(send(r.right[cycle], r.sides[cycle].at[slot], r.s_near[cycle], 2 + slot, at(dx, 1)))
            copies.append(send(r.left[cycle], r.sides[cycle].at[slot + 1], r.s_near[cycle], 3 + slot, at(dx, -1)))
        return copies

    def add_near(cycle, lo=0, hi=24):
        half_lane = lane_iota(hi - lo) >> 1
        even, odd_rows = pl.ds(PAD + 2 * lo, hi - lo, stride=2), pl.ds(PAD + 2 * lo + 1, hi - lo, stride=2)
        fine = slice(PAD + 2 * lo, PAD + 2 * hi)
        for k in range(NZ):
            pair, odd, g, q = k // 2, k % 2, k // 16, k % 16
            for block_row in range(3):
                middle = r.mine[cycle][pair] if block_row == 1 else r.near[cycle][block_row // 2, pair]
                lower, upper = r.sides[cycle][2 * block_row, g], r.sides[cycle][2 * block_row + 1, g]
                aside = jnp.where(lane8 < 96, roll(upper, 64 - 8 * q, 1), roll(lower, 120 - 8 * q, 1))
                value = jnp.where(lane8 < 64, roll(middle, 64 * odd, 1), aside)
                levels[1].T[k, 8 * block_row : 8 * block_row + 8, :] = value

        def body(k):
            value = levels[1].T[k, lo:hi, :] * r.M1[lo:hi, :]
            for s, lanes in ((0, half_lane), (1, half_lane + 64)):
                spread = lane_gather(value, lanes)
                r.U[s][k + 1, even, :] = spread
                r.U[s][k + 1, odd_rows, :] = spread
                r.V[s][k + 1, fine, :] = r.V[s][k + 1, fine, :] + r.U[s][k + 1, fine, :]

        each_layer(body)

    for copy in tiles:
        copy.wait_recv()
    sent.extend(tiles)
    each_layer(mask_start)
    fine_sweep(r.V, r.U)
    fine_sweep(r.U, r.V)
    down(8, 40)
    pack_second(0)
    second0 = start_second(0)

    cfd_wait(1, r.TS, copies1)
    loaded(13, 14)

    def divergence(quarter):
        mine = [r.TS[cells_of(c * EXT, quarter), :] for c in range(3)]

        def face(f, carry):
            flow, pull, weights = carry
            beside = beside_of(r.TS, 4, f, quarter)
            for c in range(3):
                flow = flow + normal_of(c, f, quarter) * (mine[c] + beside[c])
            weight = r.weight[part(f, quarter), :]
            return flow, pull + weight * beside[3], weights + weight

        flow, pull, weights = lax.fori_loop(0, FACES // 2, lambda i, t: face(2 * i + 1, face(2 * i, t)), (zero,) * 3)
        here = cells_of(0, quarter)
        flow, inverse_sum = 0.5 * flow, 1.0 / weights
        r.DIV[here, :] = flow
        r.IWS[here, :] = inverse_sum
        r.TP[0][here, :] = (pull - flow) * inverse_sum

    def descend_second(cycle, copies):
        for copy in copies:
            copy.wait_recv()
        sent.extend(copies)
        unpack_second(cycle)
        if cycle == 0:
            deep_coefficients(2)
        descend(levels[2], 0, 8)
        pack_deep(cycle)
        return start_deep(cycle)

    pl.loop(0, 2)(divergence)
    deep0 = descend_second(0, second0)
    pl.loop(2, 4)(divergence)
    cfd_send(2, r.TP[0])
    copies2 = cfd_start(2)

    for copy in deep0:
        copy.wait_recv()
    sent.extend(deep0)
    unpack_deep(0)
    deep_coefficients(3)
    deep_coefficients(4)
    solve_deep()
    near0 = start_near(0)

    def pressure_sweep(before, after):
        @pl.loop(0, 4)
        def _(quarter):
            pull = zero
            for f in range(FACES):
                pull = pull + r.weight[part(f, quarter), :] * beside_of(before, 1, f, quarter)[0]
            here = cells_of(0, quarter)
            after[here, :] = (pull - r.DIV[here, :]) * r.IWS[here, :]

    cfd_wait(2, r.TP[0], copies2)
    pressure_sweep(r.TP[0], r.TP[1])
    cfd_send(3, r.TP[1])
    copies3 = cfd_start(3)

    for copy in near0:
        copy.wait_recv()
    sent.extend(near0)
    add_near(0)
    fine_sweep(r.V, r.U)
    fine_sweep(r.U, r.V)
    fine_sweep(r.V, r.U, 8, 40)
    fine_sweep(r.U, r.V, 8, 40)
    down(8, 40)
    pack_second(1)
    second1 = start_second(1)

    cfd_wait(3, r.TP[1], copies3)
    pressure_sweep(r.TP[1], r.TP[2])
    cfd_send(4, r.TP[2])
    copies4 = cfd_start(4)
    pressure_copy = pltpu.make_async_copy(r.TP[2].at[pl.ds(0, ROWS), :], pressure_out, r.load.at[18])
    pressure_copy.start()
    deep1 = descend_second(1, second1)

    for copy in deep1:
        copy.wait_recv()
    sent.extend(deep1)
    unpack_deep(1)
    solve_deep()
    near1 = start_near(1)

    cfd_wait(4, r.TP[2], copies4)

    @pl.loop(0, 4)
    def _(quarter):
        here = cells_of(0, quarter)
        pressure = r.TP[2][here, :]
        totals = [zero] * 3
        for f in range(FACES):
            difference = beside_of(r.TP[2], 1, f, quarter)[0] - pressure
            totals = [totals[c] + normal_of(c, f, quarter) * difference for c in range(3)]
        for c in range(3):
            r.COR[cells_of(c * ROWS, quarter), :] = r.TS[cells_of(c * EXT, quarter), :] - r.step[here, :] * (
                0.5 * totals[c]
            )

    for copy in near1:
        copy.wait_recv()
    sent.extend(near1)
    add_near(1, 4, 20)
    fine_sweep(r.V, r.U, 8, 40)
    fine_sweep(r.U, r.V, 16, 32, (0,))

    loaded(14, 18)

    own_rows = pl.ds(pl.multiple_of(x * 8, 8), 8)

    def interpolate(quarter):
        corner = r.corner[cells_of(0, quarter), :]
        column = corner & 127
        point_row = (corner >> 7) & 15
        point_layer = corner >> 11

        def layer(k, picks):
            found = []
            for lanes in (column, column + 1):
                low, high = zero, zero
                before = None
                for i in range(16):
                    row = jnp.broadcast_to(r.V[0][k + 1, PAD + 16 + i : PAD + 17 + i, :], (8, 128))
                    value = lane_gather(row, lanes)
                    here = point_row == i
                    if i < 15:
                        low = jnp.where(here, value, low)
                    if before is not None:
                        high = jnp.where(before, value, high)
                    before = here
                found.append((low, high))
            found = (found[0][0], found[1][0], found[0][1], found[1][1])
            lower, upper = point_layer == k, point_layer == k - 1
            return tuple(jnp.where(lower, found[i], picks[i]) for i in range(4)) + tuple(
                jnp.where(upper, found[i], picks[4 + i]) for i in range(4)
            )

        picks = (zero,) * 8
        for k in range(NZ):
            picks = layer(k, picks)
        for quantity in range(4):
            total = zero
            for p in range(8):
                total = total + r.stencil[cells_of((quantity * 8 + p) * ROWS, quarter), :] * picks[p]
            for i in range(8):
                r.S[pl.ds(64 * quarter + 8 * i + quantity, 1), :] = total[i : i + 1, :]

    potential_copy = pltpu.make_async_copy(r.V[0].at[pl.ds(1, NZ), middle, :], potential_out, r.load.at[19])
    potential_copy.start()

    everyone = []
    for away in (2, 1, 3, 0):
        quarter = lax.rem(x // 8 + away, 4)
        interpolate(quarter)
        for i in range(0 if away else 1, 8):
            there_x = quarter * 8 + (i if away else lax.rem(x + i, 8))
            rows = pl.ds(pl.multiple_of(there_x * 8, 8), 8)
            slot = lax.rem(there_x - x + NPX, NPX)
            everyone.append(send(r.S.at[rows, :], r.RB.at[own_rows, :], r.s_all, slot, (there_x, y)))
    r.RB[own_rows, :] = r.S[own_rows, :]
    for o in range(1, NPX):
        pltpu.make_async_remote_copy(
            src_ref=r.S.at[0:8, :],
            dst_ref=r.RB.at[0:8, :],
            send_sem=r.s_all[0].at[o],
            recv_sem=r.s_all[1].at[o],
            device_id=at(o, 0),
            device_id_type=MESH,
        ).wait_recv()
    sent.extend(everyone)

    @pl.loop(0, 4)
    def _(quarter):
        here = cells_of(0, quarter)
        slot_hi, slot_lo = r.INV[here, :] - 1, r.INV[cells_of(ROWS, quarter), :]
        targets = table_gather(lambda c, j: r.RB[8 * j + c : 8 * j + c + 1, :], NPX, 4, slot_hi, slot_lo)
        strength = jnp.where(slot_hi >= 0, r.blend[here, :], 0.0)
        for c in range(3):
            velocity = r.COR[cells_of(c * ROWS, quarter), :]
            velocity_out[cells_of(c * ROWS, quarter), :] = velocity - strength * (velocity - targets[c])
        level_target = jax.nn.sigmoid(4.0 * (targets[3] - r.height[here, :]))
        fraction = r.FRAC[here, :]
        fraction_out[here, :] = fraction - strength * (fraction - level_target)

    pressure_copy.wait()
    potential_copy.wait()
    for copy in sent:
        copy.wait_send()


def hand_over(*refs):
    given, results, held, arrive, leave = refs[0:4], refs[4:8], refs[8:12], refs[12], refs[13]
    ins = [pltpu.make_async_copy(given[i], held[i], arrive.at[i]) for i in range(4)]
    outs = [pltpu.make_async_copy(held[i], results[i], leave.at[i]) for i in range(4)]
    for copy in ins:
        copy.start()
    for i in range(4):
        ins[i].wait()
        outs[i].start()
    for copy in outs:
        copy.wait()


def on_device(
    source, water_depth, potential_start, velocity, fraction, pressure, neighbour, send_slot,
    face_normal, face_weight, step_scale, height, blend_weight, corner, stencil_weight, receive_cell,
):
    def lanes(array):
        return array.reshape(-1, 128)

    args = (
        source, water_depth, potential_start, lanes(velocity), lanes(fraction), lanes(pressure), lanes(neighbour),
        send_slot, lanes(face_normal), lanes(face_weight), lanes(step_scale), lanes(height),
        lanes(blend_weight), lanes(corner), lanes(stencil_weight), lanes(receive_cell),
    )
    shapes = ((NZ, 16, 128), (3 * ROWS, 128), (ROWS, 128), (ROWS, 128))
    results = pl.pallas_call(
        kernel,
        name="step",
        out_shape=[jax.ShapeDtypeStruct(shape, F32) for shape in shapes],
        in_specs=[pl.BlockSpec(memory_space=pltpu.HBM)] * len(args),
        out_specs=[pl.BlockSpec(memory_space=space) for space in (pltpu.HBM, pltpu.VMEM, pltpu.VMEM, pltpu.HBM)],
        scratch_shapes=jax.tree_util.tree_leaves(scratch_plan()),
        compiler_params=pltpu.CompilerParams(
            collective_id=0, has_side_effects=True, vmem_limit_bytes=67043328
        ),
    )(*args)
    dma = pltpu.SemaphoreType.DMA
    results = pl.pallas_call(
        hand_over,
        name="hand_over",
        out_shape=[jax.ShapeDtypeStruct(shape, F32) for shape in shapes],
        in_specs=[pl.BlockSpec(memory_space=pltpu.HBM)] * len(shapes),
        out_specs=[pl.BlockSpec(memory_space=pltpu.HBM)] * len(shapes),
        scratch_shapes=[pltpu.VMEM(shape, F32) for shape in shapes] + [dma((4,)), dma((4,))],
        compiler_params=pltpu.CompilerParams(vmem_limit_bytes=67043328),
    )(*results)
    potential, velocity_out, fraction_out, pressure_out = results
    return (
        potential,
        velocity_out.reshape(3, 1, 1, -1),
        fraction_out.reshape(1, 1, -1),
        pressure_out.reshape(1, 1, -1),
    )


def solution(mesh):
    in_specs = (
        P(None, "px", "py"),
        P("px", "py"),
        P(None, "px", "py"),
        P(None, "px", "py", None),
        P("px", "py", None),
        P("px", "py", None),
        P(None, "px", "py", None),
        P(None, "px", "py", None),
        P(None, None, "px", "py", None),
        P(None, "px", "py", None),
        P("px", "py", None),
        P("px", "py", None),
        P("px", "py", None),
        P("px", "py", None),
        P(None, None, "px", "py", None),
        P("px", "py", None),
    )
    out_specs = (
        P(None, "px", "py"),
        P(None, "px", "py", None),
        P("px", "py", None),
        P("px", "py", None),
    )
    return jax.shard_map(on_device, mesh=mesh, in_specs=in_specs, out_specs=out_specs, check_vma=False)
```
